32 devices in a mesh: dp: 8 (over z, y), mp: 4 (over x, core).
Axes of the slice: x: 2, y: 2, z: 4, core: 2. Of those that a mesh axis runs over, the one named last changes fastest.
Arguments:
- hidden: bfloat16 [24, 1024, 1024], P('dp', 'mp'), may hold values from -6 to 6
- cotangent: bfloat16 [24, 1024, 1024], P('dp', 'mp'), may hold values from -6 to 6
- adapter_ids: int32 [24], P('dp'), may hold values from 0 to 7
- attn_gain: bfloat16 [1024], replicated, may hold values from 0.25 to 1.75
- mlp_gain: bfloat16 [1024], replicated, may hold values from 0.25 to 1.75
- joined_weight: bfloat16 [1024, 3, 1024], P('dp', None, 'mp'), may hold values from -0.1875 to 0.1875
- merge_weight_matrix: bfloat16 [1024, 1024], P('dp', 'mp'), may hold values from -0.75 to 0.75
- expand_weight: bfloat16 [1024, 2, 2624], P('dp', None, 'mp'), may hold values from -0.1875 to 0.1875
- shrink_weight_matrix: bfloat16 [1024, 2624], P('dp', 'mp'), may hold values from -0.15625 to 0.15625
- joined_lower: bfloat16 [8, 1024, 16], replicated, may hold values from -0.1875 to 0.1875
- joined_up_matrices: bfloat16 [8, 16, 3, 1024], P(None, None, None, 'mp'), may hold values from -0.375 to 0.375
- merge_lower: bfloat16 [8, 1024, 16], P(None, 'mp'), may hold values from -0.75 to 0.75
- merge_up_matrices: bfloat16 [8, 16, 1024], replicated, may hold values from -0.375 to 0.375
- expand_lower: bfloat16 [8, 1024, 16], replicated, may hold values from -0.1875 to 0.1875
- expand_up_matrices: bfloat16 [8, 16, 2, 2624], P(None, None, None, 'mp'), may hold values from -0.375 to 0.375
- shrink_lower: bfloat16 [8, 2624, 16], P(None, 'mp'), may hold values from -0.15625 to 0.15625
- shrink_up_matrices: bfloat16 [8, 16, 1024], replicated, may hold values from -0.375 to 0.375
Outputs:
- output: bfloat16 [24, 1024, 1024], P('dp', 'mp')
- hidden_grad: bfloat16 [24, 1024, 1024], P('dp', 'mp')
- joined_lower_grad: float32 [8, 1024, 16], replicated
- joined_upper_grad: float32 [8, 16, 3, 1024], P(None, None, None, 'mp')
- merge_lower_grad: float32 [8, 1024, 16], P(None, 'mp')
- merge_upper_grad: float32 [8, 16, 1024], replicated
- expand_lower_grad: float32 [8, 1024, 16], replicated
- expand_upper_grad: float32 [8, 16, 2, 2624], P(None, None, None, 'mp')
- shrink_lower_grad: float32 [8, 2624, 16], P(None, 'mp')
- shrink_upper_grad: float32 [8, 16, 1024], replicated
The draws below stay inside these ranges and needn't reach their ends.
All inputs are finite; a program needn't handle non-finite values.
Results may differ from the reference program's by a relative error of at most 0.024.
Values may be sent and summed in bfloat16 or wider, within the bound.
No kernel may reach another device: no remote copies, remote signals or barrier semaphores. Data moves between devices by JAX's collectives and lax.ppermute only.
A program may use at most 320 MiB of HBM per device.

```python
import jax
import jax.numpy as jnp
from jax import lax

D = 1024
HEADS = 16
HEAD_DIM = 64
FF = 2624
RANK = 16
ADAPTERS = 8
SEQ_LEN = 1024
SEQS = 24


def touch_ends(entries, rng, least, high):
    place = [jax.random.randint(jax.random.fold_in(rng, axis), (), 0, length) for axis, length in enumerate(entries.shape)]
    longest = entries.shape.index(max(entries.shape))
    beside = place[:longest] + [(place[longest] + 1) % entries.shape[longest]] + place[longest + 1:]
    return entries.at[tuple(place)].set(least).at[tuple(beside)].set(high)


def steps_of(own_key, extent, split, low, largest):
    gain, own = 1.0, jax.random.fold_in(own_key, 6)
    for axis_at, parts in split:
        draws = jnp.exp(jax.random.uniform(jax.random.fold_in(own, axis_at), (parts,), jnp.float32, low / len(split), largest / len(split)))
        gain = gain * jnp.repeat(draws, extent[axis_at] // parts).reshape([-1 if axis == axis_at else 1 for axis in range(len(extent))])
    return gain


def bell_draw(key, extent, scale, reach, split=(), kind=jnp.bfloat16):
    values = scale * jax.random.normal(key, extent, jnp.float32)
    if split:
        values = values * steps_of(key, extent, split, -0.22, 0.18)
    return jnp.clip(values, -reach, reach).astype(kind)


def setup_inputs(seed: int = 0) -> dict:
    keys = jax.random.split(jax.random.key(seed), 18)
    hidden = bell_draw(keys[0], (SEQS, SEQ_LEN, D), 1.0, 6.0, ((0, 8), (1, 4)))
    cotangent = bell_draw(keys[1], (SEQS, SEQ_LEN, D), 1.0, 6.0, ((0, 8), (1, 4)))
    adapter_ids = touch_ends(jax.random.randint(keys[2], (SEQS,), 0, ADAPTERS), jax.random.fold_in(keys[2], 1), 0, ADAPTERS - 1).astype(jnp.int32)
    attn_gain = jnp.clip(1.0 + 0.15 * jax.random.normal(keys[3], (D,), jnp.float32), 0.25, 1.75).astype(jnp.bfloat16)
    mlp_gain = jnp.clip(1.0 + 0.15 * jax.random.normal(keys[4], (D,), jnp.float32), 0.25, 1.75).astype(jnp.bfloat16)
    joined_weight = bell_draw(keys[5], (D, 3, D), D ** -0.5, 0.1875, ((0, 8), (2, 4)))
    merge_weight_matrix = bell_draw(keys[6], (D, D), (D // 16) ** -0.5, 0.75, ((0, 8), (1, 4)))
    expand_weight = bell_draw(keys[7], (D, 2, FF), D ** -0.5, 0.1875, ((0, 8), (2, 4)))
    shrink_weight_matrix = bell_draw(keys[8], (D, FF), (FF // 2) ** -0.5, 0.15625, ((0, 8), (1, 4)))
    joined_lower = bell_draw(keys[9], (ADAPTERS, D, RANK), D ** -0.5, 0.1875)
    joined_up_matrices = bell_draw(keys[10], (ADAPTERS, RANK, 3, D), (16 * RANK) ** -0.5, 0.375, ((3, 4),))
    merge_lower = bell_draw(keys[11], (ADAPTERS, D, RANK), (D // 16) ** -0.5, 0.75, ((1, 4),))
    merge_up_matrices = bell_draw(keys[12], (ADAPTERS, RANK, D), (16 * RANK) ** -0.5, 0.375)
    expand_lower = bell_draw(keys[13], (ADAPTERS, D, RANK), D ** -0.5, 0.1875)
    expand_up_matrices = bell_draw(keys[14], (ADAPTERS, RANK, 2, FF), (16 * RANK) ** -0.5, 0.375, ((3, 4),))
    shrink_lower = bell_draw(keys[15], (ADAPTERS, FF, RANK), (FF // 2) ** -0.5, 0.15625, ((1, 4),))
    shrink_up_matrices = bell_draw(keys[16], (ADAPTERS, RANK, D), (16 * RANK) ** -0.5, 0.375)
    return {"hidden": hidden, "cotangent": cotangent, "adapter_ids": adapter_ids, "attn_gain": attn_gain, "mlp_gain": mlp_gain, "joined_weight": joined_weight, "merge_weight_matrix": merge_weight_matrix, "expand_weight": expand_weight, "shrink_weight_matrix": shrink_weight_matrix, "joined_lower": joined_lower, "joined_up_matrices": joined_up_matrices, "merge_lower": merge_lower, "merge_up_matrices": merge_up_matrices, "expand_lower": expand_lower, "expand_up_matrices": expand_up_matrices, "shrink_lower": shrink_lower, "shrink_up_matrices": shrink_up_matrices}


@jax.custom_vjp
def low(v):
    return lax.optimization_barrier(v.astype(jnp.bfloat16)).astype(jnp.float32)

@jax.custom_vjp
def low_back(v):
    return v

def low_keep(v):
    return (low(v), None)

def low_pass(kept, grad):
    return (grad,)

def back_keep(v):
    return (v, None)

def back_low(kept, grad):
    return (low(grad),)
low.defvjp(low_keep, low_pass)
low_back.defvjp(back_keep, back_low)
MATMUL_PRECISION = lax.Precision.HIGHEST
ADAPTER_SCALE = 2.0
NORM_EPS = 1e-05
ROPE_BASE = 160000.0

def norm_rows(values, norm_gain):
    centred = values - lax.optimization_barrier(jnp.mean(values, axis=-1, keepdims=True))
    spread = lax.optimization_barrier(jnp.mean(centred * centred, axis=-1, keepdims=True))
    return centred * lax.rsqrt(spread + NORM_EPS) * norm_gain

def rotary_tables(length, head_width):
    half_width = head_width // 2
    inverse = ROPE_BASE ** (-(jnp.arange(half_width, dtype=jnp.float32) * 2.0 / head_width))
    angles = jnp.arange(length, dtype=jnp.float32)[:, None] * inverse[None, :]
    angles = jnp.concatenate([angles, angles], axis=1)
    return (jnp.cos(angles), jnp.sin(angles))

def rotate(values, cosine_table, sine_table):
    half_width = values.shape[-1] // 2
    turned = jnp.concatenate([-values[..., half_width:], values[..., :half_width]], axis=-1)
    return values * cosine_table[:, None, :] + turned * sine_table[:, None, :]

def select(lookup, chosen):
    return jnp.tensordot(chosen, lookup, axes=1, precision=MATMUL_PRECISION)

def layer(start_rows, fixed, adapters, chosen):
    attn_gain, mlp_gain, joined_weight, merge_weight_matrix, expand_weight, shrink_weight_matrix = fixed
    joined_lower = select(adapters[0], chosen)
    joined_up_matrices = select(adapters[1], chosen)
    merge_lower = select(adapters[2], chosen)
    merge_up_matrices = select(adapters[3], chosen)
    expand_lower = select(adapters[4], chosen)
    expand_up_matrices = select(adapters[5], chosen)
    shrink_lower = select(adapters[6], chosen)
    shrink_up_matrices = select(adapters[7], chosen)
    length = start_rows.shape[0]
    normed = low(norm_rows(start_rows, attn_gain))
    joined_down_proj = jnp.dot(normed, joined_lower, precision=MATMUL_PRECISION)
    joined_projection = jnp.einsum('ld,dce->lce', normed, joined_weight, precision=MATMUL_PRECISION)
    joined_projection = joined_projection + ADAPTER_SCALE * jnp.einsum('vj,jfk->vfk', joined_down_proj, joined_up_matrices, precision=MATMUL_PRECISION)
    joined_projection = low_back(joined_projection)
    cosine_table, sine_table = rotary_tables(length, HEAD_DIM)
    query_rows = low(rotate(joined_projection[:, 0].reshape(length, HEADS, HEAD_DIM), cosine_table, sine_table))
    key_rows = low(rotate(joined_projection[:, 1].reshape(length, HEADS, HEAD_DIM), cosine_table, sine_table))
    value_rows = low(joined_projection[:, 2].reshape(length, HEADS, HEAD_DIM))
    scores = jnp.einsum('qhe,khe->hqk', query_rows, key_rows, precision=MATMUL_PRECISION) * HEAD_DIM ** (-0.5)
    scores = low_back(scores)
    attn_probs = low(jax.nn.softmax(scores, axis=-1))
    context_rows = jnp.einsum('hqk,khe->qhe', attn_probs, value_rows, precision=MATMUL_PRECISION).reshape(length, D)
    context_rows = low(low_back(context_rows))
    merge_down_proj = jnp.dot(context_rows, merge_lower, precision=MATMUL_PRECISION)
    merged_output = jnp.dot(context_rows, merge_weight_matrix.T, precision=MATMUL_PRECISION) + ADAPTER_SCALE * jnp.dot(merge_down_proj, merge_up_matrices, precision=MATMUL_PRECISION)
    middle = start_rows + low_back(merged_output)
    normed_mlp = low(norm_rows(middle, mlp_gain))
    expand_down_proj = jnp.dot(normed_mlp, expand_lower, precision=MATMUL_PRECISION)
    expanded_hidden = jnp.einsum('ld,dcf->lcf', normed_mlp, expand_weight, precision=MATMUL_PRECISION)
    expanded_hidden = low_back(expanded_hidden + ADAPTER_SCALE * jnp.einsum('xv,vmj->xmj', expand_down_proj, expand_up_matrices, precision=MATMUL_PRECISION))
    activated_hidden = low(jax.nn.gelu(expanded_hidden[:, 0], approximate=False) * expanded_hidden[:, 1])
    shrink_down_proj = jnp.dot(activated_hidden, shrink_lower, precision=MATMUL_PRECISION)
    shrunk_output = jnp.dot(activated_hidden, shrink_weight_matrix.T, precision=MATMUL_PRECISION) + ADAPTER_SCALE * jnp.dot(shrink_down_proj, shrink_up_matrices, precision=MATMUL_PRECISION)
    return middle + low_back(shrunk_output)

def reference(hidden, cotangent, adapter_ids, attn_gain, mlp_gain, joined_weight, merge_weight_matrix, expand_weight, shrink_weight_matrix, joined_lower, joined_up_matrices, merge_lower, merge_up_matrices, expand_lower, expand_up_matrices, shrink_lower, shrink_up_matrices):
    fixed = tuple((member.astype(jnp.float32) for member in (attn_gain, mlp_gain, joined_weight, merge_weight_matrix, expand_weight, shrink_weight_matrix)))
    adapters = tuple((member.astype(jnp.float32) for member in (joined_lower, joined_up_matrices, merge_lower, merge_up_matrices, expand_lower, expand_up_matrices, shrink_lower, shrink_up_matrices)))

    def one_sequence(totals, sequence):
        seq_rows, grads_in, which_set = sequence
        chosen = (jnp.arange(ADAPTERS, dtype=jnp.int32) == which_set).astype(jnp.float32)

        def forward(start_rows, tables):
            return layer(start_rows, fixed, tables, chosen)
        result, pull = jax.vjp(forward, seq_rows.astype(jnp.float32), adapters)
        grad_rows, grad_tables = pull(grads_in.astype(jnp.float32))
        totals = tuple((running + added for running, added in zip(totals, grad_tables)))
        return (totals, (result.astype(jnp.bfloat16), grad_rows.astype(jnp.bfloat16)))
    initial = tuple((jnp.zeros_like(member) for member in adapters))
    totals, stacked = lax.scan(one_sequence, initial, (hidden, cotangent, adapter_ids))
    return (stacked[0], stacked[1], totals[0], totals[1], totals[2], totals[3], totals[4], totals[5], totals[6], totals[7])
```

```python
import jax
import jax.numpy as jnp
from jax import lax
from jax.experimental import pallas as pl
from jax.experimental.pallas import tpu as pltpu
from jax.sharding import PartitionSpec as P

HEAD_DIM = 64
ADAPTERS = 8
ADAPTER_SCALE = 2.0
NORM_EPS = 1e-05
ROPE_BASE = 160000.0
LANES = 128
BF = jnp.bfloat16
F32 = jnp.float32


def nt(a, b):
    return lax.dot_general(a, b, (((1,), (1,)), ((), ())), preferred_element_type=F32)


def nn(a, b):
    return lax.dot_general(a, b, (((1,), (0,)), ((), ())), preferred_element_type=F32)


def tn(a, b):
    return lax.dot_general(a, b, (((0,), (0,)), ((), ())), preferred_element_type=F32)


def lanes_of(ref, first=0, count=None):
    count = ref.shape[2] if count is None else count
    return jnp.concatenate(
        [ref[part, 0, pl.ds(first, count), :] for part in range(ref.shape[0])], axis=1
    )


def full(shape):
    return pl.BlockSpec(shape, lambda *_: (0,) * len(shape))


def norm_parts(values):
    centred = values - jnp.mean(values, axis=-1, keepdims=True)
    spread = jnp.mean(centred * centred, axis=-1, keepdims=True)
    scale = lax.rsqrt(spread + NORM_EPS)
    return centred * scale, scale


def norm_back(grads, normed, scale, gain):
    weighted = grads * gain
    return scale * (
        weighted
        - jnp.mean(weighted, axis=-1, keepdims=True)
        - normed * jnp.mean(weighted * normed, axis=-1, keepdims=True)
    )


def turn(values, cosine, sine_up, sine_down):
    width = values.shape[1]
    half = HEAD_DIM // 2
    return (
        values * cosine
        + pltpu.roll(values, width - half, 1) * sine_up
        + pltpu.roll(values, half, 1) * sine_down
    )


def project_kernel(
    rows, weight, low, up, mask, cosine, sine_up, sine_down,
    query, pairs_a, pairs_b, down, *, split, wide
):
    @pl.when(pl.program_id(0) == 0)
    def _():
        down[...] = (nt(rows[...], low[...]) * (ADAPTER_SCALE * mask[...])).astype(BF)

    table = lanes_of(weight)
    out = nt(rows[...], table) + nn(down[...], up[0])
    cos, su, sd = cosine[...], sine_up[...], sine_down[...]
    turned = turn(out[:, :wide], cos, su, sd)
    query[...] = (turned * HEAD_DIM**-0.5).astype(BF)
    key = turn(out[:, wide : 2 * wide], cos, su, sd).astype(BF)
    value = out[:, 2 * wide :].astype(BF)
    pairs_a[0] = key[:split]
    pairs_a[1] = value[:split]
    pairs_b[0] = key[split:]
    pairs_b[1] = value[split:]


def project(rows, weight, low, up, mask, tables, split):
    count, model = rows.shape
    parts, blocks, tall, lane = weight.shape
    wide = tall // 3
    rank = low.shape[0]
    rest = count - split
    return pl.pallas_call(
        lambda *refs: project_kernel(*refs, split=split, wide=wide),
        grid=(blocks,),
        in_specs=[
            full((count, model)),
            pl.BlockSpec((parts, 1, tall, lane), lambda m: (0, m, 0, 0)),
            full((rank, model)),
            pl.BlockSpec((1, rank, tall), lambda m: (m, 0, 0)),
            full((count, rank)),
            full((count, wide)),
            full((count, wide)),
            full((count, wide)),
        ],
        out_specs=[
            pl.BlockSpec((count, wide), lambda m: (0, m)),
            pl.BlockSpec((2, split, wide), lambda m: (0, 0, m)),
            pl.BlockSpec((2, rest, wide), lambda m: (0, 0, m)),
            full((count, rank)),
        ],
        out_shape=[
            jax.ShapeDtypeStruct((count, blocks * wide), BF),
            jax.ShapeDtypeStruct((2, split, blocks * wide), BF),
            jax.ShapeDtypeStruct((2, rest, blocks * wide), BF),
            jax.ShapeDtypeStruct((count, rank), BF),
        ],
        name="project",
    )(rows, weight, low, up, mask, *tables)


def project_back_kernel(
    rows, grad_query, own_a, got_a, own_b, got_b, weight, low, up, mask, down,
    cosine, sine_up, sine_down, out, up_grad, low_grad, down_grad, *, split, wide, blocks
):
    step = pl.program_id(0)

    @pl.when(step == 0)
    def _():
        out[...] = jnp.zeros(out.shape, F32)
        down_grad[...] = jnp.zeros(down_grad.shape, F32)

    cos, su, sd = cosine[...], -sine_up[...], -sine_down[...]
    query = turn(grad_query[...] * HEAD_DIM**-0.5, cos, su, sd).astype(BF)
    key = jnp.concatenate(
        [own_a[0] + got_a[0].astype(F32), own_b[0] + got_b[0].astype(F32)], axis=0
    )
    key = turn(key, cos, su, sd).astype(BF)
    value = jnp.concatenate(
        [own_a[1] + got_a[1].astype(F32), own_b[1] + got_b[1].astype(F32)], axis=0
    ).astype(BF)
    grads = jnp.concatenate([query, key, value], axis=1)
    table = lanes_of(weight)
    out[...] += nn(grads, table)
    down_grad[...] += nt(grads, up[0])
    up_grad[0] = tn(down[...], grads)

    @pl.when(step == blocks - 1)
    def _():
        small = (down_grad[...] * (ADAPTER_SCALE * mask[...])).astype(BF)
        out[...] += nn(small, low[...])
        low_grad[...] = tn(small, rows[...])


def project_back(rows, grad_query, own_a, got_a, own_b, got_b, weight, low, up, mask, down, tables, split):
    count, model = rows.shape
    parts, blocks, tall, lane = weight.shape
    wide = tall // 3
    rank = low.shape[0]
    rest = count - split
    pair_a = pl.BlockSpec((2, split, wide), lambda m: (0, 0, m))
    pair_b = pl.BlockSpec((2, rest, wide), lambda m: (0, 0, m))
    return pl.pallas_call(
        lambda *refs: project_back_kernel(*refs, split=split, wide=wide, blocks=blocks),
        grid=(blocks,),
        in_specs=[
            full((count, model)),
            pl.BlockSpec((count, wide), lambda m: (0, m)),
            pair_a,
            pair_a,
            pair_b,
            pair_b,
            pl.BlockSpec((parts, 1, tall, lane), lambda m: (0, m, 0, 0)),
            full((rank, model)),
            pl.BlockSpec((1, rank, tall), lambda m: (m, 0, 0)),
            full((count, rank)),
            full((count, rank)),
            full((count, wide)),
            full((count, wide)),
            full((count, wide)),
        ],
        out_specs=[
            full((count, model)),
            pl.BlockSpec((1, rank, tall), lambda m: (m, 0, 0)),
            full((rank, model)),
        ],
        out_shape=[
            jax.ShapeDtypeStruct((count, model), F32),
            jax.ShapeDtypeStruct((blocks, rank, tall), F32),
            jax.ShapeDtypeStruct((rank, model), F32),
        ],
        scratch_shapes=[pltpu.VMEM((count, rank), F32)],
        name="project_back",
    )(rows, grad_query, own_a, got_a, own_b, got_b, weight, low, up, mask, down, *tables)


def one_head(values, head):
    lane = lax.broadcasted_iota(jnp.int32, values.shape, 1)
    return jnp.where((lane // HEAD_DIM) == head, values, jnp.zeros_like(values))


def attend_kernel(query, *refs):
    *pairs, context, log_total = refs
    rows = query[...]
    keys = jnp.concatenate([pair[0] for pair in pairs], axis=0)
    values = jnp.concatenate([pair[1] for pair in pairs], axis=0)
    turned = values.T
    outs = []
    for head in range(2):
        scores = nt(keys, one_head(rows, head))
        top = jnp.max(scores, axis=0, keepdims=True)
        raised = jnp.exp(scores - top)
        total = jnp.sum(raised, axis=0, keepdims=True)
        part = nn(turned[head * HEAD_DIM : (head + 1) * HEAD_DIM], raised.astype(BF))
        outs.append(part * (1.0 / total))
        log_total[0, head : head + 1] = top + jnp.log(total)
    context[...] = jnp.concatenate(outs, axis=0).T.astype(BF)


def attend(query, first, count, pairs):
    model = query.shape[1]
    blocks = model // LANES
    at = first // count
    return pl.pallas_call(
        attend_kernel,
        grid=(blocks,),
        in_specs=[pl.BlockSpec((count, LANES), lambda h: (at, h))]
        + [pl.BlockSpec((2, pair.shape[1], LANES), lambda h: (0, 0, h)) for pair in pairs],
        out_specs=[
            pl.BlockSpec((count, LANES), lambda h: (0, h)),
            pl.BlockSpec((1, 2, count), lambda h: (h, 0, 0)),
        ],
        out_shape=[
            jax.ShapeDtypeStruct((count, model), BF),
            jax.ShapeDtypeStruct((blocks, 2, count), F32),
        ],
        name="attend",
    )(query, *pairs)


def attend_back_kernel(query, grad, log_total, *refs, pieces):
    pairs = refs[:pieces]
    grad_query = refs[pieces]
    grad_pairs = refs[pieces + 1 :]
    rows = query[...]
    outer = grad[...]
    keys = jnp.concatenate([pair[0] for pair in pairs], axis=0)
    values = jnp.concatenate([pair[1] for pair in pairs], axis=0)
    turned = keys.T
    query_parts = []
    grad_keys = None
    grad_values = None
    for head in range(2):
        own = one_head(rows, head)
        own_grad = one_head(outer, head)
        scores = nt(keys, own)
        probs = jnp.exp(scores - log_total[0, head : head + 1])
        wide = nt(values, own_grad)
        mean = jnp.sum(probs * wide, axis=0, keepdims=True)
        back = (probs * (wide - mean)).astype(BF)
        query_parts.append(nn(turned[head * HEAD_DIM : (head + 1) * HEAD_DIM], back))
        more_keys = nn(back, own)
        more_values = nn(probs.astype(BF), own_grad)
        grad_keys = more_keys if grad_keys is None else grad_keys + more_keys
        grad_values = more_values if grad_values is None else grad_values + more_values
    grad_query[...] = jnp.concatenate(query_parts, axis=0).T
    start = 0
    for out in grad_pairs:
        size = out.shape[1]
        out[0] = grad_keys[start : start + size].astype(out.dtype)
        out[1] = grad_values[start : start + size].astype(out.dtype)
        start += size


def attend_back(query, grad, first, count, log_total, pairs, kinds):
    model = query.shape[1]
    blocks = model // LANES
    at = first // count
    row_spec = pl.BlockSpec((count, LANES), lambda h: (at, h))
    pair_specs = [pl.BlockSpec((2, pair.shape[1], LANES), lambda h: (0, 0, h)) for pair in pairs]
    return pl.pallas_call(
        lambda *refs: attend_back_kernel(*refs, pieces=len(pairs)),
        grid=(blocks,),
        in_specs=[row_spec, row_spec, pl.BlockSpec((1, 2, count), lambda h: (h, 0, 0))] + pair_specs,
        out_specs=[pl.BlockSpec((count, LANES), lambda h: (0, h))] + pair_specs,
        out_shape=[jax.ShapeDtypeStruct((count, model), F32)]
        + [jax.ShapeDtypeStruct(pair.shape, kind) for pair, kind in zip(pairs, kinds)],
        name="attend_back",
    )(query, grad, log_total, *pairs)


def block_rows(weight):
    return jnp.concatenate(
        [
            jnp.concatenate([weight[part, m] for part in range(weight.shape[0])], axis=1)
            for m in range(weight.shape[1])
        ],
        axis=0,
    )


def merge_kernel(context, start, weight, low, up, mask, gain, middle, normed, down):
    rows = context[...]
    small = (nt(rows, low[...]) * (ADAPTER_SCALE * mask[...])).astype(BF)
    down[...] = small
    total = start[...].astype(F32) + nn(rows, block_rows(weight)) + nn(small, up[...])
    middle[...] = total
    normed[...] = (norm_parts(total)[0] * gain[...]).astype(BF)


def merge(context, start, weight, low, up, mask, gain):
    count, model = context.shape
    tile = 256
    rank = low.shape[0]
    row = pl.BlockSpec((tile, model), lambda t: (t, 0))
    small = pl.BlockSpec((tile, rank), lambda t: (t, 0))
    return pl.pallas_call(
        merge_kernel,
        grid=(count // tile,),
        in_specs=[row, row, full(weight.shape), full(low.shape), full(up.shape), small, full((1, model))],
        out_specs=[row, row, small],
        out_shape=[
            jax.ShapeDtypeStruct((count, model), F32),
            jax.ShapeDtypeStruct((count, model), BF),
            jax.ShapeDtypeStruct((count, rank), BF),
        ],
        name="merge",
    )(context, start, weight, low, up, mask, gain)


def merge_back_kernel(
    grad_normed, middle, out_grad, context, down, weight, low, up, mask, gain,
    grad_middle, grad_context, low_grad, up_grad
):
    @pl.when(pl.program_id(0) == 0)
    def _():
        low_grad[...] = jnp.zeros(low_grad.shape, F32)
        up_grad[...] = jnp.zeros(up_grad.shape, F32)

    normed, scale = norm_parts(middle[...])
    total = out_grad[...].astype(F32) + norm_back(grad_normed[...], normed, scale, gain[...])
    grad_middle[...] = total
    rows = total.astype(BF)
    small = (nt(rows, up[...]) * (ADAPTER_SCALE * mask[...])).astype(BF)
    grad_context[...] = (nt(rows, block_rows(weight)) + nn(small, low[...])).astype(BF)
    low_grad[...] += tn(small, context[...])
    up_grad[...] += tn(down[...], rows)


def merge_back(grad_normed, middle, out_grad, context, down, weight, low, up, mask, gain):
    count, model = context.shape
    tile = 256
    rank = low.shape[0]
    row = pl.BlockSpec((tile, model), lambda t: (t, 0))
    small = pl.BlockSpec((tile, rank), lambda t: (t, 0))
    return pl.pallas_call(
        merge_back_kernel,
        grid=(count // tile,),
        in_specs=[row, row, row, row, small, full(weight.shape), full(low.shape), full(up.shape), small, full((1, model))],
        out_specs=[row, row, full((rank, model)), full((rank, model))],
        out_shape=[
            jax.ShapeDtypeStruct((count, model), F32),
            jax.ShapeDtypeStruct((count, model), BF),
            jax.ShapeDtypeStruct((rank, model), F32),
            jax.ShapeDtypeStruct((rank, model), F32),
        ],
        name="merge_back",
    )(grad_normed, middle, out_grad, context, down, weight, low, up, mask, gain)


def gated_kernel(
    rows, out_grad, expand, shrink, expand_up, shrink_low, expand_low, shrink_up, mask,
    total, grad_rows, expand_up_grad, shrink_low_grad, expand_low_grad, shrink_up_grad,
    down, down_grad, late, late_grad, *, width, blocks
):
    step = pl.program_id(0)
    scaled = ADAPTER_SCALE * mask[...]

    @pl.when(step == 0)
    def _():
        total[...] = jnp.zeros(total.shape, F32)
        grad_rows[...] = jnp.zeros(grad_rows.shape, F32)
        down[...] = (nt(rows[...], expand_low[...]) * scaled).astype(BF)
        down_grad[...] = (nt(out_grad[...], shrink_up[...]) * scaled).astype(BF)
        late[...] = jnp.zeros(late.shape, F32)
        late_grad[...] = jnp.zeros(late_grad.shape, F32)

    values = lanes_of(expand, 0, width)
    gates = lanes_of(expand, width, width)
    outs = lanes_of(shrink)
    up_values = expand_up[0, :, :width]
    up_gates = expand_up[0, :, expand_up.shape[2] // 2 : expand_up.shape[2] // 2 + width]
    low_outs = shrink_low[0, :, :width]
    first = nt(rows[...], values) + nn(down[...], up_values)
    second = nt(rows[...], gates) + nn(down[...], up_gates)
    chance = 0.5 + 0.5 * lax.erf(first * (0.5**0.5))
    curve = first * chance
    slope = chance + first * (jnp.exp(-0.5 * first * first) * 0.3989422804014327)
    active = (curve * second).astype(BF)
    grads = nt(out_grad[...], outs) + nn(down_grad[...], low_outs)
    first_grad = (grads * second * slope).astype(BF)
    second_grad = (grads * curve).astype(BF)
    total[...] += nn(active, outs)
    late[...] += nt(active, low_outs)
    grad_rows[...] += nn(first_grad, values) + nn(second_grad, gates)
    late_grad[...] += nt(first_grad, up_values) + nt(second_grad, up_gates)
    expand_up_grad[0, 0] = tn(down[...], first_grad)
    expand_up_grad[0, 1] = tn(down[...], second_grad)
    shrink_low_grad[0] = tn(down_grad[...], active)

    @pl.when(step == blocks - 1)
    def _():
        small = (late[...] * scaled).astype(BF)
        total[...] += nn(small, shrink_up[...])
        shrink_up_grad[...] = tn(small, out_grad[...])
        small_grad = (late_grad[...] * scaled).astype(BF)
        grad_rows[...] += nn(small_grad, expand_low[...])
        expand_low_grad[...] = tn(small_grad, rows[...])


def gated(rows, out_grad, weights, width, expand_up, shrink_low, expand_low, shrink_up, mask):
    count, model = rows.shape
    parts, blocks, _, lane = weights.shape
    rank = expand_low.shape[0]
    pad = shrink_low.shape[2]
    return pl.pallas_call(
        lambda *refs: gated_kernel(*refs, width=width, blocks=blocks),
        grid=(blocks,),
        in_specs=[
            full((count, model)),
            full((count, model)),
            pl.BlockSpec((parts, 1, 2 * width, lane), lambda m: (0, m, 0, 0)),
            pl.BlockSpec((parts, 1, width, lane), lambda m: (0, m, 2, 0)),
            pl.BlockSpec((1, rank, 2 * pad), lambda m: (m, 0, 0)),
            pl.BlockSpec((1, rank, pad), lambda m: (m, 0, 0)),
            full((rank, model)),
            full((rank, model)),
            full((count, rank)),
        ],
        out_specs=[
            full((count, model)),
            full((count, model)),
            pl.BlockSpec((1, 2, rank, width), lambda m: (m, 0, 0, 0)),
            pl.BlockSpec((1, rank, width), lambda m: (m, 0, 0)),
            full((rank, model)),
            full((rank, model)),
        ],
        out_shape=[
            jax.ShapeDtypeStruct((count, model), F32),
            jax.ShapeDtypeStruct((count, model), F32),
            jax.ShapeDtypeStruct((blocks, 2, rank, width), F32),
            jax.ShapeDtypeStruct((blocks, rank, width), F32),
            jax.ShapeDtypeStruct((rank, model), F32),
            jax.ShapeDtypeStruct((rank, model), F32),
        ],
        scratch_shapes=[
            pltpu.VMEM((count, rank), BF),
            pltpu.VMEM((count, rank), BF),
            pltpu.VMEM((count, rank), F32),
            pltpu.VMEM((count, rank), F32),
        ],
        name="gated",
    )(rows, out_grad, weights, weights, expand_up, shrink_low, expand_low, shrink_up, mask)


def pair_swap(values, bit):
    size = lax.axis_size("mp")
    return lax.ppermute(values, "mp", [(i, i ^ bit) for i in range(size)])


def gather_weight(rows):
    parts, blocks = lax.axis_size("dp"), lax.axis_size("mp")
    count, own = rows.shape
    whole = lax.all_gather(rows, ("dp", "mp"), axis=0, tiled=True).reshape(parts, blocks, count, own)
    if own == LANES:
        return whole
    tiles = parts * own // LANES
    whole = whole.transpose(1, 2, 0, 3).reshape(blocks, count, tiles, LANES)
    return whole.transpose(2, 0, 1, 3)


def local(
    hidden,
    cotangent,
    adapter_ids,
    attn_gain,
    mlp_gain,
    joined_weight,
    merge_weight_matrix,
    expand_weight,
    shrink_weight_matrix,
    joined_lower,
    joined_up_matrices,
    merge_lower,
    merge_up_matrices,
    expand_lower,
    expand_up_matrices,
    shrink_lower,
    shrink_up_matrices,
):
    parts, blocks = lax.axis_size("dp"), lax.axis_size("mp")
    place = lax.axis_index("mp")
    pair = place // 2
    core = place % 2
    own_rows, model = hidden.shape[1], hidden.shape[2]
    row_in = joined_weight.shape[0]
    wide = joined_weight.shape[2]
    width = expand_weight.shape[2]
    rank = joined_lower.shape[2]
    split = 2 * own_rows
    count = 3 * own_rows

    joined_whole = gather_weight(joined_weight.reshape(row_in, 3 * wide).T)
    rest = jnp.concatenate(
        [expand_weight.reshape(row_in, 2 * width).T, shrink_weight_matrix.T], axis=0
    )
    merge_whole = gather_weight(merge_weight_matrix.T)
    rest_whole = gather_weight(rest)

    keep = lax.dynamic_index_in_dim(hidden, pair, 0, keepdims=False)
    give = lax.dynamic_index_in_dim(hidden, 1 - pair, 0, keepdims=False)
    start = jnp.concatenate([keep, pair_swap(give, 2), hidden[2]], axis=0)
    keep_grad = lax.dynamic_index_in_dim(cotangent, pair, 0, keepdims=False)
    give_grad = lax.dynamic_index_in_dim(cotangent, 1 - pair, 0, keepdims=False)
    out_grad = jnp.concatenate([keep_grad, pair_swap(give_grad, 2), cotangent[2]], axis=0)

    sets = jnp.stack([adapter_ids[pair], adapter_ids[2]])

    def whole_low(table):
        picked = jnp.take(table, sets, axis=0)
        return picked.transpose(0, 2, 1).reshape(2 * rank, -1)

    def whole_up(table):
        return jnp.take(table, sets, axis=0).reshape(2 * rank, -1)

    joined_low = whole_low(joined_lower)
    expand_low = whole_low(expand_lower)
    merge_up = whole_up(merge_up_matrices)
    shrink_up = whole_up(shrink_up_matrices)
    pad = -(-width // LANES) * LANES
    side = [(0, 0), (0, 0), (0, pad - width)]
    mine = jnp.concatenate(
        [
            joined_up_matrices.reshape(ADAPTERS, rank, 3 * wide),
            merge_lower.transpose(0, 2, 1),
            jnp.pad(expand_up_matrices[:, :, 0], side),
            jnp.pad(expand_up_matrices[:, :, 1], side),
            jnp.pad(shrink_lower.transpose(0, 2, 1), side),
        ],
        axis=2,
    )
    mine = jnp.take(mine, adapter_ids, axis=0)
    across = pair_swap(mine, 2)
    beside = pair_swap(mine, 1)
    corner = pair_swap(across, 1)
    around = jnp.stack([mine, beside, across, corner])
    order = place ^ jnp.arange(blocks)
    split_sets = jnp.take(around, order, axis=0)
    split_sets = jnp.take(split_sets, jnp.stack([pair, 2]), axis=1).reshape(blocks, 2 * rank, -1)
    at = 3 * wide
    joined_up = split_sets[:, :, :at]
    merge_low = split_sets[:, :, at : at + wide].transpose(1, 0, 2).reshape(2 * rank, blocks * wide)
    expand_up = split_sets[:, :, at + wide : at + wide + 2 * pad]
    shrink_low = split_sets[:, :, at + wide + 2 * pad :]
    group = (jnp.arange(count) >= split).astype(jnp.int32)
    mask = (group[:, None] == (jnp.arange(2 * rank) // rank)[None, :]).astype(F32)

    steps = jnp.arange(own_rows)
    spots = jnp.concatenate(
        [
            place * own_rows + steps,
            (place ^ 2) * own_rows + steps,
            place * own_rows + steps,
        ]
    ).astype(F32)
    half = HEAD_DIM // 2
    inverse = ROPE_BASE ** (-(jnp.arange(half, dtype=F32) * 2.0 / HEAD_DIM))
    angles = spots[:, None] * inverse[None, :]
    cosine, sine, none = jnp.cos(angles), jnp.sin(angles), jnp.zeros_like(angles)
    heads = wide // HEAD_DIM
    tables = (
        jnp.tile(jnp.concatenate([cosine, cosine], axis=1), (1, heads)),
        jnp.tile(jnp.concatenate([-sine, none], axis=1), (1, heads)),
        jnp.tile(jnp.concatenate([none, sine], axis=1), (1, heads)),
    )

    attn_scale = attn_gain.astype(F32)[None, :]
    mlp_scale = mlp_gain.astype(F32)[None, :]
    first_normed, first_scale = norm_parts(start.astype(F32))
    normed = (first_normed * attn_scale).astype(BF)

    query, pairs_a, pairs_b, joined_down = project(
        normed, joined_whole, joined_low, joined_up, mask, tables, split
    )
    beside_a = pair_swap(pairs_a, 1)
    across_b = pair_swap(pairs_b, 2)
    beside_b = pair_swap(pairs_b, 1)
    corner_b = pair_swap(across_b, 1)
    sets_a = (pairs_a, beside_a)
    sets_b = (pairs_b, across_b, beside_b, corner_b)
    context_a, log_a = attend(query, 0, split, sets_a)
    context_b, log_b = attend(query, split, own_rows, sets_b)
    context = jnp.concatenate([context_a, context_b], axis=0)
    middle, normed_mlp, merge_down = merge(
        context, start, merge_whole, merge_low, merge_up, mask, mlp_scale
    )
    (
        shrunk,
        grad_normed_mlp,
        expand_up_grad,
        shrink_low_grad,
        expand_low_grad,
        shrink_up_grad,
    ) = gated(
        normed_mlp, out_grad, rest_whole, width,
        expand_up, shrink_low, expand_low, shrink_up, mask,
    )
    result = (middle + shrunk).astype(BF)
    back = pair_swap(result[own_rows:split], 2)

    grad_middle, grad_context, merge_low_grad, merge_up_grad = merge_back(
        grad_normed_mlp, middle, out_grad, context, merge_down,
        merge_whole, merge_low, merge_up, mask, mlp_scale,
    )
    grad_query_b, own_b, far_b, near_b, last_b = attend_back(
        query, grad_context, split, own_rows, log_b, sets_b, (F32, F32, BF, BF)
    )
    near_got = pair_swap(near_b, 1)
    last_got = pair_swap(last_b, 1)
    far_sum = (far_b + last_got.astype(F32)).astype(BF)
    own_b = own_b + near_got.astype(F32)
    got_b = pair_swap(far_sum, 2)
    grad_query_a, own_a, near_a = attend_back(
        query, grad_context, 0, split, log_a, sets_a, (F32, BF)
    )
    got_a = pair_swap(near_a, 1)
    grad_query = jnp.concatenate([grad_query_a, grad_query_b], axis=0)
    grad_normed, joined_up_grad, joined_low_grad = project_back(
        normed, grad_query, own_a, got_a, own_b, got_b,
        joined_whole, joined_low, joined_up, mask, joined_down, tables, split,
    )
    grad_start = grad_middle + norm_back(grad_normed, first_normed, first_scale, attn_scale)
    grad_start = grad_start.astype(BF)
    back_grad = pair_swap(grad_start[own_rows:split], 2)

    def settle(values, swapped):
        mine_first = jnp.stack([values[:own_rows], swapped])
        other_first = jnp.stack([swapped, values[:own_rows]])
        two = jnp.where(pair == 0, mine_first, other_first)
        return jnp.concatenate([two, values[None, split:]], axis=0)

    every_id = lax.all_gather(adapter_ids, "dp", axis=0)
    first_ids = jnp.repeat(every_id[:, :2], blocks // 2, axis=1)
    ids = jnp.stack([first_ids, jnp.broadcast_to(every_id[:, 2:], first_ids.shape)], axis=2)
    choose = (jnp.arange(ADAPTERS)[:, None] == ids.reshape(1, -1)).astype(BF)

    def by_block(grad):
        return grad.reshape(2 * rank, blocks, -1).transpose(1, 0, 2)

    def spread(pieces):
        sizes = [piece.shape[2] for piece in pieces]
        packed = jnp.concatenate([piece.astype(BF) for piece in pieces], axis=2)
        total = packed.shape[2]
        packed = packed.reshape(blocks, 2, parts, -1).transpose(2, 0, 1, 3)
        packed = packed.reshape(parts * blocks, 2, -1)
        landed = lax.all_to_all(packed, ("dp", "mp"), 0, 0, tiled=True)
        landed = landed.reshape(parts * blocks * 2, -1)
        summed = jnp.dot(choose, landed, preferred_element_type=F32)
        return summed.astype(BF), sizes, total

    def share(summed, sizes, total, common):
        whole = lax.all_gather(summed, "dp", axis=0)
        whole = whole.transpose(1, 0, 2).reshape(ADAPTERS, rank, total)
        cuts, start_at = [], 0
        for size, shared in zip(sizes, common):
            cuts.append(whole[:, :, start_at : start_at + size])
            start_at += size
        joint = [cut for cut, shared in zip(cuts, common) if shared]
        joint = lax.all_gather(jnp.stack(joint), "mp", axis=0)
        outs, at_joint = [], 0
        for cut, shared in zip(cuts, common):
            if shared:
                outs.append(joint[:, at_joint].transpose(1, 2, 0, 3).reshape(ADAPTERS, rank, -1).astype(F32))
                at_joint += 1
            else:
                outs.append(cut.astype(F32))
        return outs

    early = spread(
        [
            by_block(expand_low_grad),
            by_block(shrink_up_grad),
            expand_up_grad[:, 0],
            expand_up_grad[:, 1],
            shrink_low_grad,
            by_block(merge_up_grad),
            by_block(merge_low_grad),
        ]
    )
    out_early = share(*early, (True, True, False, False, False, True, False))
    late = spread([by_block(joined_low_grad), joined_up_grad])
    out_late = share(*late, (True, False))

    def tall(values):
        return values.transpose(0, 2, 1)

    return (
        settle(result, back),
        settle(grad_start, back_grad),
        tall(out_late[0]),
        out_late[1].reshape(ADAPTERS, rank, 3, wide),
        tall(out_early[6]),
        out_early[5],
        tall(out_early[0]),
        jnp.stack([out_early[2], out_early[3]], axis=2),
        tall(out_early[4]),
        out_early[1],
    )


def solution(mesh):
    in_specs = (
        P("dp", "mp", None),
        P("dp", "mp", None),
        P("dp"),
        P(),
        P(),
        P("dp", None, "mp"),
        P("dp", "mp"),
        P("dp", None, "mp"),
        P("dp", "mp"),
        P(),
        P(None, None, None, "mp"),
        P(None, "mp", None),
        P(),
        P(),
        P(None, None, None, "mp"),
        P(None, "mp", None),
        P(),
    )
    out_specs = (
        P("dp", "mp", None),
        P("dp", "mp", None),
        P(),
        P(None, None, None, "mp"),
        P(None, "mp", None),
        P(),
        P(),
        P(None, None, None, "mp"),
        P(None, "mp", None),
        P(),
    )
    return jax.shard_map(local, mesh=mesh, in_specs=in_specs, out_specs=out_specs, check_vma=False)
```

```python
import jax
import jax.numpy as jnp
from jax import lax
from jax.experimental import pallas as pl
from jax.experimental.pallas import tpu as pltpu
from jax.sharding import PartitionSpec as P

HEAD_DIM = 64
ADAPTERS = 8
ADAPTER_SCALE = 2.0
NORM_EPS = 1e-05
ROPE_BASE = 160000.0
LANES = 128
BF = jnp.bfloat16
F32 = jnp.float32


def nt(a, b):
    return lax.dot_general(a, b, (((1,), (1,)), ((), ())), preferred_element_type=F32)


def nn(a, b):
    return lax.dot_general(a, b, (((1,), (0,)), ((), ())), preferred_element_type=F32)


def tn(a, b):
    return lax.dot_general(a, b, (((0,), (0,)), ((), ())), preferred_element_type=F32)


def lanes_of(ref, first=0, count=None, spot=None):
    count = ref.shape[2] if count is None else count
    places = [part if spot is None else spot[1 + part] for part in range(ref.shape[0])]
    return jnp.concatenate([ref[place, 0, pl.ds(first, count), :] for place in places], axis=1)


def full(shape):
    return pl.BlockSpec(shape, lambda *_: (0,) * len(shape))


def norm_parts(values):
    centred = values - jnp.mean(values, axis=-1, keepdims=True)
    spread = jnp.mean(centred * centred, axis=-1, keepdims=True)
    scale = lax.rsqrt(spread + NORM_EPS)
    return centred * scale, scale


def norm_back(grads, normed, scale, gain):
    weighted = grads * gain
    return scale * (
        weighted
        - jnp.mean(weighted, axis=-1, keepdims=True)
        - normed * jnp.mean(weighted * normed, axis=-1, keepdims=True)
    )


def turn(values, cosine, sine):
    width = values.shape[1]
    half = HEAD_DIM // 2
    many = width // LANES
    if many > 1:
        cosine = jnp.concatenate([cosine] * many, axis=1)
        sine = jnp.concatenate([sine] * many, axis=1)
    lane = lax.broadcasted_iota(jnp.int32, values.shape, 1)
    turned = jnp.where(
        lane % HEAD_DIM < half,
        -pltpu.roll(values, width - half, 1),
        pltpu.roll(values, half, 1),
    )
    return values * cosine + turned * sine


def project_kernel(
    place, own, beside, across, corner, weight, low, up, cosine, sine,
    query, key, value, down, *, wide
):
    table = lanes_of(weight, 0, 3 * wide, place)
    for step, piece in enumerate((own, beside, across, corner)):
        spot = place[0] ^ step
        rows = piece[0]
        small = (nt(rows, low[0]) * ADAPTER_SCALE).astype(BF)
        down[0, step] = small
        out = nt(rows, table) + nn(small, up[0])
        cos, sin = cosine[spot], sine[spot]
        turned = turn(out[:, :wide], cos, sin)
        query[0, spot] = (turned * HEAD_DIM**-0.5).astype(BF)
        key[0, spot] = turn(out[:, wide : 2 * wide], cos, sin).astype(BF)
        value[0, spot] = out[:, 2 * wide :].astype(BF)


def project(place, pieces, weight, low, up, tables):
    seqs, own, model = pieces[0].shape
    tall = up.shape[2]
    wide = tall // 3
    rank = low.shape[1]
    blocks = len(pieces)
    piece = pl.BlockSpec((1, own, model), lambda s, p: (s, 0, 0))
    result = pl.BlockSpec((1, blocks, own, wide), lambda s, p: (s, 0, 0, 0))
    table = pl.BlockSpec((blocks, own, LANES), lambda s, p: (0, 0, 0))
    return pl.pallas_call(
        lambda *refs: project_kernel(*refs, wide=wide),
        grid_spec=pltpu.PrefetchScalarGridSpec(
            num_scalar_prefetch=1,
            grid=(seqs,),
            in_specs=[piece] * blocks
            + [
                pl.BlockSpec(weight.shape, lambda s, p: (0, 0, 0, 0)),
                pl.BlockSpec((1, rank, model), lambda s, p: (s, 0, 0)),
                pl.BlockSpec((1, rank, tall), lambda s, p: (s, 0, 0)),
                table,
                table,
            ],
            out_specs=[result] * 3
            + [pl.BlockSpec((1, blocks, own, rank), lambda s, p: (s, 0, 0, 0))],
        ),
        out_shape=[jax.ShapeDtypeStruct((seqs, blocks, own, wide), BF)] * 3
        + [jax.ShapeDtypeStruct((seqs, blocks, own, rank), BF)],
        name="project",
    )(place, *pieces, weight, low, up, *tables)


def joined_grads_kernel(
    place, grad_query, grad_key, grad_value, own, beside, across, corner, up, down,
    small_grad, up_grad, low_grad
):
    up_total = jnp.zeros(up_grad.shape, F32)
    low_total = jnp.zeros(low_grad.shape, F32)
    for step, piece in enumerate((own, beside, across, corner)):
        spot = place[0] ^ step
        grads = jnp.concatenate([grad_query[spot], grad_key[spot], grad_value[spot]], axis=1)
        small = (nt(grads, up[0]) * ADAPTER_SCALE).astype(BF)
        small_grad[step] = small
        up_total += tn(down[0, step], grads)
        low_total += tn(small, piece[0])
    up_grad[...] = up_total
    low_grad[...] = low_total


def joined_grads(place, seq, grads, pieces, up, down):
    _, own, model = pieces[0].shape
    _, rank, tall = up.shape
    wide = tall // 3
    blocks = len(pieces)
    whole = lambda shape: pl.BlockSpec(shape, lambda i, p: (0,) * len(shape))
    of_seq = lambda shape: pl.BlockSpec((1,) + shape, lambda i, p: (seq,) + (0,) * len(shape))
    return pl.pallas_call(
        joined_grads_kernel,
        grid_spec=pltpu.PrefetchScalarGridSpec(
            num_scalar_prefetch=1,
            grid=(1,),
            in_specs=[whole((blocks, own, wide))] * 3
            + [of_seq((own, model))] * blocks
            + [of_seq((rank, tall)), of_seq((blocks, own, rank))],
            out_specs=[whole((blocks, own, rank)), whole((rank, tall)), whole((rank, model))],
        ),
        out_shape=[
            jax.ShapeDtypeStruct((blocks, own, rank), BF),
            jax.ShapeDtypeStruct((rank, tall), F32),
            jax.ShapeDtypeStruct((rank, model), F32),
        ],
        name="joined_grads",
    )(place, *grads, *pieces, up, down)


def project_back_kernel(place, grad_query, grad_key, grad_value, small_grad, weight, low, here, there):
    table = lanes_of(weight, 0, 3 * grad_query.shape[2], place)
    for step in range(grad_query.shape[0]):
        spot = place[0] ^ step
        grads = jnp.concatenate([grad_query[spot], grad_key[spot], grad_value[spot]], axis=1)
        out = nn(grads, table) + nn(small_grad[step], low[0])
        if step % 2:
            there[step // 2] = out.astype(BF)
        else:
            here[step // 2] = out


def project_back(place, seq, grads, small_grad, weight, low):
    blocks, own, wide = grads[0].shape
    _, rank, model = low.shape
    whole = lambda shape: pl.BlockSpec(shape, lambda i, p: (0,) * len(shape))
    return pl.pallas_call(
        project_back_kernel,
        grid_spec=pltpu.PrefetchScalarGridSpec(
            num_scalar_prefetch=1,
            grid=(1,),
            in_specs=[whole((blocks, own, wide))] * 3
            + [
                whole((blocks, own, rank)),
                whole(weight.shape),
                pl.BlockSpec((1, rank, model), lambda i, p: (seq, 0, 0)),
            ],
            out_specs=[whole((blocks // 2, own, model))] * 2,
        ),
        out_shape=[
            jax.ShapeDtypeStruct((blocks // 2, own, model), F32),
            jax.ShapeDtypeStruct((blocks // 2, own, model), BF),
        ],
        name="project_back",
    )(place, *grads, small_grad, weight, low)


def one_head(values, head):
    lane = lax.broadcasted_iota(jnp.int32, values.shape, 1)
    return jnp.where((lane // HEAD_DIM) == head, values, jnp.zeros_like(values))


def attend_kernel(place, query, key, value, *outs):
    *contexts, log_total = outs
    blocks, own = query.shape[1:3]
    keys = key[0].reshape(blocks * own, LANES)
    turned = value[0].reshape(blocks * own, LANES).T
    for step in range(0, blocks, 2):
        rows = jnp.concatenate([query[0, place[0] ^ (step + i)] for i in range(2)], axis=0)
        parts = []
        for head in range(2):
            scores = nt(keys, one_head(rows, head))
            top = jnp.max(scores, axis=0, keepdims=True)
            raised = jnp.exp(scores - top)
            total = jnp.sum(raised, axis=0, keepdims=True)
            part = nn(turned[head * HEAD_DIM : (head + 1) * HEAD_DIM], raised.astype(BF))
            parts.append(part * (1.0 / total))
            logs = top + jnp.log(total)
            for i in range(2):
                log_total[0, step + i, head : head + 1] = logs[:, i * own : (i + 1) * own]
        merged = jnp.concatenate(parts, axis=0).T.astype(BF)
        for i in range(2):
            contexts[step + i][...] = merged[i * own : (i + 1) * own]


def attend(place, query, key, value, seq):
    _, blocks, own, wide = query.shape
    pairs = wide // LANES
    whole = pl.BlockSpec((1, blocks, own, LANES), lambda h, p: (seq, 0, 0, h))
    *contexts, logs = pl.pallas_call(
        attend_kernel,
        grid_spec=pltpu.PrefetchScalarGridSpec(
            num_scalar_prefetch=1,
            grid=(pairs,),
            in_specs=[whole] * 3,
            out_specs=[pl.BlockSpec((own, LANES), lambda h, p: (0, h))] * blocks
            + [pl.BlockSpec((1, blocks, 2, own), lambda h, p: (h, 0, 0, 0))],
        ),
        out_shape=[jax.ShapeDtypeStruct((own, wide), BF)] * blocks
        + [jax.ShapeDtypeStruct((pairs, blocks, 2, own), F32)],
        name="attend",
    )(place, query, key, value)
    return contexts, logs


def attend_back_kernel(place, query, key, value, *refs):
    blocks, own = query.shape[1:3]
    pieces = refs[:blocks]
    log_total, cosine, sine, grad_query, grad_key, grad_value = refs[blocks:]
    keys = key[0].reshape(blocks * own, LANES)
    values = value[0].reshape(blocks * own, LANES)
    turned = keys.T
    grad_keys = jnp.zeros(keys.shape, F32)
    grad_values = jnp.zeros(keys.shape, F32)
    for step in range(0, blocks, 2):
        spots = [place[0] ^ (step + i) for i in range(2)]
        rows = jnp.concatenate([query[0, spot] for spot in spots], axis=0)
        outer = jnp.concatenate([pieces[step + i][...] for i in range(2)], axis=0)
        parts = []
        for head in range(2):
            mine = one_head(rows, head)
            mine_grad = one_head(outer, head)
            scores = nt(keys, mine)
            logs = jnp.concatenate([log_total[0, step + i, head : head + 1] for i in range(2)], axis=1)
            probs = jnp.exp(scores - logs)
            wide = nt(values, mine_grad)
            mean = jnp.sum(probs * wide, axis=0, keepdims=True)
            back = (probs * (wide - mean)).astype(BF)
            parts.append(nn(turned[head * HEAD_DIM : (head + 1) * HEAD_DIM], back))
            grad_keys += nn(back, mine)
            grad_values += nn(probs.astype(BF), mine_grad)
        queries = jnp.concatenate(parts, axis=0).T * HEAD_DIM**-0.5
        for i, spot in enumerate(spots):
            part = queries[i * own : (i + 1) * own]
            grad_query[spot] = turn(part, cosine[spot], -sine[spot]).astype(BF)
    for step in range(blocks):
        part = slice(step * own, (step + 1) * own)
        grad_key[step] = turn(grad_keys[part], cosine[step], -sine[step]).astype(BF)
        grad_value[step] = grad_values[part].astype(BF)


def attend_back(place, query, key, value, seq, pieces, log_total, tables):
    _, blocks, own, wide = query.shape
    pairs = wide // LANES
    whole = pl.BlockSpec((1, blocks, own, LANES), lambda h, p: (seq, 0, 0, h))
    column = pl.BlockSpec((blocks, own, LANES), lambda h, p: (0, 0, h))
    table = pl.BlockSpec((blocks, own, LANES), lambda h, p: (0, 0, 0))
    return pl.pallas_call(
        attend_back_kernel,
        grid_spec=pltpu.PrefetchScalarGridSpec(
            num_scalar_prefetch=1,
            grid=(pairs,),
            in_specs=[whole] * 3
            + [pl.BlockSpec((own, LANES), lambda h, p: (0, h))] * blocks
            + [pl.BlockSpec((1, blocks, 2, own), lambda h, p: (h, 0, 0, 0)), table, table],
            out_specs=[column] * 3,
        ),
        out_shape=[jax.ShapeDtypeStruct((blocks, own, wide), BF)] * 3,
        name="attend_back",
    )(place, query, key, value, *pieces, log_total, *tables)


def merge_kernel(spot, *refs, blocks, seqs):
    contexts = refs[: blocks * seqs]
    start, near, far, low, up, gain, middle, normed, down = refs[blocks * seqs :]
    tables = [lanes_of((far if i // 2 else near).at[:, pl.ds(i % 2, 1)], spot=spot) for i in range(blocks)]
    for seq in range(seqs):
        total = start[seq].astype(F32)
        small = jnp.zeros(down.shape[1:], F32)
        for step in range(blocks):
            rows = contexts[seq * blocks + step][...]
            small += nt(rows, low[step, seq])
            total += nn(rows, tables[step])
        small = (small * ADAPTER_SCALE).astype(BF)
        down[seq] = small
        total += nn(small, up[seq])
        middle[seq] = total
        normed[seq] = (norm_parts(total)[0] * gain[...]).astype(BF)


def merge(spot, contexts, start, near, far, low, up, gain):
    seqs, own, model = start.shape
    blocks, _, rank, wide = low.shape
    inputs = [piece for context in contexts for piece in context]
    inputs += [start, near, far, low, up, gain]
    results = [
        jax.ShapeDtypeStruct((seqs, own, model), F32),
        jax.ShapeDtypeStruct((seqs, own, model), BF),
        jax.ShapeDtypeStruct((seqs, own, rank), BF),
    ]
    return pl.pallas_call(
        lambda *refs: merge_kernel(*refs, blocks=blocks, seqs=seqs),
        grid_spec=pltpu.PrefetchScalarGridSpec(
            num_scalar_prefetch=1,
            grid=(1,),
            in_specs=[full(each.shape) for each in inputs],
            out_specs=[full(each.shape) for each in results],
        ),
        out_shape=results,
        name="merge",
    )(spot, *inputs)


def merge_back_kernel(spot, *refs, blocks):
    contexts = refs[:blocks]
    grad_normed, middle, out_grad, down, near, far, low, up, gain = refs[blocks : blocks + 9]
    grad_contexts = refs[blocks + 9 : 2 * blocks + 9]
    grad_middle, low_grad, up_grad = refs[2 * blocks + 9 :]
    normed, scale = norm_parts(middle[0])
    total = out_grad[0].astype(F32) + norm_back(grad_normed[0], normed, scale, gain[...])
    grad_middle[0] = total
    rows = total.astype(BF)
    small = (nt(rows, up[0]) * ADAPTER_SCALE).astype(BF)
    for step, out in enumerate(grad_contexts):
        ref = far if step // 2 else near
        table = lanes_of(ref.at[:, pl.ds(step % 2, 1)], spot=spot)
        out[...] = (nt(rows, table) + nn(small, low[step, 0])).astype(BF)
        low_grad[step] = tn(small, contexts[step][...])
    up_grad[...] = tn(down[0], rows)


def merge_back(spot, seq, contexts, grad_normed, middle, out_grad, down, near, far, low, up, gain):
    _, own, model = middle.shape
    blocks, _, rank, wide = low.shape
    row = pl.BlockSpec((1, own, model), lambda i, p: (seq, 0, 0))
    one = full((1, own, model))
    *grads, grad_middle, low_grad, up_grad = pl.pallas_call(
        lambda *refs: merge_back_kernel(*refs, blocks=blocks),
        grid_spec=pltpu.PrefetchScalarGridSpec(
        num_scalar_prefetch=1,
        grid=(1,),
        in_specs=[full((own, wide))] * blocks
        + [
            row,
            row,
            row,
            pl.BlockSpec((1, own, rank), lambda i, p: (seq, 0, 0)),
            full(near.shape),
            full(far.shape),
            pl.BlockSpec((blocks, 1, rank, wide), lambda i, p: (0, seq, 0, 0)),
            pl.BlockSpec((1, rank, model), lambda i, p: (seq, 0, 0)),
            full((1, model)),
        ],
        out_specs=[full((own, wide))] * blocks
        + [one, full((blocks, rank, wide)), full((rank, model))],
        ),
        out_shape=[jax.ShapeDtypeStruct((own, wide), BF)] * blocks
        + [
            jax.ShapeDtypeStruct((1, own, model), F32),
            jax.ShapeDtypeStruct((blocks, rank, wide), F32),
            jax.ShapeDtypeStruct((rank, model), F32),
        ],
        name="merge_back",
    )(spot, *contexts, grad_normed, middle, out_grad, down, near, far, low, up, gain)
    return grads, grad_middle, low_grad, up_grad


def gated_kernel(
    place, rows, out_grad, expand, shrink, expand_up, shrink_low, expand_low, shrink_up, mask,
    total, grad_rows, expand_up_grad, shrink_low_grad, expand_low_grad, shrink_up_grad,
    down, down_grad, late, late_grad, *, width, blocks
):
    step = pl.program_id(0)
    scaled = ADAPTER_SCALE * mask[...]

    @pl.when(step == 0)
    def _():
        total[...] = jnp.zeros(total.shape, F32)
        grad_rows[...] = jnp.zeros(grad_rows.shape, F32)
        down[...] = (nt(rows[...], expand_low[...]) * scaled).astype(BF)
        down_grad[...] = (nt(out_grad[...], shrink_up[...]) * scaled).astype(BF)
        late[...] = jnp.zeros(late.shape, F32)
        late_grad[...] = jnp.zeros(late_grad.shape, F32)

    values = lanes_of(expand, 0, width)
    gates = lanes_of(expand, width, width)
    outs = lanes_of(shrink)
    up_values = expand_up[0, :, :width]
    up_gates = expand_up[0, :, expand_up.shape[2] // 2 : expand_up.shape[2] // 2 + width]
    low_outs = shrink_low[0, :, :width]
    first = nt(rows[...], values) + nn(down[...], up_values)
    second = nt(rows[...], gates) + nn(down[...], up_gates)
    chance = 0.5 + 0.5 * lax.erf(first * (0.5**0.5))
    curve = first * chance
    slope = chance + first * (jnp.exp(-0.5 * first * first) * 0.3989422804014327)
    active = (curve * second).astype(BF)
    grads = nt(out_grad[...], outs) + nn(down_grad[...], low_outs)
    first_grad = (grads * second * slope).astype(BF)
    second_grad = (grads * curve).astype(BF)
    total[...] += nn(active, outs)
    late[...] += nt(active, low_outs)
    grad_rows[...] += nn(first_grad, values) + nn(second_grad, gates)
    late_grad[...] += nt(first_grad, up_values) + nt(second_grad, up_gates)
    expand_up_grad[0, 0] = tn(down[...], first_grad)
    expand_up_grad[0, 1] = tn(down[...], second_grad)
    shrink_low_grad[0] = tn(down_grad[...], active)

    @pl.when(step == blocks - 1)
    def _():
        small = (late[...] * scaled).astype(BF)
        total[...] += nn(small, shrink_up[...])
        shrink_up_grad[...] = tn(small, out_grad[...])
        small_grad = (late_grad[...] * scaled).astype(BF)
        grad_rows[...] += nn(small_grad, expand_low[...])
        expand_low_grad[...] = tn(small_grad, rows[...])


def gated(place, rows, out_grad, weights, width, expand_up, shrink_low, expand_low, shrink_up, mask):
    count, model = rows.shape
    parts, blocks, _, lane = weights.shape
    rank = expand_low.shape[0]
    pad = shrink_low.shape[2]
    return pl.pallas_call(
        lambda *refs: gated_kernel(*refs, width=width, blocks=blocks),
        grid_spec=pltpu.PrefetchScalarGridSpec(
        num_scalar_prefetch=1,
        grid=(blocks,),
        in_specs=[
            full((count, model)),
            full((count, model)),
            pl.BlockSpec((parts, 1, 2 * width, lane), lambda m, p: (0, m, 0, 0)),
            pl.BlockSpec((parts, 1, width, lane), lambda m, p: (0, m, 2, 0)),
            pl.BlockSpec((1, rank, 2 * pad), lambda m, p: (p[0] ^ m, 0, 0)),
            pl.BlockSpec((1, rank, pad), lambda m, p: (p[0] ^ m, 0, 0)),
            full((rank, model)),
            full((rank, model)),
            full((count, rank)),
        ],
        out_specs=[
            full((count, model)),
            full((count, model)),
            pl.BlockSpec((1, 2, rank, width), lambda m, p: (m, 0, 0, 0)),
            pl.BlockSpec((1, rank, width), lambda m, p: (m, 0, 0)),
            full((rank, model)),
            full((rank, model)),
        ],
        scratch_shapes=[
            pltpu.VMEM((count, rank), BF),
            pltpu.VMEM((count, rank), BF),
            pltpu.VMEM((count, rank), F32),
            pltpu.VMEM((count, rank), F32),
        ],
        ),
        out_shape=[
            jax.ShapeDtypeStruct((count, model), F32),
            jax.ShapeDtypeStruct((count, model), F32),
            jax.ShapeDtypeStruct((blocks, 2, rank, width), F32),
            jax.ShapeDtypeStruct((blocks, rank, width), F32),
            jax.ShapeDtypeStruct((rank, model), F32),
            jax.ShapeDtypeStruct((rank, model), F32),
        ],
        name="gated",
    )(place, rows, out_grad, weights, weights, expand_up, shrink_low, expand_low, shrink_up, mask)


def settle_early_kernel(place, got, low, shrink_up, merge_up, merge_low, expand_up, shrink_low, *, parts, blocks, sets, part, wide, width, pad):
    at = 3 * part
    for g in range(parts):
        for block in range(blocks):
            rows = got[g * blocks + block, :, :at].astype(F32)
            for i, out in enumerate((low, shrink_up, merge_up)):
                for two in range(2):
                    cut = rows[two * sets : (two + 1) * sets, i * part : (i + 1) * part]
                    out[:, two * parts + g, block * part : (block + 1) * part] = cut
        rows = got[g * blocks + place[0], :, at:].astype(F32)
        for two in range(2):
            cut = rows[two * sets : (two + 1) * sets]
            rank = two * parts + g
            merge_low[:, rank, :] = cut[:, :wide]
            for kind in range(2):
                first = wide + kind * pad
                expand_up[:, rank, kind, :] = cut[:, first : first + width]
            shrink_low[:, rank, :] = cut[:, wide + 2 * pad : wide + 2 * pad + width]


def settle_early(place, got, parts, sets, wide, width, pad):
    owners, rows, features = got.shape
    blocks = owners // parts
    rank = rows // sets * parts
    part = (features - wide - 3 * pad) // 3
    model = blocks * part
    shapes = [(rank, model)] * 3 + [(rank, wide), (rank, 2, width), (rank, width)]
    shapes = [(sets,) + shape for shape in shapes]
    whole = lambda shape: pl.BlockSpec(shape, lambda i, p: (0,) * len(shape))
    return pl.pallas_call(
        lambda *refs: settle_early_kernel(
            *refs, parts=parts, blocks=blocks, sets=sets, part=part, wide=wide, width=width, pad=pad
        ),
        grid_spec=pltpu.PrefetchScalarGridSpec(
            num_scalar_prefetch=1,
            grid=(1,),
            in_specs=[whole(got.shape)],
            out_specs=[whole(shape) for shape in shapes],
        ),
        out_shape=[jax.ShapeDtypeStruct(shape, F32) for shape in shapes],
        name="settle_early",
    )(place, got)


def settle_late_kernel(got, low, up, *, parts, blocks, sets, part, piece):
    wide = up.shape[3]
    for g in range(parts):
        rows = [got[g * blocks + block].astype(F32) for block in range(blocks)]
        tail = jnp.concatenate([row[:, part : part + piece] for row in rows], axis=1)
        for two in range(2):
            rank = two * parts + g
            for block, row in enumerate(rows):
                low[:, rank, block * part : (block + 1) * part] = row[two * sets : (two + 1) * sets, :part]
            for kind in range(up.shape[1]):
                up[:, kind, rank, :] = tail[two * sets : (two + 1) * sets, kind * wide : (kind + 1) * wide]


def settle_late(got, parts, sets, part, wide):
    owners, rows, features = got.shape
    blocks = owners // parts
    rank = rows // sets * parts
    piece = features - part
    shapes = [(sets, rank, blocks * part), (sets, blocks * piece // wide, rank, wide)]
    return pl.pallas_call(
        lambda *refs: settle_late_kernel(*refs, parts=parts, blocks=blocks, sets=sets, part=part, piece=piece),
        grid=(1,),
        in_specs=[full(got.shape)],
        out_specs=[full(shape) for shape in shapes],
        out_shape=[jax.ShapeDtypeStruct(shape, F32) for shape in shapes],
        name="settle_late",
    )(got)


def pair_swap(values, bit):
    size = lax.axis_size("mp")
    return lax.ppermute(values, "mp", [(i, i ^ bit) for i in range(size)])


def tie(values, after):
    return lax.optimization_barrier((values, after))[0]


def swap_all(values, axes):
    return lax.all_to_all(values, axes, 0, 0, tiled=True)


def share_all(values, axes):
    size = 1
    for axis in (axes,) if isinstance(axes, str) else axes:
        size *= lax.axis_size(axis)
    return swap_all(jnp.broadcast_to(values[None], (size,) + values.shape), axes)


def gather_parts(values):
    parts = lax.axis_size("dp")
    here = lax.axis_index("dp")
    every = jnp.arange(parts, dtype=jnp.int32)
    if parts != 8:
        return share_all(values, "dp"), every
    stack = [values]
    for shift in range(2, parts, 2):
        stack.append(lax.ppermute(values, "dp", [(i, (i + shift) % parts) for i in range(parts)]))
    stack = jnp.stack(stack)
    other = lax.ppermute(stack, "dp", [(i, i ^ 1) for i in range(parts)])
    order = (every % 2 ^ here % 2) * (parts // 2) + (here // 2 - every // 2) % (parts // 2)
    return jnp.concatenate([stack, other]), order.astype(jnp.int32)


def full_lanes(whole):
    parts, blocks, count, own = whole.shape
    if own == LANES:
        return whole
    tiles = parts * own // LANES
    whole = whole.transpose(1, 2, 0, 3).reshape(blocks, count, tiles, LANES)
    return whole.transpose(2, 0, 1, 3)


def local(
    hidden,
    cotangent,
    adapter_ids,
    attn_gain,
    mlp_gain,
    joined_weight,
    merge_weight_matrix,
    expand_weight,
    shrink_weight_matrix,
    joined_lower,
    joined_up_matrices,
    merge_lower,
    merge_up_matrices,
    expand_lower,
    expand_up_matrices,
    shrink_lower,
    shrink_up_matrices,
):
    parts, blocks = lax.axis_size("dp"), lax.axis_size("mp")
    place = lax.axis_index("mp")
    pair, core = place // 2, place % 2
    spot = place[None].astype(jnp.int32)
    seqs, own, model = hidden.shape
    length = own * blocks
    row_in = joined_weight.shape[0]
    wide = joined_weight.shape[2]
    width = expand_weight.shape[2]
    rank = joined_lower.shape[2]
    count = seqs * own

    rest = jnp.concatenate(
        [expand_weight.reshape(row_in, 2 * width).T, shrink_weight_matrix.T], axis=0
    )
    rest_whole = full_lanes(
        lax.all_gather(rest, ("dp", "mp"), axis=0, tiled=True).reshape(parts, blocks, 3 * width, row_in)
    )

    note = jnp.zeros((8, row_in), BF).at[0, :seqs].set(adapter_ids.astype(BF))
    joined_mine = jnp.concatenate(
        [joined_weight.reshape(row_in, 3 * wide).T, merge_weight_matrix.T, note], axis=0
    )
    joined_got, order = gather_parts(joined_mine)
    every_id = joined_got[:, 4 * wide, :seqs][order].astype(jnp.int32)
    if row_in != LANES:
        order = jnp.arange(model // LANES, dtype=jnp.int32)
    spot = jnp.concatenate([spot, order])
    joined_whole = full_lanes(joined_got[:, None])

    attn_scale = attn_gain.astype(F32)[None, :]
    mlp_scale = mlp_gain.astype(F32)[None, :]
    first_normed, first_scale = norm_parts(hidden.astype(F32))
    normed = (first_normed * attn_scale).astype(BF)
    def pick(table):
        return table.at[adapter_ids].get(mode="promise_in_bounds")

    def pick_low(table):
        return pick(table).transpose(0, 2, 1)

    def pick_up(table):
        return pick(table).reshape(seqs, rank, -1)

    joined_low, joined_up = pick_low(joined_lower), pick_up(joined_up_matrices)
    expand_low = pick_low(expand_lower).reshape(seqs * rank, model)
    merge_up = pick_up(merge_up_matrices)
    shrink_up = pick_up(shrink_up_matrices).reshape(seqs * rank, model)
    pad = -(-width // LANES) * LANES
    side = [(0, 0), (0, 0), (0, pad - width)]
    expand_mine = pick(expand_up_matrices)
    mine = jnp.concatenate(
        [
            pick_low(merge_lower),
            jnp.pad(expand_mine[:, :, 0], side),
            jnp.pad(expand_mine[:, :, 1], side),
            jnp.pad(pick_low(shrink_lower), side),
        ],
        axis=2,
    )
    far_sets = pair_swap(mine, 2)
    split_sets = jnp.stack([mine, pair_swap(mine, 1), far_sets, pair_swap(far_sets, 1)])
    merge_low = split_sets[:, :, :, :wide]
    expand_up = split_sets[:, :, :, wide : wide + 2 * pad].reshape(blocks, seqs * rank, 2 * pad)
    shrink_low = split_sets[:, :, :, wide + 2 * pad :].reshape(blocks, seqs * rank, pad)
    mask = (
        (jnp.arange(count) // own)[:, None] == (jnp.arange(seqs * rank) // rank)[None, :]
    ).astype(F32)

    half = HEAD_DIM // 2
    inverse = ROPE_BASE ** (-((jnp.arange(LANES) % half).astype(F32) * 2.0 / HEAD_DIM))
    angles = jnp.arange(length, dtype=F32)[:, None] * inverse[None, :]
    tables = [table.reshape(blocks, own, LANES) for table in (jnp.cos(angles), jnp.sin(angles))]

    across = pair_swap(normed, 2)
    beside = pair_swap(normed, 1)
    (
        across, joined_low, joined_up, tables, merge_low, merge_up,
        expand_low, expand_up, shrink_low, shrink_up, mask,
    ) = lax.optimization_barrier(
        (
            across, joined_low, joined_up, tables, merge_low, merge_up,
            expand_low, expand_up, shrink_low, shrink_up, mask,
        )
    )
    corner = pair_swap(across, 1)
    pieces = (normed, beside, across, corner)
    query, key, value, joined_down = project(
        spot, pieces, joined_whole, joined_low, joined_up,
        tables,
    )
    merge_own = joined_whole[:, :, 3 * wide : 4 * wide]
    merge_near = jnp.concatenate([merge_own, pair_swap(merge_own, 1)], axis=1)
    contexts, logs = [], []
    for seq in range(seqs):
        if seq:
            query = tie(query, context[0])
        context, log_total = attend(spot, query, key, value, seq)
        context = [context[0]] + [pair_swap(context[bit], bit) for bit in range(1, blocks)]
        contexts.append(context)
        logs.append(log_total)
    merge_far = pair_swap(merge_near, 2)
    middle, normed_mlp, merge_down = merge(
        spot, contexts, hidden, merge_near, merge_far, merge_low, merge_up, mlp_scale
    )
    (
        shrunk,
        grad_normed_mlp,
        expand_up_grad,
        shrink_low_grad,
        expand_low_grad,
        shrink_up_grad,
    ) = gated(
        spot, normed_mlp.reshape(count, model), cotangent.reshape(count, model), rest_whole, width,
        expand_up, shrink_low, expand_low, shrink_up, mask,
    )
    result = (middle + shrunk.reshape(middle.shape)).astype(BF)
    grad_normed_mlp = grad_normed_mlp.reshape(seqs, own, model)

    paired = rank == 2 * parts
    everyone = ("dp", "mp")
    owners = parts * blocks
    ids = jnp.broadcast_to(every_id[:, None], (parts, blocks, seqs))
    choose = (jnp.arange(ADAPTERS)[:, None] == ids.reshape(1, -1)).astype(BF)
    choose_own = (jnp.arange(ADAPTERS)[:, None] == every_id.reshape(1, -1)).astype(BF)
    part_width = model // blocks

    def by_block(grad):
        return grad.reshape(seqs * rank, blocks, -1).transpose(1, 0, 2)

    def ranks_out(grad):
        if paired:
            split = grad.reshape(grad.shape[0], seqs, 2, parts, -1).transpose(3, 0, 1, 2, 4)
            return split.reshape(split.shape[:3] + (-1,))
        return grad.reshape(grad.shape[0], seqs, parts, -1).transpose(2, 0, 1, 3)

    def ranks_in(whole, features):
        whole = whole.transpose(2, 1, 0, 3).reshape(ADAPTERS, whole.shape[1], rank, features)
        return whole.transpose(0, 2, 1, 3)

    def tall(values):
        return values.transpose(0, 2, 1).astype(F32)

    merge_low_grads, merge_up_grads, joined_low_grads, joined_up_grads = [], [], [], []
    halfway, grad_normeds = [], []
    for seq in range(seqs):
        if seq:
            grad_normed_mlp = tie(grad_normed_mlp, grad_middle)
        if seq == 2:
            grad_normed_mlp = tie(grad_normed_mlp, halfway[0][1][2:])
        pieces_back, grad_middle, low_grad, up_grad = merge_back(
            spot, seq, contexts[seq], grad_normed_mlp, middle, cotangent, merge_down,
            merge_near, merge_far, merge_low, merge_up, mlp_scale,
        )
        merge_low_grads.append(low_grad)
        merge_up_grads.append(up_grad)
        pieces_back = [pieces_back[0]] + [pair_swap(pieces_back[bit], bit) for bit in range(1, blocks)]
        halfway.append((grad_middle[0], pieces_back))

    early = jnp.concatenate(
        [
            piece.astype(BF)
            for piece in (
                by_block(expand_low_grad),
                by_block(shrink_up_grad),
                by_block(jnp.concatenate(merge_up_grads)),
                jnp.take(jnp.concatenate(merge_low_grads, axis=1), place ^ jnp.arange(blocks), axis=0),
                jnp.pad(expand_up_grad[:, 0], side),
                jnp.pad(expand_up_grad[:, 1], side),
                jnp.pad(shrink_low_grad, side),
            )
        ],
        axis=2,
    )
    early_width = early.shape[2]

    early = tie(early, halfway[0][1][2])
    early = swap_all(ranks_out(early).reshape(owners, seqs, -1), everyone)
    chip, far = None, None
    for seq in range(seqs):
        grad_middle, pieces_back = halfway[seq]
        if seq:
            pieces_back[0] = tie(pieces_back[0], here)
        grads = list(attend_back(spot, query, key, value, seq, pieces_back, logs[seq], tables))
        if seq == 0:
            grads[0], halfway[1], halfway[2] = lax.optimization_barrier((grads[0], halfway[1], halfway[2]))
        if seq == 1:
            grads[0], far, early = lax.optimization_barrier((grads[0], far, early))
            early = jnp.dot(choose, early.reshape(owners * seqs, -1), preferred_element_type=F32)
            if paired:
                early = jnp.concatenate([early[:, :early_width], early[:, early_width:]], axis=0)
            shared = lax.all_gather(early.astype(BF), everyone, axis=0)
        if seq == 2:
            grads[0], far = lax.optimization_barrier((grads[0], far))
        if seq:
            grad_normeds.append(chip + far.astype(F32))
        small_grad, up_grad, low_grad = joined_grads(spot, seq, grads, pieces, joined_up, joined_down)
        here, there = project_back(spot, seq, grads, small_grad, joined_whole, joined_low)
        joined_up_grads.append(up_grad)
        joined_low_grads.append(low_grad)
        there = pair_swap(there, 1).astype(F32)
        chip, give = here[0] + there[0], (here[1] + there[1]).astype(BF)
        far = pair_swap(give, 2)

    piece = 3 * wide // blocks
    late_low = ranks_out(by_block(jnp.concatenate(joined_low_grads)).astype(BF))
    late_up = jnp.stack(joined_up_grads).astype(BF).reshape(seqs * rank, blocks, piece)
    late_up = ranks_out(late_up.transpose(1, 0, 2))
    some = 2 if paired else 1
    late_low, late_up = (each.reshape(owners, seqs * some, -1) for each in (late_low, late_up))
    low_size = late_low.shape[2]
    late = jnp.concatenate([late_low, late_up], axis=2)
    late = tie(late, give)
    late, far = lax.optimization_barrier((swap_all(late, everyone), far))
    late = late.reshape(parts, blocks, seqs, some, -1)
    grad_normeds.append(chip + far.astype(F32))
    grad_middle = jnp.stack([each[0] for each in halfway])
    grad_hidden = grad_middle + norm_back(jnp.stack(grad_normeds), first_normed, first_scale, attn_scale)
    late_low = late[..., :low_size].reshape(owners * seqs, -1)
    late_up = late[..., low_size:].transpose(1, 0, 2, 3, 4).reshape(blocks, parts * seqs, -1)
    late_low = jnp.dot(choose, late_low, preferred_element_type=F32).astype(BF)
    late_up = jnp.einsum("as,bsf->baf", choose_own, late_up, preferred_element_type=F32).astype(BF)
    if paired:
        half_low, half_up = late_low.shape[1] // 2, late_up.shape[2] // 2
        late_low = jnp.concatenate([late_low[:, :half_low], late_low[:, half_low:]], axis=0)
        late_up = jnp.concatenate([late_up[:, :, :half_up], late_up[:, :, half_up:]], axis=1)
    late = jnp.concatenate(
        [jnp.broadcast_to(late_low[None], (blocks,) + late_low.shape), late_up], axis=2
    )
    late = jnp.broadcast_to(late[None], (parts,) + late.shape).reshape((owners,) + late.shape[1:])
    late = swap_all(late, everyone)
    if paired:
        (
            expand_low_out, shrink_up_out, merge_up_out, merge_low_out, expand_up_out, shrink_low_out,
        ) = settle_early(spot, shared, parts, ADAPTERS, wide, width, pad)
        late, shrink_up_out = lax.optimization_barrier((late, shrink_up_out))
        joined_low_out, joined_up_out = settle_late(late, parts, ADAPTERS, part_width, wide)
        joined_up_out = joined_up_out.transpose(0, 2, 1, 3)
        joined_low_out, expand_low_out, merge_low_out, shrink_low_out = (
            tall(each) for each in (joined_low_out, expand_low_out, merge_low_out, shrink_low_out)
        )
    else:
        late = late.reshape(parts, blocks, ADAPTERS, -1)
        joined_low_out = tall(ranks_in(late[..., :low_size], part_width).reshape(ADAPTERS, rank, model))
        joined_up_out = ranks_in(late[..., low_size:], piece).reshape(ADAPTERS, rank, 3, wide).astype(F32)
        shared = ranks_in(shared.reshape(parts, blocks, ADAPTERS, -1), early_width).astype(F32)
        expand_low_out, shrink_up_out, merge_up_out = (
            shared[..., i * part_width : (i + 1) * part_width].reshape(ADAPTERS, rank, model)
            for i in range(3)
        )
        expand_low_out = tall(expand_low_out)
        divided = lax.dynamic_index_in_dim(shared[..., 3 * part_width :], place, 2, keepdims=False)
        merge_low_out = tall(divided[:, :, :wide])
        expand_up_out = jnp.stack(
            [divided[:, :, wide + i * pad : wide + i * pad + width] for i in range(2)], axis=2
        )
        shrink_low_out = tall(divided[:, :, wide + 2 * pad : wide + 2 * pad + width])
    return (
        result,
        grad_hidden.astype(BF),
        joined_low_out,
        joined_up_out,
        merge_low_out,
        merge_up_out,
        expand_low_out,
        expand_up_out,
        shrink_low_out,
        shrink_up_out,
    )


def solution(mesh):
    in_specs = (
        P("dp", "mp", None),
        P("dp", "mp", None),
        P("dp"),
        P(),
        P(),
        P("dp", None, "mp"),
        P("dp", "mp"),
        P("dp", None, "mp"),
        P("dp", "mp"),
        P(),
        P(None, None, None, "mp"),
        P(None, "mp", None),
        P(),
        P(),
        P(None, None, None, "mp"),
        P(None, "mp", None),
        P(),
    )
    out_specs = (
        P("dp", "mp", None),
        P("dp", "mp", None),
        P(),
        P(None, None, None, "mp"),
        P(None, "mp", None),
        P(),
        P(),
        P(None, None, None, "mp"),
        P(None, "mp", None),
        P(),
    )
    return jax.shard_map(local, mesh=mesh, in_specs=in_specs, out_specs=out_specs, check_vma=False)
```

```python
import jax
import jax.numpy as jnp
from jax import lax
from jax.experimental import pallas as pl
from jax.experimental.pallas import tpu as pltpu
from jax.sharding import PartitionSpec as P

HEAD_DIM = 64
ADAPTERS = 8
ADAPTER_SCALE = 2.0
NORM_EPS = 1e-05
ROPE_BASE = 160000.0
LANES = 128
BF = jnp.bfloat16
F32 = jnp.float32


def nt(a, b):
    return lax.dot_general(a, b, (((1,), (1,)), ((), ())), preferred_element_type=F32)


def nn(a, b):
    return lax.dot_general(a, b, (((1,), (0,)), ((), ())), preferred_element_type=F32)


def tn(a, b):
    return lax.dot_general(a, b, (((0,), (0,)), ((), ())), preferred_element_type=F32)


def lanes_of(ref, first=0, count=None, spot=None):
    count = ref.shape[2] if count is None else count
    places = [part if spot is None else spot[1 + part] for part in range(ref.shape[0])]
    return jnp.concatenate([ref[place, 0, pl.ds(first, count), :] for place in places], axis=1)


def full(shape):
    return pl.BlockSpec(shape, lambda *_: (0,) * len(shape))


def full_once(shape):
    return pl.BlockSpec(shape, lambda *_: (0,) * len(shape), pipeline_mode=pl.Buffered(1))


def norm_parts(values):
    centred = values - jnp.mean(values, axis=-1, keepdims=True)
    spread = jnp.mean(centred * centred, axis=-1, keepdims=True)
    scale = lax.rsqrt(spread + NORM_EPS)
    return centred * scale, scale


def norm_back(grads, normed, scale, gain):
    weighted = grads * gain
    return scale * (
        weighted
        - jnp.mean(weighted, axis=-1, keepdims=True)
        - normed * jnp.mean(weighted * normed, axis=-1, keepdims=True)
    )


def turn(values, cosine, sine):
    width = values.shape[1]
    half = HEAD_DIM // 2
    many = width // LANES
    if many > 1:
        cosine = jnp.concatenate([cosine] * many, axis=1)
        sine = jnp.concatenate([sine] * many, axis=1)
    lane = lax.broadcasted_iota(jnp.int32, values.shape, 1)
    turned = jnp.where(
        lane % HEAD_DIM < half,
        -pltpu.roll(values, width - half, 1),
        pltpu.roll(values, half, 1),
    )
    return values * cosine + turned * sine


def project_kernel(
    place, own, beside, across, corner, weight, low, up, cosine, sine,
    query, key, value, down, *, wide
):
    table = lanes_of(weight, 0, 3 * wide, place)
    for step, piece in enumerate((own, beside, across, corner)):
        spot = place[0] ^ step
        rows = piece[0]
        small = (nt(rows, low[0]) * ADAPTER_SCALE).astype(BF)
        down[0, step] = small
        out = nt(rows, table) + nn(small, up[0])
        cos, sin = cosine[spot], sine[spot]
        turned = turn(out[:, :wide], cos, sin)
        query[0, spot] = (turned * HEAD_DIM**-0.5).astype(BF)
        key[0, spot] = turn(out[:, wide : 2 * wide], cos, sin).astype(BF)
        value[0, spot] = out[:, 2 * wide :].astype(BF)


def project(place, pieces, weight, low, up, tables):
    seqs, own, model = pieces[0].shape
    tall = up.shape[2]
    wide = tall // 3
    rank = low.shape[1]
    blocks = len(pieces)
    piece = pl.BlockSpec((1, own, model), lambda s, p: (s, 0, 0))
    result = pl.BlockSpec((1, blocks, own, wide), lambda s, p: (s, 0, 0, 0))
    table = pl.BlockSpec((blocks, own, LANES), lambda s, p: (0, 0, 0))
    return pl.pallas_call(
        lambda *refs: project_kernel(*refs, wide=wide),
        grid_spec=pltpu.PrefetchScalarGridSpec(
            num_scalar_prefetch=1,
            grid=(seqs,),
            in_specs=[piece] * blocks
            + [
                pl.BlockSpec(weight.shape, lambda s, p: (0, 0, 0, 0)),
                pl.BlockSpec((1, rank, model), lambda s, p: (s, 0, 0)),
                pl.BlockSpec((1, rank, tall), lambda s, p: (s, 0, 0)),
                table,
                table,
            ],
            out_specs=[result] * 3
            + [pl.BlockSpec((1, blocks, own, rank), lambda s, p: (s, 0, 0, 0))],
        ),
        out_shape=[jax.ShapeDtypeStruct((seqs, blocks, own, wide), BF)] * 3
        + [jax.ShapeDtypeStruct((seqs, blocks, own, rank), BF)],
        name="project",
    )(place, *pieces, weight, low, up, *tables)


def one_head(values, head):
    lane = lax.broadcasted_iota(jnp.int32, values.shape, 1)
    return jnp.where((lane // HEAD_DIM) == head, values, jnp.zeros_like(values))


def attend_kernel(place, query, key, value, *outs):
    *contexts, probs, shrinks = outs
    blocks, own = query.shape[1:3]
    keys = key[0].reshape(blocks * own, LANES)
    turned = value[0].reshape(blocks * own, LANES).T
    for step in range(0, blocks, 2):
        rows = jnp.concatenate([query[0, place[0] ^ (step + i)] for i in range(2)], axis=0)
        parts = []
        for head in range(2):
            scores = nt(keys, one_head(rows, head))
            top = jnp.max(scores, axis=0, keepdims=True)
            raised = jnp.exp(scores - top)
            shrink = 1.0 / jnp.sum(raised, axis=0, keepdims=True)
            raised = raised.astype(BF)
            probs[0, step // 2, head] = raised
            shrinks[0, step // 2, head : head + 1] = shrink
            parts.append(nn(turned[head * HEAD_DIM : (head + 1) * HEAD_DIM], raised) * shrink)
        merged = jnp.concatenate(parts, axis=0).T.astype(BF)
        for i in range(2):
            contexts[step + i][...] = merged[i * own : (i + 1) * own]


def attend(place, query, key, value, seq):
    _, blocks, own, wide = query.shape
    pairs = wide // LANES
    whole = pl.BlockSpec((1, blocks, own, LANES), lambda h, p: (seq, 0, 0, h))
    *contexts, probs, shrinks = pl.pallas_call(
        attend_kernel,
        grid_spec=pltpu.PrefetchScalarGridSpec(
            num_scalar_prefetch=1,
            grid=(pairs,),
            in_specs=[whole] * 3,
            out_specs=[pl.BlockSpec((own, LANES), lambda h, p: (0, h))] * blocks
            + [
                pl.BlockSpec((1, blocks // 2, 2, blocks * own, 2 * own), lambda h, p: (h, 0, 0, 0, 0)),
                pl.BlockSpec((1, blocks // 2, 2, 2 * own), lambda h, p: (h, 0, 0, 0)),
            ],
        ),
        out_shape=[jax.ShapeDtypeStruct((own, wide), BF)] * blocks
        + [
            jax.ShapeDtypeStruct((pairs, blocks // 2, 2, blocks * own, 2 * own), BF),
            jax.ShapeDtypeStruct((pairs, blocks // 2, 2, 2 * own), F32),
        ],
        name="attend",
    )(place, query, key, value)
    return contexts, (probs, shrinks, list(contexts))


def attend_back_kernel(place, query, key, value, probs, shrinks, *refs):
    blocks, own = query.shape[1:3]
    contexts = refs[:blocks]
    pieces = refs[blocks : 2 * blocks]
    rows_in = refs[2 * blocks : 3 * blocks]
    cosine, sine, weight, low, up, down, here, there, up_grad, low_grad, total, small, turn_keys = refs[3 * blocks :]
    pair = pl.program_id(0)
    last = pl.num_programs(0) - 1
    wide = LANES * pl.num_programs(0)
    keys = key[0].reshape(blocks * own, LANES)
    values = value[0].reshape(blocks * own, LANES)
    turned = keys.T
    backs, mines, mine_grads = [], [], []
    grad_queries = []
    for step in range(0, blocks, 2):
        spots = [place[0] ^ (step + i) for i in range(2)]
        rows = jnp.concatenate([query[0, spot] for spot in spots], axis=0)
        outer = jnp.concatenate([pieces[step + i][0] for i in range(2)], axis=0).astype(F32)
        inner = jnp.concatenate([contexts[step + i][...] for i in range(2)], axis=0).astype(F32)
        product = (outer * inner).T
        factors = [shrinks[0, step // 2, head : head + 1] for head in range(2)]
        spread = jnp.concatenate([jnp.broadcast_to(f, (HEAD_DIM, 2 * own)) for f in factors], axis=0).T
        outer = (outer * spread).astype(BF)
        parts = []
        for head in range(2):
            mine_grad = one_head(outer, head)
            chances = probs[0, step // 2, head]
            half = product[head * HEAD_DIM : (head + 1) * HEAD_DIM]
            mean = jnp.sum(half, axis=0, keepdims=True) * factors[head]
            back = (chances.astype(F32) * (nt(values, mine_grad) - mean)).astype(BF)
            parts.append(nn(turned[head * HEAD_DIM : (head + 1) * HEAD_DIM], back))
            backs.append(back)
            mines.append(one_head(rows, head))
            mine_grads.append(mine_grad)
        queries = jnp.concatenate(parts, axis=0).T * HEAD_DIM**-0.5
        for i, spot in enumerate(spots):
            part = queries[i * own : (i + 1) * own]
            grad_queries.append(turn(part, cosine[spot], -sine[spot]).astype(BF))
    grad_keys = nn(jnp.concatenate(backs, axis=1), jnp.concatenate(mines, axis=0))
    chances = [probs[0, i // 2, i % 2] for i in range(blocks)]
    grad_values = nn(jnp.concatenate(chances, axis=1), jnp.concatenate(mine_grads, axis=0))
    for step in range(blocks):
        part = slice(step * own, (step + 1) * own)
        turn_keys[0, step] = turn(grad_keys[part], cosine[step], -sine[step]).astype(BF)
        turn_keys[1, step] = grad_values[part].astype(BF)
    grads = [
        jnp.concatenate(grad_queries, axis=0),
        jnp.concatenate([turn_keys[0, place[0] ^ step] for step in range(blocks)], axis=0),
        jnp.concatenate([turn_keys[1, place[0] ^ step] for step in range(blocks)], axis=0),
    ]
    grads = jnp.concatenate(grads, axis=1)
    firsts = [pl.multiple_of(kind * wide + pair * LANES, LANES) for kind in range(3)]
    table = jnp.concatenate([lanes_of(weight, first, LANES, place) for first in firsts], axis=0)
    ups = jnp.concatenate([up[0, :, pl.ds(first, LANES)] for first in firsts], axis=1)
    downs = jnp.concatenate([down[0, step] for step in range(blocks)], axis=0)
    more = nn(grads, table)
    more_small = nt(grads, ups)
    up_part = tn(downs, grads)
    for kind in range(3):
        up_grad[kind] = up_part[:, kind * LANES : (kind + 1) * LANES]

    @pl.when(pair == 0)
    def _():
        total[...] = more
        small[...] = more_small

    @pl.when(pair > 0)
    def _():
        total[...] += more
        small[...] += more_small

    @pl.when(pair == last)
    def _():
        narrow = (small[...] * ADAPTER_SCALE).astype(BF)
        low_grad[...] = tn(narrow, jnp.concatenate([piece[0] for piece in rows_in], axis=0))
        done = total[...] + nn(narrow, low[0])
        for step in range(blocks):
            part = done[step * own : (step + 1) * own]
            if step % 2:
                there[step // 2] = part.astype(BF)
            else:
                here[step // 2] = part


def attend_back(place, seq, query, key, value, kept, grads, pieces, tables, weight, low, up, down):
    _, blocks, own, wide = query.shape
    _, rank, model = low.shape
    tall = up.shape[2]
    pairs = wide // LANES
    whole = lambda shape: pl.BlockSpec(shape, lambda h, p: (0,) * len(shape))
    of_seq = lambda shape: pl.BlockSpec((1,) + shape, lambda h, p: (seq,) + (0,) * len(shape))
    heads = pl.BlockSpec((1, blocks, own, LANES), lambda h, p: (seq, 0, 0, h))
    probs, shrinks, contexts = kept
    return pl.pallas_call(
        attend_back_kernel,
        grid_spec=pltpu.PrefetchScalarGridSpec(
            num_scalar_prefetch=1,
            grid=(pairs,),
            in_specs=[heads] * 3
            + [pl.BlockSpec((1,) + probs.shape[1:], lambda h, p: (h, 0, 0, 0, 0))]
            + [pl.BlockSpec((1,) + shrinks.shape[1:], lambda h, p: (h, 0, 0, 0))]
            + [pl.BlockSpec((own, LANES), lambda h, p: (0, h))] * blocks
            + [pl.BlockSpec((1, own, LANES), lambda h, p: (max(seq - 1, 0), 0, h))] * blocks
            + [of_seq((own, model))] * blocks
            + [whole((blocks, own, LANES))] * 2
            + [
                whole(weight.shape),
                of_seq((rank, model)),
                of_seq((rank, tall)),
                of_seq((blocks, own, rank)),
            ],
            out_specs=[
                whole((blocks // 2, own, model)),
                whole((blocks // 2, own, model)),
                pl.BlockSpec((3, rank, LANES), lambda h, p: (0, 0, h)),
                whole((rank, model)),
            ],
            scratch_shapes=[
                pltpu.VMEM((blocks * own, model), F32),
                pltpu.VMEM((blocks * own, rank), F32),
                pltpu.VMEM((2, blocks, own, LANES), BF),
            ],
        ),
        out_shape=[
            jax.ShapeDtypeStruct((blocks // 2, own, model), F32),
            jax.ShapeDtypeStruct((blocks // 2, own, model), BF),
            jax.ShapeDtypeStruct((3, rank, wide), F32),
            jax.ShapeDtypeStruct((rank, model), F32),
        ],
        name="attend_back",
    )(place, query, key, value, probs, shrinks, *contexts, *grads, *pieces, *tables, weight, low, up, down)


def merge_kernel(spot, *refs, blocks, seqs):
    contexts = refs[: blocks * seqs]
    start, near, far, low, up, gain, middle, normed, down = refs[blocks * seqs :]
    tables = [lanes_of((far if i // 2 else near).at[:, pl.ds(i % 2, 1)], spot=spot) for i in range(blocks)]
    for seq in range(seqs):
        total = start[seq].astype(F32)
        small = jnp.zeros(down.shape[1:], F32)
        for step in range(blocks):
            rows = contexts[seq * blocks + step][...]
            small += nt(rows, low[step, seq])
            total += nn(rows, tables[step])
        small = (small * ADAPTER_SCALE).astype(BF)
        down[seq] = small
        total += nn(small, up[seq])
        middle[seq] = total
        normed[seq] = (norm_parts(total)[0] * gain[...]).astype(BF)


def merge(spot, contexts, start, near, far, low, up, gain):
    seqs, own, model = start.shape
    blocks, _, rank, wide = low.shape
    inputs = [piece for context in contexts for piece in context]
    inputs += [start, near, far, low, up, gain]
    results = [
        jax.ShapeDtypeStruct((seqs, own, model), F32),
        jax.ShapeDtypeStruct((seqs, own, model), BF),
        jax.ShapeDtypeStruct((seqs, own, rank), BF),
    ]
    return pl.pallas_call(
        lambda *refs: merge_kernel(*refs, blocks=blocks, seqs=seqs),
        grid_spec=pltpu.PrefetchScalarGridSpec(
            num_scalar_prefetch=1,
            grid=(1,),
            in_specs=[full(each.shape) for each in inputs],
            out_specs=[full(each.shape) for each in results],
        ),
        out_shape=results,
        name="merge",
    )(spot, *inputs)


def gated_kernel(
    place, rows, out_grad, middle, expand, shrink, expand_up, shrink_low, expand_low, shrink_up, mask,
    near, far, merge_low, merge_up, gain, merge_down, *refs, width, blocks, seqs
):
    contexts = refs[: seqs * blocks]
    (
        result, expand_up_grad, shrink_low_grad, expand_low_grad, shrink_up_grad,
        grad_middle, merge_low_grad, merge_up_grad,
    ) = refs[seqs * blocks : seqs * blocks + 8]
    firsts = refs[seqs * blocks + 8 : seqs * blocks + 8 + blocks]
    others = refs[seqs * blocks + 8 + blocks : seqs * blocks + 8 + 2 * blocks]
    total, grad_rows, down, down_grad, late, late_grad = refs[seqs * blocks + 8 + 2 * blocks :]
    step = pl.program_id(0)
    scaled = ADAPTER_SCALE * mask[...]

    @pl.when(step == 0)
    def _():
        total[...] = middle[...]
        grad_rows[...] = jnp.zeros(grad_rows.shape, F32)
        down[...] = (nt(rows[...], expand_low[...]) * scaled).astype(BF)
        down_grad[...] = (nt(out_grad[...], shrink_up[...]) * scaled).astype(BF)
        late[...] = jnp.zeros(late.shape, F32)
        late_grad[...] = jnp.zeros(late_grad.shape, F32)

    values = lanes_of(expand, 0, width)
    gates = lanes_of(expand, width, width)
    outs = lanes_of(shrink)
    up_values = expand_up[0, :, :width]
    up_gates = expand_up[0, :, expand_up.shape[2] // 2 : expand_up.shape[2] // 2 + width]
    low_outs = shrink_low[0, :, :width]
    first = nt(rows[...], values) + nn(down[...], up_values)
    second = nt(rows[...], gates) + nn(down[...], up_gates)
    chance = 0.5 + 0.5 * lax.erf(first * (0.5**0.5))
    curve = first * chance
    slope = chance + first * (jnp.exp(-0.5 * first * first) * 0.3989422804014327)
    active = (curve * second).astype(BF)
    grads = nt(out_grad[...], outs) + nn(down_grad[...], low_outs)
    first_grad = (grads * second * slope).astype(BF)
    second_grad = (grads * curve).astype(BF)
    total[...] += nn(active, outs)
    late[...] += nt(active, low_outs)
    grad_rows[...] += nn(first_grad, values) + nn(second_grad, gates)
    late_grad[...] += nt(first_grad, up_values) + nt(second_grad, up_gates)
    expand_up_grad[0, 0] = tn(down[...], first_grad)
    expand_up_grad[0, 1] = tn(down[...], second_grad)
    shrink_low_grad[0] = tn(down_grad[...], active)

    @pl.when(step == blocks - 1)
    def _():
        small = (late[...] * scaled).astype(BF)
        result[...] = (total[...] + nn(small, shrink_up[...])).astype(BF)
        shrink_up_grad[...] = tn(small, out_grad[...])
        small_grad = (late_grad[...] * scaled).astype(BF)
        expand_low_grad[...] = tn(small_grad, rows[...])
        own = rows.shape[0] // seqs
        for seq in range(seqs):
            part = slice(seq * own, (seq + 1) * own)
            normed, scale = norm_parts(middle[part])
            grad_normed = grad_rows[part] + nn(small_grad[part], expand_low[...])
            whole = out_grad[part].astype(F32) + norm_back(grad_normed, normed, scale, gain[...])
            grad_middle[seq] = whole
            low_rows = whole.astype(BF)
            small = (nt(low_rows, merge_up[seq]) * ADAPTER_SCALE).astype(BF)
            for move in range(blocks):
                ref = far if move // 2 else near
                table = lanes_of(ref.at[:, pl.ds(move % 2, 1)], spot=place)
                out = (nt(low_rows, table) + nn(small, merge_low[move, seq])).astype(BF)
                if seq:
                    others[move][seq - 1] = out
                else:
                    firsts[move][0] = out
                merge_low_grad[seq, move] = tn(small, contexts[seq * blocks + move][...])
            merge_up_grad[seq] = tn(merge_down[seq], low_rows)


def gated(
    place, rows, out_grad, middle, weights, width, expand_up, shrink_low, expand_low, shrink_up, mask,
    near, far, merge_low, merge_up, gain, merge_down, contexts
):
    count, model = rows.shape
    parts, blocks, _, lane = weights.shape
    seqs = len(contexts)
    own, wide = contexts[0][0].shape
    some = merge_up.shape[1]
    rank = expand_low.shape[0]
    pad = shrink_low.shape[2]
    pieces = [piece for context in contexts for piece in context]
    shapes = [
        ((count, model), BF),
        ((blocks, 2, rank, width), F32),
        ((blocks, rank, width), F32),
        ((rank, model), F32),
        ((rank, model), F32),
        ((seqs, own, model), F32),
        ((seqs, blocks, some, wide), F32),
        ((seqs, some, model), F32),
    ]
    shapes += [((1, own, wide), BF)] * blocks + [((seqs - 1, own, wide), BF)] * blocks
    out_specs = [full_once(shape) for shape, _ in shapes]
    out_specs[1] = pl.BlockSpec((1, 2, rank, width), lambda m, p: (m, 0, 0, 0))
    out_specs[2] = pl.BlockSpec((1, rank, width), lambda m, p: (m, 0, 0))
    return pl.pallas_call(
        lambda *refs: gated_kernel(*refs, width=width, blocks=blocks, seqs=seqs),
        grid_spec=pltpu.PrefetchScalarGridSpec(
            num_scalar_prefetch=1,
            grid=(blocks,),
            in_specs=[
                full_once((count, model)),
                full_once((count, model)),
                full_once((count, model)),
                pl.BlockSpec((parts, 1, 2 * width, lane), lambda m, p: (0, m, 0, 0)),
                pl.BlockSpec((parts, 1, width, lane), lambda m, p: (0, m, 2, 0)),
                pl.BlockSpec((1, rank, 2 * pad), lambda m, p: (p[0] ^ m, 0, 0)),
                pl.BlockSpec((1, rank, pad), lambda m, p: (p[0] ^ m, 0, 0)),
                full_once((rank, model)),
                full_once((rank, model)),
                full_once((count, rank)),
                full_once(near.shape),
                full_once(far.shape),
                full_once(merge_low.shape),
                full_once(merge_up.shape),
                full_once(gain.shape),
                full_once(merge_down.shape),
            ]
            + [full_once((own, wide))] * len(pieces),
            out_specs=out_specs,
            scratch_shapes=[
                pltpu.VMEM((count, model), F32),
                pltpu.VMEM((count, model), F32),
                pltpu.VMEM((count, rank), BF),
                pltpu.VMEM((count, rank), BF),
                pltpu.VMEM((count, rank), F32),
                pltpu.VMEM((count, rank), F32),
            ],
        ),
        out_shape=[jax.ShapeDtypeStruct(shape, kind) for shape, kind in shapes],
        name="gated",
    )(
        place, rows, out_grad, middle, weights, weights, expand_up, shrink_low, expand_low, shrink_up, mask,
        near, far, merge_low, merge_up, gain, merge_down, *pieces,
    )


def settle_early_kernel(place, got, low, shrink_up, merge_up, merge_low, expand_up, shrink_low, *, parts, blocks, sets, part, wide, width, pad):
    at = 3 * part
    for g in range(parts):
        for block in range(blocks):
            rows = got[g * blocks + block, :, :at].astype(F32)
            for i, out in enumerate((low, shrink_up, merge_up)):
                for two in range(2):
                    cut = rows[two * sets : (two + 1) * sets, i * part : (i + 1) * part]
                    out[:, two * parts + g, block * part : (block + 1) * part] = cut
        rows = got[g * blocks + place[0], :, at:].astype(F32)
        for two in range(2):
            cut = rows[two * sets : (two + 1) * sets]
            rank = two * parts + g
            merge_low[:, rank, :] = cut[:, :wide]
            for kind in range(2):
                first = wide + kind * pad
                expand_up[:, rank, kind, :] = cut[:, first : first + width]
            shrink_low[:, rank, :] = cut[:, wide + 2 * pad : wide + 2 * pad + width]


def settle_early(place, got, parts, sets, wide, width, pad):
    owners, rows, features = got.shape
    blocks = owners // parts
    rank = rows // sets * parts
    part = (features - wide - 3 * pad) // 3
    model = blocks * part
    shapes = [(rank, model)] * 3 + [(rank, wide), (rank, 2, width), (rank, width)]
    shapes = [(sets,) + shape for shape in shapes]
    whole = lambda shape: pl.BlockSpec(shape, lambda i, p: (0,) * len(shape))
    return pl.pallas_call(
        lambda *refs: settle_early_kernel(
            *refs, parts=parts, blocks=blocks, sets=sets, part=part, wide=wide, width=width, pad=pad
        ),
        grid_spec=pltpu.PrefetchScalarGridSpec(
            num_scalar_prefetch=1,
            grid=(1,),
            in_specs=[whole(got.shape)],
            out_specs=[whole(shape) for shape in shapes],
        ),
        out_shape=[jax.ShapeDtypeStruct(shape, F32) for shape in shapes],
        name="settle_early",
    )(place, got)


def settle_late_kernel(got, low, up, *, parts, blocks, sets, part, piece):
    wide = up.shape[3]
    for g in range(parts):
        rows = [got[g * blocks + block].astype(F32) for block in range(blocks)]
        tail = jnp.concatenate([row[:, part : part + piece] for row in rows], axis=1)
        for two in range(2):
            rank = two * parts + g
            for block, row in enumerate(rows):
                low[:, rank, block * part : (block + 1) * part] = row[two * sets : (two + 1) * sets, :part]
            for kind in range(up.shape[1]):
                up[:, kind, rank, :] = tail[two * sets : (two + 1) * sets, kind * wide : (kind + 1) * wide]


def settle_late(got, parts, sets, part, wide):
    owners, rows, features = got.shape
    blocks = owners // parts
    rank = rows // sets * parts
    piece = features - part
    shapes = [(sets, rank, blocks * part), (sets, blocks * piece // wide, rank, wide)]
    return pl.pallas_call(
        lambda *refs: settle_late_kernel(*refs, parts=parts, blocks=blocks, sets=sets, part=part, piece=piece),
        grid=(1,),
        in_specs=[full(got.shape)],
        out_specs=[full(shape) for shape in shapes],
        out_shape=[jax.ShapeDtypeStruct(shape, F32) for shape in shapes],
        name="settle_late",
    )(got)


def pair_swap(values, bit):
    size = lax.axis_size("mp")
    return lax.ppermute(values, "mp", [(i, i ^ bit) for i in range(size)])


def tie(values, after):
    return lax.optimization_barrier((values, after))[0]


def swap_all(values, axes):
    return lax.all_to_all(values, axes, 0, 0, tiled=True)


def share_all(values, axes):
    size = 1
    for axis in (axes,) if isinstance(axes, str) else axes:
        size *= lax.axis_size(axis)
    return swap_all(jnp.broadcast_to(values[None], (size,) + values.shape), axes)


def gather_parts(values):
    parts = lax.axis_size("dp")
    here = lax.axis_index("dp")
    every = jnp.arange(parts, dtype=jnp.int32)
    if parts != 8:
        return share_all(values, "dp"), every
    stack = [values]
    for shift in range(2, parts, 2):
        stack.append(lax.ppermute(values, "dp", [(i, (i + shift) % parts) for i in range(parts)]))
    stack = jnp.stack(stack)
    other = lax.ppermute(stack, "dp", [(i, i ^ 1) for i in range(parts)])
    order = (every % 2 ^ here % 2) * (parts // 2) + (here // 2 - every // 2) % (parts // 2)
    return jnp.concatenate([stack, other]), order.astype(jnp.int32)


def full_lanes(whole):
    parts, blocks, count, own = whole.shape
    if own == LANES:
        return whole
    tiles = parts * own // LANES
    whole = whole.transpose(1, 2, 0, 3).reshape(blocks, count, tiles, LANES)
    return whole.transpose(2, 0, 1, 3)


def local(
    hidden,
    cotangent,
    adapter_ids,
    attn_gain,
    mlp_gain,
    joined_weight,
    merge_weight_matrix,
    expand_weight,
    shrink_weight_matrix,
    joined_lower,
    joined_up_matrices,
    merge_lower,
    merge_up_matrices,
    expand_lower,
    expand_up_matrices,
    shrink_lower,
    shrink_up_matrices,
):
    parts, blocks = lax.axis_size("dp"), lax.axis_size("mp")
    place = lax.axis_index("mp")
    pair, core = place // 2, place % 2
    spot = place[None].astype(jnp.int32)
    seqs, own, model = hidden.shape
    length = own * blocks
    row_in = joined_weight.shape[0]
    wide = joined_weight.shape[2]
    width = expand_weight.shape[2]
    rank = joined_lower.shape[2]
    count = seqs * own

    rest = jnp.concatenate(
        [expand_weight.reshape(row_in, 2 * width).T, shrink_weight_matrix.T], axis=0
    )
    rest_whole = full_lanes(
        lax.all_gather(rest, ("dp", "mp"), axis=0, tiled=True).reshape(parts, blocks, 3 * width, row_in)
    )

    note = jnp.zeros((8, row_in), BF).at[0, :seqs].set(adapter_ids.astype(BF))
    joined_mine = jnp.concatenate(
        [joined_weight.reshape(row_in, 3 * wide).T, merge_weight_matrix.T, note], axis=0
    )
    joined_got, order = gather_parts(joined_mine)
    every_id = joined_got[:, 4 * wide, :seqs][order].astype(jnp.int32)
    if row_in != LANES:
        order = jnp.arange(model // LANES, dtype=jnp.int32)
    spot = jnp.concatenate([spot, order])
    joined_whole = full_lanes(joined_got[:, None])

    attn_scale = attn_gain.astype(F32)[None, :]
    mlp_scale = mlp_gain.astype(F32)[None, :]
    first_normed, first_scale = norm_parts(hidden.astype(F32))
    normed = (first_normed * attn_scale).astype(BF)
    def pick(table):
        return table.at[adapter_ids].get(mode="promise_in_bounds")

    def pick_low(table):
        return pick(table).transpose(0, 2, 1)

    def pick_up(table):
        return pick(table).reshape(seqs, rank, -1)

    joined_low, joined_up = pick_low(joined_lower), pick_up(joined_up_matrices)
    expand_low = pick_low(expand_lower).reshape(seqs * rank, model)
    merge_up = pick_up(merge_up_matrices)
    shrink_up = pick_up(shrink_up_matrices).reshape(seqs * rank, model)
    pad = -(-width // LANES) * LANES
    side = [(0, 0), (0, 0), (0, pad - width)]
    expand_mine = pick(expand_up_matrices)
    mine = jnp.concatenate(
        [
            pick_low(merge_lower),
            jnp.pad(expand_mine[:, :, 0], side),
            jnp.pad(expand_mine[:, :, 1], side),
            jnp.pad(pick_low(shrink_lower), side),
        ],
        axis=2,
    )
    far_sets = pair_swap(mine, 2)
    split_sets = jnp.stack([mine, pair_swap(mine, 1), far_sets, pair_swap(far_sets, 1)])
    merge_low = split_sets[:, :, :, :wide]
    expand_up = split_sets[:, :, :, wide : wide + 2 * pad].reshape(blocks, seqs * rank, 2 * pad)
    shrink_low = split_sets[:, :, :, wide + 2 * pad :].reshape(blocks, seqs * rank, pad)
    mask = (
        (jnp.arange(count) // own)[:, None] == (jnp.arange(seqs * rank) // rank)[None, :]
    ).astype(F32)

    half = HEAD_DIM // 2
    inverse = ROPE_BASE ** (-((jnp.arange(LANES) % half).astype(F32) * 2.0 / HEAD_DIM))
    angles = jnp.arange(length, dtype=F32)[:, None] * inverse[None, :]
    tables = [table.reshape(blocks, own, LANES) for table in (jnp.cos(angles), jnp.sin(angles))]

    across = pair_swap(normed, 2)
    beside = pair_swap(normed, 1)
    (
        across, joined_low, joined_up, tables, merge_low, merge_up,
        expand_low, expand_up, shrink_low, shrink_up, mask,
    ) = lax.optimization_barrier(
        (
            across, joined_low, joined_up, tables, merge_low, merge_up,
            expand_low, expand_up, shrink_low, shrink_up, mask,
        )
    )
    corner = pair_swap(across, 1)
    pieces = (normed, beside, across, corner)
    query, key, value, joined_down = project(
        spot, pieces, joined_whole, joined_low, joined_up,
        tables,
    )
    merge_own = joined_whole[:, :, 3 * wide : 4 * wide]
    merge_near = jnp.concatenate([merge_own, pair_swap(merge_own, 1)], axis=1)
    contexts, logs = [], []
    for seq in range(seqs):
        if seq:
            query = tie(query, context[0])
        context, probs = attend(spot, query, key, value, seq)
        context = [context[0]] + [pair_swap(context[bit], bit) for bit in range(1, blocks)]
        contexts.append(context)
        logs.append(probs)
    merge_far = pair_swap(merge_near, 2)
    middle, normed_mlp, merge_down = merge(
        spot, contexts, hidden, merge_near, merge_far, merge_low, merge_up, mlp_scale
    )
    (
        result, expand_up_grad, shrink_low_grad, expand_low_grad, shrink_up_grad,
        grad_middle, merge_low_grads, merge_up_grads, *grad_contexts,
    ) = gated(
        spot, normed_mlp.reshape(count, model), cotangent.reshape(count, model),
        middle.reshape(count, model), rest_whole, width,
        expand_up, shrink_low, expand_low, shrink_up, mask,
        merge_near, merge_far, merge_low, merge_up, mlp_scale, merge_down, contexts,
    )
    result = result.reshape(middle.shape)
    halfway = []
    for some in (grad_contexts[:blocks], grad_contexts[blocks:]):
        halfway.append([some[0]] + [pair_swap(some[bit], bit) for bit in range(1, blocks)])

    paired = rank == 2 * parts
    everyone = ("dp", "mp")
    owners = parts * blocks
    ids = jnp.broadcast_to(every_id[:, None], (parts, blocks, seqs))
    choose = (jnp.arange(ADAPTERS)[:, None] == ids.reshape(1, -1)).astype(BF)
    choose_own = (jnp.arange(ADAPTERS)[:, None] == every_id.reshape(1, -1)).astype(BF)
    part_width = model // blocks

    def by_block(grad):
        return grad.reshape(seqs * rank, blocks, -1).transpose(1, 0, 2)

    def ranks_out(grad):
        if paired:
            split = grad.reshape(grad.shape[0], seqs, 2, parts, -1).transpose(3, 0, 1, 2, 4)
            return split.reshape(split.shape[:3] + (-1,))
        return grad.reshape(grad.shape[0], seqs, parts, -1).transpose(2, 0, 1, 3)

    def ranks_in(whole, features):
        whole = whole.transpose(2, 1, 0, 3).reshape(ADAPTERS, whole.shape[1], rank, features)
        return whole.transpose(0, 2, 1, 3)

    def tall(values):
        return values.transpose(0, 2, 1).astype(F32)

    joined_low_grads, joined_up_grads = [], []
    grad_normeds = []
    early = jnp.concatenate(
        [
            piece.astype(BF)
            for piece in (
                by_block(expand_low_grad),
                by_block(shrink_up_grad),
                by_block(merge_up_grads.reshape(seqs * rank, model)),
                jnp.take(
                    merge_low_grads.transpose(1, 0, 2, 3).reshape(blocks, seqs * rank, wide),
                    place ^ jnp.arange(blocks), axis=0,
                ),
                jnp.pad(expand_up_grad[:, 0], side),
                jnp.pad(expand_up_grad[:, 1], side),
                jnp.pad(shrink_low_grad, side),
            )
        ],
        axis=2,
    )
    early_width = early.shape[2]

    early, halfway[0] = lax.optimization_barrier((early, halfway[0]))
    early = swap_all(ranks_out(early).reshape(owners, seqs, -1), everyone)
    chip, far = None, None
    for seq in range(seqs):
        pieces_back = list(halfway[min(seq, 1)])
        if seq:
            pieces_back[0] = tie(pieces_back[0], here)
        here, there, up_grad, low_grad = attend_back(
            spot, seq, query, key, value, logs[seq], pieces_back, pieces, tables,
            joined_whole, joined_low, joined_up, joined_down,
        )
        if seq == 0:
            there, halfway[1] = lax.optimization_barrier((there, halfway[1]))
        if seq == 1:
            there, far, early = lax.optimization_barrier((there, far, early))
            early = jnp.dot(choose, early.reshape(owners * seqs, -1), preferred_element_type=F32)
            if paired:
                early = jnp.concatenate([early[:, :early_width], early[:, early_width:]], axis=0)
            shared = lax.all_gather(early.astype(BF), everyone, axis=0)
        if seq == 2:
            there, far = lax.optimization_barrier((there, far))
        if seq:
            grad_normeds.append(chip + far.astype(F32))
        joined_up_grads.append(up_grad.transpose(1, 0, 2).reshape(rank, 3 * wide))
        joined_low_grads.append(low_grad)
        there = pair_swap(there, 1).astype(F32)
        chip, give = here[0] + there[0], (here[1] + there[1]).astype(BF)
        far = pair_swap(give, 2)

    piece = 3 * wide // blocks
    late_low = ranks_out(by_block(jnp.concatenate(joined_low_grads)).astype(BF))
    late_up = jnp.stack(joined_up_grads).astype(BF).reshape(seqs * rank, blocks, piece)
    late_up = ranks_out(late_up.transpose(1, 0, 2))
    some = 2 if paired else 1
    late_low, late_up = (each.reshape(owners, seqs * some, -1) for each in (late_low, late_up))
    low_size = late_low.shape[2]
    late = jnp.concatenate([late_low, late_up], axis=2)
    late = tie(late, give)
    late, far = lax.optimization_barrier((swap_all(late, everyone), far))
    late = late.reshape(parts, blocks, seqs, some, -1)
    grad_normeds.append(chip + far.astype(F32))
    grad_hidden = grad_middle + norm_back(jnp.stack(grad_normeds), first_normed, first_scale, attn_scale)
    late_low = late[..., :low_size].reshape(owners * seqs, -1)
    late_up = late[..., low_size:].transpose(1, 0, 2, 3, 4).reshape(blocks, parts * seqs, -1)
    late_low = jnp.dot(choose, late_low, preferred_element_type=F32).astype(BF)
    late_up = jnp.einsum("as,bsf->baf", choose_own, late_up, preferred_element_type=F32).astype(BF)
    if paired:
        half_low, half_up = late_low.shape[1] // 2, late_up.shape[2] // 2
        late_low = jnp.concatenate([late_low[:, :half_low], late_low[:, half_low:]], axis=0)
        late_up = jnp.concatenate([late_up[:, :, :half_up], late_up[:, :, half_up:]], axis=1)
    late = jnp.concatenate(
        [jnp.broadcast_to(late_low[None], (blocks,) + late_low.shape), late_up], axis=2
    )
    late = jnp.broadcast_to(late[None], (parts,) + late.shape).reshape((owners,) + late.shape[1:])
    late = swap_all(late, everyone)
    if paired:
        (
            expand_low_out, shrink_up_out, merge_up_out, merge_low_out, expand_up_out, shrink_low_out,
        ) = settle_early(spot, shared, parts, ADAPTERS, wide, width, pad)
        late, shrink_up_out = lax.optimization_barrier((late, shrink_up_out))
        joined_low_out, joined_up_out = settle_late(late, parts, ADAPTERS, part_width, wide)
        joined_up_out = joined_up_out.transpose(0, 2, 1, 3)
        joined_low_out, expand_low_out, merge_low_out, shrink_low_out = (
            tall(each) for each in (joined_low_out, expand_low_out, merge_low_out, shrink_low_out)
        )
    else:
        late = late.reshape(parts, blocks, ADAPTERS, -1)
        joined_low_out = tall(ranks_in(late[..., :low_size], part_width).reshape(ADAPTERS, rank, model))
        joined_up_out = ranks_in(late[..., low_size:], piece).reshape(ADAPTERS, rank, 3, wide).astype(F32)
        shared = ranks_in(shared.reshape(parts, blocks, ADAPTERS, -1), early_width).astype(F32)
        expand_low_out, shrink_up_out, merge_up_out = (
            shared[..., i * part_width : (i + 1) * part_width].reshape(ADAPTERS, rank, model)
            for i in range(3)
        )
        expand_low_out = tall(expand_low_out)
        divided = lax.dynamic_index_in_dim(shared[..., 3 * part_width :], place, 2, keepdims=False)
        merge_low_out = tall(divided[:, :, :wide])
        expand_up_out = jnp.stack(
            [divided[:, :, wide + i * pad : wide + i * pad + width] for i in range(2)], axis=2
        )
        shrink_low_out = tall(divided[:, :, wide + 2 * pad : wide + 2 * pad + width])
    return (
        result,
        grad_hidden.astype(BF),
        joined_low_out,
        joined_up_out,
        merge_low_out,
        merge_up_out,
        expand_low_out,
        expand_up_out,
        shrink_low_out,
        shrink_up_out,
    )


def solution(mesh):
    in_specs = (
        P("dp", "mp", None),
        P("dp", "mp", None),
        P("dp"),
        P(),
        P(),
        P("dp", None, "mp"),
        P("dp", "mp"),
        P("dp", None, "mp"),
        P("dp", "mp"),
        P(),
        P(None, None, None, "mp"),
        P(None, "mp", None),
        P(),
        P(),
        P(None, None, None, "mp"),
        P(None, "mp", None),
        P(),
    )
    out_specs = (
        P("dp", "mp", None),
        P("dp", "mp", None),
        P(),
        P(None, None, None, "mp"),
        P(None, "mp", None),
        P(),
        P(),
        P(None, None, None, "mp"),
        P(None, "mp", None),
        P(),
    )
    return jax.shard_map(local, mesh=mesh, in_specs=in_specs, out_specs=out_specs, check_vma=False)
```

```python
import jax
import jax.numpy as jnp
from jax import lax
from jax.experimental import pallas as pl
from jax.experimental.pallas import tpu as pltpu
from jax.sharding import PartitionSpec as P

HEAD_DIM = 64
ADAPTERS = 8
ADAPTER_SCALE = 2.0
NORM_EPS = 1e-05
ROPE_BASE = 160000.0
LANES = 128
CH = 256
BF = jnp.bfloat16
F32 = jnp.float32


def nt(a, b):
    return lax.dot_general(a, b, (((1,), (1,)), ((), ())), preferred_element_type=F32)


def nn(a, b):
    return lax.dot_general(a, b, (((1,), (0,)), ((), ())), preferred_element_type=F32)


def tn(a, b):
    return lax.dot_general(a, b, (((0,), (0,)), ((), ())), preferred_element_type=F32)


def lanes_of(ref, first=0, count=None, spot=None):
    count = ref.shape[2] if count is None else count
    places = [part if spot is None else spot[1 + part] for part in range(ref.shape[0])]
    return jnp.concatenate([ref[place, 0, pl.ds(first, count), :] for place in places], axis=1)


def full(shape):
    return pl.BlockSpec(shape, lambda *_: (0,) * len(shape))


def full_once(shape):
    return pl.BlockSpec(shape, lambda *_: (0,) * len(shape), pipeline_mode=pl.Buffered(1))


def norm_parts(values):
    centred = values - jnp.mean(values, axis=-1, keepdims=True)
    spread = jnp.mean(centred * centred, axis=-1, keepdims=True)
    scale = lax.rsqrt(spread + NORM_EPS)
    return centred * scale, scale


def norm_back(grads, normed, scale, gain):
    weighted = grads * gain
    return scale * (
        weighted
        - jnp.mean(weighted, axis=-1, keepdims=True)
        - normed * jnp.mean(weighted * normed, axis=-1, keepdims=True)
    )


def turn(values, cosine, sine):
    width = values.shape[1]
    half = HEAD_DIM // 2
    many = width // LANES
    if many > 1:
        cosine = jnp.concatenate([cosine] * many, axis=1)
        sine = jnp.concatenate([sine] * many, axis=1)
    lane = lax.broadcasted_iota(jnp.int32, values.shape, 1)
    turned = jnp.where(
        lane % HEAD_DIM < half,
        -pltpu.roll(values, width - half, 1),
        pltpu.roll(values, half, 1),
    )
    return values * cosine + turned * sine


def project_kernel(
    place, own, beside, across, corner, weight, low, up, cosine, sine,
    query, key, value, down, *, wide
):
    table = lanes_of(weight, 0, 3 * wide, place)
    for step, piece in enumerate((own, beside, across, corner)):
        spot = place[0] ^ step
        rows = piece[0]
        small = (nt(rows, low[0]) * ADAPTER_SCALE).astype(BF)
        down[0, step] = small
        out = nt(rows, table) + nn(small, up[0])
        cos, sin = cosine[spot], sine[spot]
        turned = turn(out[:, :wide], cos, sin)
        query[0, spot] = (turned * HEAD_DIM**-0.5).astype(BF)
        key[0, spot] = turn(out[:, wide : 2 * wide], cos, sin).astype(BF)
        value[0, spot] = out[:, 2 * wide :].astype(BF)


def project(place, pieces, weight, low, up, tables):
    seqs, own, model = pieces[0].shape
    tall = up.shape[2]
    wide = tall // 3
    rank = low.shape[1]
    blocks = len(pieces)
    piece = pl.BlockSpec((1, own, model), lambda s, p: (s, 0, 0))
    result = pl.BlockSpec((1, blocks, own, wide), lambda s, p: (s, 0, 0, 0))
    table = pl.BlockSpec((blocks, own, LANES), lambda s, p: (0, 0, 0))
    return pl.pallas_call(
        lambda *refs: project_kernel(*refs, wide=wide),
        grid_spec=pltpu.PrefetchScalarGridSpec(
            num_scalar_prefetch=1,
            grid=(seqs,),
            in_specs=[piece] * blocks
            + [
                pl.BlockSpec(weight.shape, lambda s, p: (0, 0, 0, 0)),
                pl.BlockSpec((1, rank, model), lambda s, p: (s, 0, 0)),
                pl.BlockSpec((1, rank, tall), lambda s, p: (s, 0, 0)),
                table,
                table,
            ],
            out_specs=[result] * 3
            + [pl.BlockSpec((1, blocks, own, rank), lambda s, p: (s, 0, 0, 0))],
        ),
        out_shape=[jax.ShapeDtypeStruct((seqs, blocks, own, wide), BF)] * 3
        + [jax.ShapeDtypeStruct((seqs, blocks, own, rank), BF)],
        name="project",
    )(place, *pieces, weight, low, up, *tables)


def one_head(values, head):
    lane = lax.broadcasted_iota(jnp.int32, values.shape, 1)
    return jnp.where((lane // HEAD_DIM) == head, values, jnp.zeros_like(values))


def attend_kernel(place, query, key, value, *outs):
    *contexts, probs, shrinks, held = outs
    blocks, own = query.shape[1:3]
    tile = pl.program_id(1)
    keys = key[0].reshape(blocks * own, LANES)
    turned = value[0].reshape(blocks * own, LANES).T
    rows = jnp.concatenate([query[0, place[0] ^ (2 * tile + i)] for i in range(2)], axis=0)
    parts = []
    for head in range(2):
        mine = one_head(rows, head)
        held[...] = nt(keys, mine)
        top = jnp.max(held[...], axis=0, keepdims=True)

        def some(i, sums):
            at = pl.ds(pl.multiple_of(i * CH, CH), CH)
            raised = jnp.exp(held[at, :] - top)
            probs[0, 0, head, at, :] = raised.astype(BF)
            return sums + jnp.sum(raised.reshape(CH // 8, 8, raised.shape[1]), axis=0)

        sums = lax.fori_loop(0, blocks * own // CH, some, jnp.zeros((8, 2 * own), F32))
        shrink = 1.0 / jnp.sum(sums, axis=0, keepdims=True)
        shrinks[0, 0, head : head + 1] = shrink
        parts.append(nn(turned[head * HEAD_DIM : (head + 1) * HEAD_DIM], probs[0, 0, head]) * shrink)
    merged = jnp.concatenate(parts, axis=0).T.astype(BF)
    for half in range(blocks // 2):
        @pl.when(tile == half)
        def _():
            for i in range(2):
                contexts[2 * half + i][...] = merged[i * own : (i + 1) * own]


def attend(place, query, key, value, seq):
    _, blocks, own, wide = query.shape
    pairs = wide // LANES
    whole = pl.BlockSpec((1, blocks, own, LANES), lambda h, t, p: (seq, 0, 0, h))
    *contexts, probs, shrinks = pl.pallas_call(
        attend_kernel,
        grid_spec=pltpu.PrefetchScalarGridSpec(
            num_scalar_prefetch=1,
            grid=(pairs, blocks // 2),
            in_specs=[whole] * 3,
            out_specs=[pl.BlockSpec((own, LANES), lambda h, t, p: (0, h))] * blocks
            + [
                pl.BlockSpec((1, 1, 2, blocks * own, 2 * own), lambda h, t, p: (h, t, 0, 0, 0)),
                pl.BlockSpec((1, 1, 2, 2 * own), lambda h, t, p: (h, t, 0, 0)),
            ],
            scratch_shapes=[pltpu.VMEM((blocks * own, 2 * own), F32)],
        ),
        out_shape=[jax.ShapeDtypeStruct((own, wide), BF)] * blocks
        + [
            jax.ShapeDtypeStruct((pairs, blocks // 2, 2, blocks * own, 2 * own), BF),
            jax.ShapeDtypeStruct((pairs, blocks // 2, 2, 2 * own), F32),
        ],
        name="attend",
    )(place, query, key, value)
    return contexts, (probs, shrinks, list(contexts))


def attend_back_kernel(place, query, key, value, probs, shrinks, *refs):
    blocks, own = query.shape[1:3]
    contexts = refs[:blocks]
    pieces = refs[blocks : 2 * blocks]
    rows_in = refs[2 * blocks : 3 * blocks]
    cosine, sine, weight, low, up, down, here, there, up_grad, low_grad, total, small, turn_keys = refs[3 * blocks :]
    pair = pl.program_id(0)
    last = pl.num_programs(0) - 1
    wide = LANES * pl.num_programs(0)
    keys = key[0].reshape(blocks * own, LANES)
    values = value[0].reshape(blocks * own, LANES)
    turned = keys.T
    backs, mines, mine_grads = [], [], []
    grad_queries = []
    for step in range(0, blocks, 2):
        spots = [place[0] ^ (step + i) for i in range(2)]
        rows = jnp.concatenate([query[0, spot] for spot in spots], axis=0)
        outer = jnp.concatenate([pieces[step + i][0] for i in range(2)], axis=0).astype(F32)
        inner = jnp.concatenate([contexts[step + i][...] for i in range(2)], axis=0).astype(F32)
        product = (outer * inner).T
        factors = [shrinks[0, step // 2, head : head + 1] for head in range(2)]
        spread = jnp.concatenate([jnp.broadcast_to(f, (HEAD_DIM, 2 * own)) for f in factors], axis=0).T
        outer = (outer * spread).astype(BF)
        parts = []
        for head in range(2):
            mine_grad = one_head(outer, head)
            chances = probs[0, step // 2, head]
            half = product[head * HEAD_DIM : (head + 1) * HEAD_DIM]
            mean = jnp.sum(half, axis=0, keepdims=True) * factors[head]
            back = (chances.astype(F32) * (nt(values, mine_grad) - mean)).astype(BF)
            parts.append(nn(turned[head * HEAD_DIM : (head + 1) * HEAD_DIM], back))
            backs.append(back)
            mines.append(one_head(rows, head))
            mine_grads.append(mine_grad)
        queries = jnp.concatenate(parts, axis=0).T * HEAD_DIM**-0.5
        for i, spot in enumerate(spots):
            part = queries[i * own : (i + 1) * own]
            grad_queries.append(turn(part, cosine[spot], -sine[spot]).astype(BF))
    grad_keys = nn(jnp.concatenate(backs, axis=1), jnp.concatenate(mines, axis=0))
    chances = [probs[0, i // 2, i % 2] for i in range(blocks)]
    grad_values = nn(jnp.concatenate(chances, axis=1), jnp.concatenate(mine_grads, axis=0))
    for step in range(blocks):
        part = slice(step * own, (step + 1) * own)
        turn_keys[0, step] = turn(grad_keys[part], cosine[step], -sine[step]).astype(BF)
        turn_keys[1, step] = grad_values[part].astype(BF)
    grads = [
        jnp.concatenate(grad_queries, axis=0),
        jnp.concatenate([turn_keys[0, place[0] ^ step] for step in range(blocks)], axis=0),
        jnp.concatenate([turn_keys[1, place[0] ^ step] for step in range(blocks)], axis=0),
    ]
    grads = jnp.concatenate(grads, axis=1)
    firsts = [pl.multiple_of(kind * wide + pair * LANES, LANES) for kind in range(3)]
    table = jnp.concatenate([lanes_of(weight, first, LANES, place) for first in firsts], axis=0)
    ups = jnp.concatenate([up[0, :, pl.ds(first, LANES)] for first in firsts], axis=1)
    downs = jnp.concatenate([down[0, step] for step in range(blocks)], axis=0)
    more = nn(grads, table)
    more_small = nt(grads, ups)
    up_part = tn(downs, grads)
    for kind in range(3):
        up_grad[kind] = up_part[:, kind * LANES : (kind + 1) * LANES].astype(BF)

    @pl.when(pair == 0)
    def _():
        total[...] = more
        small[...] = more_small

    @pl.when(pair > 0)
    def _():
        total[...] += more
        small[...] += more_small

    @pl.when(pair == last)
    def _():
        narrow = (small[...] * ADAPTER_SCALE).astype(BF)
        low_grad[...] = tn(narrow, jnp.concatenate([piece[0] for piece in rows_in], axis=0)).astype(BF)
        done = total[...] + nn(narrow, low[0])
        for step in range(blocks):
            part = done[step * own : (step + 1) * own].astype(BF)
            (there if step % 2 else here)[step // 2] = part


def attend_back(place, seq, query, key, value, kept, grads, pieces, tables, weight, low, up, down):
    _, blocks, own, wide = query.shape
    _, rank, model = low.shape
    tall = up.shape[2]
    pairs = wide // LANES
    whole = lambda shape: pl.BlockSpec(shape, lambda h, p: (0,) * len(shape))
    of_seq = lambda shape: pl.BlockSpec((1,) + shape, lambda h, p: (seq,) + (0,) * len(shape))
    heads = pl.BlockSpec((1, blocks, own, LANES), lambda h, p: (seq, 0, 0, h))
    probs, shrinks, contexts = kept
    return pl.pallas_call(
        attend_back_kernel,
        grid_spec=pltpu.PrefetchScalarGridSpec(
            num_scalar_prefetch=1,
            grid=(pairs,),
            in_specs=[heads] * 3
            + [pl.BlockSpec((1,) + probs.shape[1:], lambda h, p: (h, 0, 0, 0, 0))]
            + [pl.BlockSpec((1,) + shrinks.shape[1:], lambda h, p: (h, 0, 0, 0))]
            + [pl.BlockSpec((own, LANES), lambda h, p: (0, h))] * blocks
            + [pl.BlockSpec((1, own, LANES), lambda h, p: (max(seq - 1, 0), 0, h))] * blocks
            + [of_seq((own, model))] * blocks
            + [whole((blocks, own, LANES))] * 2
            + [
                whole(weight.shape),
                of_seq((rank, model)),
                of_seq((rank, tall)),
                of_seq((blocks, own, rank)),
            ],
            out_specs=[
                whole((blocks // 2, own, model)),
                whole((blocks // 2, own, model)),
                pl.BlockSpec((3, rank, LANES), lambda h, p: (0, 0, h)),
                whole((rank, model)),
            ],
            scratch_shapes=[
                pltpu.VMEM((blocks * own, model), F32),
                pltpu.VMEM((blocks * own, rank), F32),
                pltpu.VMEM((2, blocks, own, LANES), BF),
            ],
        ),
        out_shape=[
            jax.ShapeDtypeStruct((blocks // 2, own, model), BF),
            jax.ShapeDtypeStruct((blocks // 2, own, model), BF),
            jax.ShapeDtypeStruct((3, rank, wide), BF),
            jax.ShapeDtypeStruct((rank, model), BF),
        ],
        name="attend_back",
    )(place, query, key, value, probs, shrinks, *contexts, *grads, *pieces, *tables, weight, low, up, down)


def merge_kernel(spot, *refs, blocks, seqs):
    contexts = refs[: blocks * seqs]
    start, near, far, low, up, gain, middle, normed, down = refs[blocks * seqs :]
    tables = [lanes_of((far if i // 2 else near).at[:, pl.ds(i % 2, 1)], spot=spot) for i in range(blocks)]
    for seq in range(seqs):
        total = start[seq].astype(F32)
        small = jnp.zeros(down.shape[1:], F32)
        for step in range(blocks):
            rows = contexts[seq * blocks + step][...]
            small += nt(rows, low[step, seq])
            total += nn(rows, tables[step])
        small = (small * ADAPTER_SCALE).astype(BF)
        down[seq] = small
        total += nn(small, up[seq])
        middle[seq] = total
        normed[seq] = (norm_parts(total)[0] * gain[...]).astype(BF)


def merge(spot, contexts, start, near, far, low, up, gain):
    seqs, own, model = start.shape
    blocks, _, rank, wide = low.shape
    inputs = [piece for context in contexts for piece in context]
    inputs += [start, near, far, low, up, gain]
    results = [
        jax.ShapeDtypeStruct((seqs, own, model), F32),
        jax.ShapeDtypeStruct((seqs, own, model), BF),
        jax.ShapeDtypeStruct((seqs, own, rank), BF),
    ]
    return pl.pallas_call(
        lambda *refs: merge_kernel(*refs, blocks=blocks, seqs=seqs),
        grid_spec=pltpu.PrefetchScalarGridSpec(
            num_scalar_prefetch=1,
            grid=(1,),
            in_specs=[full(each.shape) for each in inputs],
            out_specs=[full(each.shape) for each in results],
        ),
        out_shape=results,
        name="merge",
    )(spot, *inputs)


def gated_kernel(
    place, rows, out_grad, middle, expand, shrink, expand_up, shrink_low, expand_low, shrink_up, mask,
    near, far, merge_low, merge_up, gain, merge_down, *refs, width, blocks, seqs
):
    contexts = refs[: seqs * blocks]
    (
        result, expand_up_grad, shrink_low_grad, expand_low_grad, shrink_up_grad,
        grad_middle, merge_low_grad, merge_up_grad,
    ) = refs[seqs * blocks : seqs * blocks + 8]
    firsts = refs[seqs * blocks + 8 : seqs * blocks + 8 + blocks]
    others = refs[seqs * blocks + 8 + blocks : seqs * blocks + 8 + 2 * blocks]
    total, grad_rows, down, down_grad, late, late_grad = refs[seqs * blocks + 8 + 2 * blocks :]
    step = pl.program_id(0)
    scaled = ADAPTER_SCALE * mask[...]

    @pl.when(step == 0)
    def _():
        total[...] = middle[...]
        grad_rows[...] = jnp.zeros(grad_rows.shape, F32)
        down[...] = (nt(rows[...], expand_low[...]) * scaled).astype(BF)
        down_grad[...] = (nt(out_grad[...], shrink_up[...]) * scaled).astype(BF)
        late[...] = jnp.zeros(late.shape, F32)
        late_grad[...] = jnp.zeros(late_grad.shape, F32)

    values = lanes_of(expand, 0, width)
    gates = lanes_of(expand, width, width)
    outs = lanes_of(shrink)
    up_values = expand_up[0, :, :width]
    up_gates = expand_up[0, :, expand_up.shape[2] // 2 : expand_up.shape[2] // 2 + width]
    low_outs = shrink_low[0, :, :width]
    first = nt(rows[...], values) + nn(down[...], up_values)
    second = nt(rows[...], gates) + nn(down[...], up_gates)
    chance = 0.5 + 0.5 * lax.erf(first * (0.5**0.5))
    curve = first * chance
    slope = chance + first * (jnp.exp(-0.5 * first * first) * 0.3989422804014327)
    active = (curve * second).astype(BF)
    grads = nt(out_grad[...], outs) + nn(down_grad[...], low_outs)
    first_grad = (grads * second * slope).astype(BF)
    second_grad = (grads * curve).astype(BF)
    total[...] += nn(active, outs)
    late[...] += nt(active, low_outs)
    grad_rows[...] += nn(first_grad, values) + nn(second_grad, gates)
    late_grad[...] += nt(first_grad, up_values) + nt(second_grad, up_gates)
    expand_up_grad[0, 0] = tn(down[...], first_grad).astype(BF)
    expand_up_grad[0, 1] = tn(down[...], second_grad).astype(BF)
    shrink_low_grad[0] = tn(down_grad[...], active).astype(BF)

    @pl.when(step == blocks - 1)
    def _():
        small = (late[...] * scaled).astype(BF)
        result[...] = (total[...] + nn(small, shrink_up[...])).astype(BF)
        shrink_up_grad[...] = tn(small, out_grad[...]).astype(BF)
        small_grad = (late_grad[...] * scaled).astype(BF)
        expand_low_grad[...] = tn(small_grad, rows[...]).astype(BF)
        own = rows.shape[0] // seqs
        for seq in range(seqs):
            part = slice(seq * own, (seq + 1) * own)
            normed, scale = norm_parts(middle[part])
            grad_normed = grad_rows[part] + nn(small_grad[part], expand_low[...])
            whole = out_grad[part].astype(F32) + norm_back(grad_normed, normed, scale, gain[...])
            grad_middle[seq] = whole
            low_rows = whole.astype(BF)
            small = (nt(low_rows, merge_up[seq]) * ADAPTER_SCALE).astype(BF)
            for move in range(blocks):
                ref = far if move // 2 else near
                table = lanes_of(ref.at[:, pl.ds(move % 2, 1)], spot=place)
                out = (nt(low_rows, table) + nn(small, merge_low[move, seq])).astype(BF)
                if seq:
                    others[move][seq - 1] = out
                else:
                    firsts[move][0] = out
                merge_low_grad[seq, move] = tn(small, contexts[seq * blocks + move][...]).astype(BF)
            merge_up_grad[seq] = tn(merge_down[seq], low_rows).astype(BF)


def gated(
    place, rows, out_grad, middle, weights, width, expand_up, shrink_low, expand_low, shrink_up, mask,
    near, far, merge_low, merge_up, gain, merge_down, contexts
):
    count, model = rows.shape
    parts, blocks, _, lane = weights.shape
    seqs = len(contexts)
    own, wide = contexts[0][0].shape
    some = merge_up.shape[1]
    rank = expand_low.shape[0]
    pad = shrink_low.shape[2]
    pieces = [piece for context in contexts for piece in context]
    shapes = [
        ((count, model), BF),
        ((blocks, 2, rank, width), BF),
        ((blocks, rank, width), BF),
        ((rank, model), BF),
        ((rank, model), BF),
        ((seqs, own, model), F32),
        ((seqs, blocks, some, wide), BF),
        ((seqs, some, model), BF),
    ]
    shapes += [((1, own, wide), BF)] * blocks + [((seqs - 1, own, wide), BF)] * blocks
    out_specs = [full_once(shape) for shape, _ in shapes]
    out_specs[1] = pl.BlockSpec((1, 2, rank, width), lambda m, p: (m, 0, 0, 0))
    out_specs[2] = pl.BlockSpec((1, rank, width), lambda m, p: (m, 0, 0))
    return pl.pallas_call(
        lambda *refs: gated_kernel(*refs, width=width, blocks=blocks, seqs=seqs),
        grid_spec=pltpu.PrefetchScalarGridSpec(
            num_scalar_prefetch=1,
            grid=(blocks,),
            in_specs=[
                full_once((count, model)),
                full_once((count, model)),
                full_once((count, model)),
                pl.BlockSpec((parts, 1, 2 * width, lane), lambda m, p: (0, m, 0, 0)),
                pl.BlockSpec((parts, 1, width, lane), lambda m, p: (0, m, 2, 0)),
                pl.BlockSpec((1, rank, 2 * pad), lambda m, p: (p[0] ^ m, 0, 0)),
                pl.BlockSpec((1, rank, pad), lambda m, p: (p[0] ^ m, 0, 0)),
                full_once((rank, model)),
                full_once((rank, model)),
                full_once((count, rank)),
                full_once(near.shape),
                full_once(far.shape),
                full_once(merge_low.shape),
                full_once(merge_up.shape),
                full_once(gain.shape),
                full_once(merge_down.shape),
            ]
            + [full_once((own, wide))] * len(pieces),
            out_specs=out_specs,
            scratch_shapes=[
                pltpu.VMEM((count, model), F32),
                pltpu.VMEM((count, model), F32),
                pltpu.VMEM((count, rank), BF),
                pltpu.VMEM((count, rank), BF),
                pltpu.VMEM((count, rank), F32),
                pltpu.VMEM((count, rank), F32),
            ],
        ),
        out_shape=[jax.ShapeDtypeStruct(shape, kind) for shape, kind in shapes],
        name="gated",
    )(
        place, rows, out_grad, middle, weights, weights, expand_up, shrink_low, expand_low, shrink_up, mask,
        near, far, merge_low, merge_up, gain, merge_down, *pieces,
    )


def settle_early_kernel(place, got, low, shrink_up, merge_up, merge_low, expand_up, shrink_low, *, parts, blocks, sets, part, wide, width, pad):
    at = 3 * part
    for g in range(parts):
        for block in range(blocks):
            rows = got[g * blocks + block, :, :at].astype(F32)
            for i, out in enumerate((low, shrink_up, merge_up)):
                for two in range(2):
                    cut = rows[two * sets : (two + 1) * sets, i * part : (i + 1) * part]
                    out[:, two * parts + g, block * part : (block + 1) * part] = cut
        rows = got[g * blocks + place[0], :, at:].astype(F32)
        for two in range(2):
            cut = rows[two * sets : (two + 1) * sets]
            rank = two * parts + g
            merge_low[:, rank, :] = cut[:, :wide]
            for kind in range(2):
                first = wide + kind * pad
                expand_up[:, rank, kind, :] = cut[:, first : first + width]
            shrink_low[:, rank, :] = cut[:, wide + 2 * pad : wide + 2 * pad + width]


def settle_early(place, got, parts, sets, wide, width, pad):
    owners, rows, features = got.shape
    blocks = owners // parts
    rank = rows // sets * parts
    part = (features - wide - 3 * pad) // 3
    model = blocks * part
    shapes = [(rank, model)] * 3 + [(rank, wide), (rank, 2, width), (rank, width)]
    shapes = [(sets,) + shape for shape in shapes]
    whole = lambda shape: pl.BlockSpec(shape, lambda i, p: (0,) * len(shape))
    return pl.pallas_call(
        lambda *refs: settle_early_kernel(
            *refs, parts=parts, blocks=blocks, sets=sets, part=part, wide=wide, width=width, pad=pad
        ),
        grid_spec=pltpu.PrefetchScalarGridSpec(
            num_scalar_prefetch=1,
            grid=(1,),
            in_specs=[whole(got.shape)],
            out_specs=[whole(shape) for shape in shapes],
        ),
        out_shape=[jax.ShapeDtypeStruct(shape, F32) for shape in shapes],
        name="settle_early",
    )(place, got)


def settle_late_kernel(got, low, up, *, parts, blocks, sets, part, piece):
    wide = up.shape[3]
    for g in range(parts):
        rows = [got[g * blocks + block].astype(F32) for block in range(blocks)]
        tail = jnp.concatenate([row[:, part : part + piece] for row in rows], axis=1)
        for two in range(2):
            rank = two * parts + g
            for block, row in enumerate(rows):
                low[:, rank, block * part : (block + 1) * part] = row[two * sets : (two + 1) * sets, :part]
            for kind in range(up.shape[1]):
                up[:, kind, rank, :] = tail[two * sets : (two + 1) * sets, kind * wide : (kind + 1) * wide]


def settle_late(got, parts, sets, part, wide):
    owners, rows, features = got.shape
    blocks = owners // parts
    rank = rows // sets * parts
    piece = features - part
    shapes = [(sets, rank, blocks * part), (sets, blocks * piece // wide, rank, wide)]
    return pl.pallas_call(
        lambda *refs: settle_late_kernel(*refs, parts=parts, blocks=blocks, sets=sets, part=part, piece=piece),
        grid=(1,),
        in_specs=[full(got.shape)],
        out_specs=[full(shape) for shape in shapes],
        out_shape=[jax.ShapeDtypeStruct(shape, F32) for shape in shapes],
        name="settle_late",
    )(got)


def pair_swap(values, bit):
    size = lax.axis_size("mp")
    return lax.ppermute(values, "mp", [(i, i ^ bit) for i in range(size)])


def tie(values, after):
    return lax.optimization_barrier((values, after))[0]


def swap_all(values, axes):
    return lax.all_to_all(values, axes, 0, 0, tiled=True)


def share_all(values, axes):
    size = 1
    for axis in (axes,) if isinstance(axes, str) else axes:
        size *= lax.axis_size(axis)
    return swap_all(jnp.broadcast_to(values[None], (size,) + values.shape), axes)


def gather_parts(values):
    parts = lax.axis_size("dp")
    here = lax.axis_index("dp")
    every = jnp.arange(parts, dtype=jnp.int32)
    if parts != 8:
        return share_all(values, "dp"), every
    stack = [values]
    for shift in range(2, parts, 2):
        stack.append(lax.ppermute(values, "dp", [(i, (i + shift) % parts) for i in range(parts)]))
    stack = jnp.stack(stack)
    other = lax.ppermute(stack, "dp", [(i, i ^ 1) for i in range(parts)])
    order = (every % 2 ^ here % 2) * (parts // 2) + (here // 2 - every // 2) % (parts // 2)
    return jnp.concatenate([stack, other]), order.astype(jnp.int32)


def full_lanes(whole):
    parts, blocks, count, own = whole.shape
    if own == LANES:
        return whole
    tiles = parts * own // LANES
    whole = whole.transpose(1, 2, 0, 3).reshape(blocks, count, tiles, LANES)
    return whole.transpose(2, 0, 1, 3)


def local(
    hidden,
    cotangent,
    adapter_ids,
    attn_gain,
    mlp_gain,
    joined_weight,
    merge_weight_matrix,
    expand_weight,
    shrink_weight_matrix,
    joined_lower,
    joined_up_matrices,
    merge_lower,
    merge_up_matrices,
    expand_lower,
    expand_up_matrices,
    shrink_lower,
    shrink_up_matrices,
):
    parts, blocks = lax.axis_size("dp"), lax.axis_size("mp")
    place = lax.axis_index("mp")
    pair, core = place // 2, place % 2
    spot = place[None].astype(jnp.int32)
    seqs, own, model = hidden.shape
    length = own * blocks
    row_in = joined_weight.shape[0]
    wide = joined_weight.shape[2]
    width = expand_weight.shape[2]
    rank = joined_lower.shape[2]
    count = seqs * own

    rest = jnp.concatenate(
        [expand_weight.reshape(row_in, 2 * width).T, shrink_weight_matrix.T], axis=0
    )
    rest_whole = full_lanes(
        lax.all_gather(rest, ("dp", "mp"), axis=0, tiled=True).reshape(parts, blocks, 3 * width, row_in)
    )

    note = jnp.zeros((8, row_in), BF).at[0, :seqs].set(adapter_ids.astype(BF))
    joined_mine = jnp.concatenate(
        [joined_weight.reshape(row_in, 3 * wide).T, merge_weight_matrix.T, note], axis=0
    )
    joined_got, order = gather_parts(joined_mine)
    every_id = joined_got[:, 4 * wide, :seqs][order].astype(jnp.int32)
    if row_in != LANES:
        order = jnp.arange(model // LANES, dtype=jnp.int32)
    spot = jnp.concatenate([spot, order])
    joined_whole = full_lanes(joined_got[:, None])

    attn_scale = attn_gain.astype(F32)[None, :]
    mlp_scale = mlp_gain.astype(F32)[None, :]
    first_normed, first_scale = norm_parts(hidden.astype(F32))
    normed = (first_normed * attn_scale).astype(BF)
    def pick(table):
        return table.at[adapter_ids].get(mode="promise_in_bounds")

    def pick_low(table):
        return pick(table).transpose(0, 2, 1)

    def pick_up(table):
        return pick(table).reshape(seqs, rank, -1)

    joined_low, joined_up = pick_low(joined_lower), pick_up(joined_up_matrices)
    expand_low = pick_low(expand_lower).reshape(seqs * rank, model)
    merge_up = pick_up(merge_up_matrices)
    shrink_up = pick_up(shrink_up_matrices).reshape(seqs * rank, model)
    pad = -(-width // LANES) * LANES
    side = [(0, 0), (0, 0), (0, pad - width)]
    expand_mine = pick(expand_up_matrices)
    mine = jnp.concatenate(
        [
            pick_low(merge_lower),
            jnp.pad(expand_mine[:, :, 0], side),
            jnp.pad(expand_mine[:, :, 1], side),
            jnp.pad(pick_low(shrink_lower), side),
        ],
        axis=2,
    )
    far_sets = pair_swap(mine, 2)
    split_sets = jnp.stack([mine, pair_swap(mine, 1), far_sets, pair_swap(far_sets, 1)])
    merge_low = split_sets[:, :, :, :wide]
    expand_up = split_sets[:, :, :, wide : wide + 2 * pad].reshape(blocks, seqs * rank, 2 * pad)
    shrink_low = split_sets[:, :, :, wide + 2 * pad :].reshape(blocks, seqs * rank, pad)
    mask = (
        (jnp.arange(count) // own)[:, None] == (jnp.arange(seqs * rank) // rank)[None, :]
    ).astype(F32)

    half = HEAD_DIM // 2
    inverse = ROPE_BASE ** (-((jnp.arange(LANES) % half).astype(F32) * 2.0 / HEAD_DIM))
    angles = jnp.arange(length, dtype=F32)[:, None] * inverse[None, :]
    tables = [table.reshape(blocks, own, LANES) for table in (jnp.cos(angles), jnp.sin(angles))]

    across = pair_swap(normed, 2)
    beside = pair_swap(normed, 1)
    (
        across, joined_low, joined_up, tables, merge_low, merge_up,
        expand_low, expand_up, shrink_low, shrink_up, mask,
    ) = lax.optimization_barrier(
        (
            across, joined_low, joined_up, tables, merge_low, merge_up,
            expand_low, expand_up, shrink_low, shrink_up, mask,
        )
    )
    corner = pair_swap(across, 1)
    pieces = (normed, beside, across, corner)
    query, key, value, joined_down = project(
        spot, pieces, joined_whole, joined_low, joined_up,
        tables,
    )
    merge_own = joined_whole[:, :, 3 * wide : 4 * wide]
    merge_near = jnp.concatenate([merge_own, pair_swap(merge_own, 1)], axis=1)
    contexts, logs = [], []
    for seq in range(seqs):
        if seq:
            query = tie(query, context[0])
        context, probs = attend(spot, query, key, value, seq)
        context = [context[0]] + [pair_swap(context[bit], bit) for bit in range(1, blocks)]
        contexts.append(context)
        logs.append(probs)
    merge_far = pair_swap(merge_near, 2)
    middle, normed_mlp, merge_down = merge(
        spot, contexts, hidden, merge_near, merge_far, merge_low, merge_up, mlp_scale
    )
    (
        result, expand_up_grad, shrink_low_grad, expand_low_grad, shrink_up_grad,
        grad_middle, merge_low_grads, merge_up_grads, *grad_contexts,
    ) = gated(
        spot, normed_mlp.reshape(count, model), cotangent.reshape(count, model),
        middle.reshape(count, model), rest_whole, width,
        expand_up, shrink_low, expand_low, shrink_up, mask,
        merge_near, merge_far, merge_low, merge_up, mlp_scale, merge_down, contexts,
    )
    result = result.reshape(middle.shape)
    halfway = []
    for some in (grad_contexts[:blocks], grad_contexts[blocks:]):
        halfway.append([some[0]] + [pair_swap(some[bit], bit) for bit in range(1, blocks)])

    paired = rank == 2 * parts
    everyone = ("dp", "mp")
    owners = parts * blocks
    ids = jnp.broadcast_to(every_id[:, None], (parts, blocks, seqs))
    choose = (jnp.arange(ADAPTERS)[:, None] == ids.reshape(1, -1)).astype(BF)
    choose_own = (jnp.arange(ADAPTERS)[:, None] == every_id.reshape(1, -1)).astype(BF)
    part_width = model // blocks

    def by_block(grad):
        return grad.reshape(seqs * rank, blocks, -1).transpose(1, 0, 2)

    def ranks_out(grad):
        if paired:
            split = grad.reshape(grad.shape[0], seqs, 2, parts, -1).transpose(3, 0, 1, 2, 4)
            return split.reshape(split.shape[:3] + (-1,))
        return grad.reshape(grad.shape[0], seqs, parts, -1).transpose(2, 0, 1, 3)

    def ranks_in(whole, features):
        whole = whole.transpose(2, 1, 0, 3).reshape(ADAPTERS, whole.shape[1], rank, features)
        return whole.transpose(0, 2, 1, 3)

    def tall(values):
        return values.transpose(0, 2, 1).astype(F32)

    joined_low_grads, joined_up_grads = [], []
    grad_normeds = []
    early = jnp.concatenate(
        [
            piece.astype(BF)
            for piece in (
                by_block(expand_low_grad),
                by_block(shrink_up_grad),
                by_block(merge_up_grads.reshape(seqs * rank, model)),
                jnp.take(
                    merge_low_grads.transpose(1, 0, 2, 3).reshape(blocks, seqs * rank, wide),
                    place ^ jnp.arange(blocks), axis=0,
                ),
                jnp.pad(expand_up_grad[:, 0], side),
                jnp.pad(expand_up_grad[:, 1], side),
                jnp.pad(shrink_low_grad, side),
            )
        ],
        axis=2,
    )
    early_width = early.shape[2]

    early, halfway[0] = lax.optimization_barrier((early, halfway[0]))
    early = swap_all(ranks_out(early).reshape(owners, seqs, -1), everyone)
    chip, far = None, None
    for seq in range(seqs):
        pieces_back = list(halfway[min(seq, 1)])
        if seq:
            pieces_back[0] = tie(pieces_back[0], here)
        here, there, up_grad, low_grad = attend_back(
            spot, seq, query, key, value, logs[seq], pieces_back, pieces, tables,
            joined_whole, joined_low, joined_up, joined_down,
        )
        if seq == 0:
            there, halfway[1] = lax.optimization_barrier((there, halfway[1]))
        if seq == 1:
            there, far, early = lax.optimization_barrier((there, far, early))
            by_seq = choose.reshape(ADAPTERS, owners, seqs)
            early = sum(
                jnp.dot(by_seq[:, :, i], early[:, i], preferred_element_type=F32) for i in range(seqs)
            )
            if paired:
                early = jnp.concatenate([early[:, :early_width], early[:, early_width:]], axis=0)
            shared = lax.all_gather(early.astype(BF), everyone, axis=0)
        if seq == 2:
            there, far = lax.optimization_barrier((there, far))
        if seq:
            grad_normeds.append(chip + far.astype(F32))
        joined_up_grads.append(up_grad.transpose(1, 0, 2).reshape(rank, 3 * wide))
        joined_low_grads.append(low_grad)
        there = pair_swap(there, 1).astype(F32)
        chip, give = here[0].astype(F32) + there[0], (here[1].astype(F32) + there[1]).astype(BF)
        far = pair_swap(give, 2)

    piece = 3 * wide // blocks
    late_low = ranks_out(by_block(jnp.concatenate(joined_low_grads)).astype(BF))
    late_up = jnp.stack(joined_up_grads).astype(BF).reshape(seqs * rank, blocks, piece)
    late_up = ranks_out(late_up.transpose(1, 0, 2))
    some = 2 if paired else 1
    late_low, late_up = (each.reshape(owners, seqs * some, -1) for each in (late_low, late_up))
    low_size = late_low.shape[2]
    late = jnp.concatenate([late_low, late_up], axis=2)
    late = tie(late, there)
    late, far = lax.optimization_barrier((swap_all(late, everyone), far))
    late = late.reshape(parts, blocks, seqs, some, -1)
    grad_normeds.append(chip + far.astype(F32))
    grad_hidden = grad_middle + norm_back(jnp.stack(grad_normeds), first_normed, first_scale, attn_scale)
    late_low = late[..., :low_size].reshape(owners * seqs, -1)
    late_up = late[..., low_size:].transpose(1, 0, 2, 3, 4).reshape(blocks, parts * seqs, -1)
    late_low = jnp.dot(choose, late_low, preferred_element_type=F32).astype(BF)
    late_up = jnp.einsum("as,bsf->baf", choose_own, late_up, preferred_element_type=F32).astype(BF)
    if paired:
        half_low, half_up = late_low.shape[1] // 2, late_up.shape[2] // 2
        late_low = jnp.concatenate([late_low[:, :half_low], late_low[:, half_low:]], axis=0)
        late_up = jnp.concatenate([late_up[:, :, :half_up], late_up[:, :, half_up:]], axis=1)
    late = jnp.concatenate(
        [jnp.broadcast_to(late_low[None], (blocks,) + late_low.shape), late_up], axis=2
    )
    late = jnp.broadcast_to(late[None], (parts,) + late.shape).reshape((owners,) + late.shape[1:])
    late = swap_all(late, everyone)
    if paired:
        (
            expand_low_out, shrink_up_out, merge_up_out, merge_low_out, expand_up_out, shrink_low_out,
        ) = settle_early(spot, shared, parts, ADAPTERS, wide, width, pad)
        late, shrink_up_out = lax.optimization_barrier((late, shrink_up_out))
        joined_low_out, joined_up_out = settle_late(late, parts, ADAPTERS, part_width, wide)
        joined_up_out = joined_up_out.transpose(0, 2, 1, 3)
        joined_low_out, expand_low_out, merge_low_out, shrink_low_out = (
            tall(each) for each in (joined_low_out, expand_low_out, merge_low_out, shrink_low_out)
        )
    else:
        late = late.reshape(parts, blocks, ADAPTERS, -1)
        joined_low_out = tall(ranks_in(late[..., :low_size], part_width).reshape(ADAPTERS, rank, model))
        joined_up_out = ranks_in(late[..., low_size:], piece).reshape(ADAPTERS, rank, 3, wide).astype(F32)
        shared = ranks_in(shared.reshape(parts, blocks, ADAPTERS, -1), early_width).astype(F32)
        expand_low_out, shrink_up_out, merge_up_out = (
            shared[..., i * part_width : (i + 1) * part_width].reshape(ADAPTERS, rank, model)
            for i in range(3)
        )
        expand_low_out = tall(expand_low_out)
        divided = lax.dynamic_index_in_dim(shared[..., 3 * part_width :], place, 2, keepdims=False)
        merge_low_out = tall(divided[:, :, :wide])
        expand_up_out = jnp.stack(
            [divided[:, :, wide + i * pad : wide + i * pad + width] for i in range(2)], axis=2
        )
        shrink_low_out = tall(divided[:, :, wide + 2 * pad : wide + 2 * pad + width])
    return (
        result,
        grad_hidden.astype(BF),
        joined_low_out,
        joined_up_out,
        merge_low_out,
        merge_up_out,
        expand_low_out,
        expand_up_out,
        shrink_low_out,
        shrink_up_out,
    )


def solution(mesh):
    in_specs = (
        P("dp", "mp", None),
        P("dp", "mp", None),
        P("dp"),
        P(),
        P(),
        P("dp", None, "mp"),
        P("dp", "mp"),
        P("dp", None, "mp"),
        P("dp", "mp"),
        P(),
        P(None, None, None, "mp"),
        P(None, "mp", None),
        P(),
        P(),
        P(None, None, None, "mp"),
        P(None, "mp", None),
        P(),
    )
    out_specs = (
        P("dp", "mp", None),
        P("dp", "mp", None),
        P(),
        P(None, None, None, "mp"),
        P(None, "mp", None),
        P(),
        P(),
        P(None, None, None, "mp"),
        P(None, "mp", None),
        P(),
    )
    return jax.shard_map(local, mesh=mesh, in_specs=in_specs, out_specs=out_specs, check_vma=False)
```

```python
import jax
import jax.numpy as jnp
from jax import lax
from jax.experimental import pallas as pl
from jax.experimental.pallas import tpu as pltpu
from jax.sharding import PartitionSpec as P

HEAD_DIM = 64
ADAPTERS = 8
ADAPTER_SCALE = 2.0
NORM_EPS = 1e-05
ROPE_BASE = 160000.0
LANES = 128
CH = 256
BF = jnp.bfloat16
F32 = jnp.float32


def nt(a, b):
    return lax.dot_general(a, b, (((1,), (1,)), ((), ())), preferred_element_type=F32)


def nn(a, b):
    return lax.dot_general(a, b, (((1,), (0,)), ((), ())), preferred_element_type=F32)


def tn(a, b):
    return lax.dot_general(a, b, (((0,), (0,)), ((), ())), preferred_element_type=F32)


def lanes_of(ref, first=0, count=None, spot=None):
    count = ref.shape[2] if count is None else count
    places = [part if spot is None else spot[1 + part] for part in range(ref.shape[0])]
    return jnp.concatenate([ref[place, 0, pl.ds(first, count), :] for place in places], axis=1)


def full(shape):
    return pl.BlockSpec(shape, lambda *_: (0,) * len(shape))


def full_once(shape):
    return pl.BlockSpec(shape, lambda *_: (0,) * len(shape), pipeline_mode=pl.Buffered(1))


def norm_parts(values):
    centred = values - jnp.mean(values, axis=-1, keepdims=True)
    spread = jnp.mean(centred * centred, axis=-1, keepdims=True)
    scale = lax.rsqrt(spread + NORM_EPS)
    return centred * scale, scale


def norm_back(grads, normed, scale, gain):
    weighted = grads * gain
    return scale * (
        weighted
        - jnp.mean(weighted, axis=-1, keepdims=True)
        - normed * jnp.mean(weighted * normed, axis=-1, keepdims=True)
    )


def turn(values, cosine, sine):
    width = values.shape[1]
    half = HEAD_DIM // 2
    many = width // LANES
    if many > 1:
        cosine = jnp.concatenate([cosine] * many, axis=1)
        sine = jnp.concatenate([sine] * many, axis=1)
    lane = lax.broadcasted_iota(jnp.int32, values.shape, 1)
    turned = jnp.where(
        lane % HEAD_DIM < half,
        -pltpu.roll(values, width - half, 1),
        pltpu.roll(values, half, 1),
    )
    return values * cosine + turned * sine


def project_kernel(
    place, own, beside, across, corner, weight, low, up, cosine, sine,
    query, key, value, down, *, wide
):
    table = lanes_of(weight, 0, 3 * wide, place)
    for step, piece in enumerate((own, beside, across, corner)):
        spot = place[0] ^ step
        rows = piece[0]
        small = (nt(rows, low[0]) * ADAPTER_SCALE).astype(BF)
        down[0, step] = small
        out = nt(rows, table) + nn(small, up[0])
        cos, sin = cosine[spot], sine[spot]
        turned = turn(out[:, :wide], cos, sin)
        query[0, spot] = (turned * HEAD_DIM**-0.5).astype(BF)
        key[0, spot] = turn(out[:, wide : 2 * wide], cos, sin).astype(BF)
        value[0, spot] = out[:, 2 * wide :].astype(BF)


def project(place, pieces, weight, low, up, tables):
    seqs, own, model = pieces[0].shape
    tall = up.shape[2]
    wide = tall // 3
    rank = low.shape[1]
    blocks = len(pieces)
    piece = pl.BlockSpec((1, own, model), lambda s, p: (s, 0, 0))
    result = pl.BlockSpec((1, blocks, own, wide), lambda s, p: (s, 0, 0, 0))
    table = pl.BlockSpec((blocks, own, LANES), lambda s, p: (0, 0, 0))
    return pl.pallas_call(
        lambda *refs: project_kernel(*refs, wide=wide),
        grid_spec=pltpu.PrefetchScalarGridSpec(
            num_scalar_prefetch=1,
            grid=(seqs,),
            in_specs=[piece] * blocks
            + [
                pl.BlockSpec(weight.shape, lambda s, p: (0, 0, 0, 0)),
                pl.BlockSpec((1, rank, model), lambda s, p: (s, 0, 0)),
                pl.BlockSpec((1, rank, tall), lambda s, p: (s, 0, 0)),
                table,
                table,
            ],
            out_specs=[result] * 3
            + [pl.BlockSpec((1, blocks, own, rank), lambda s, p: (s, 0, 0, 0))],
        ),
        out_shape=[jax.ShapeDtypeStruct((seqs, blocks, own, wide), BF)] * 3
        + [jax.ShapeDtypeStruct((seqs, blocks, own, rank), BF)],
        name="project",
    )(place, *pieces, weight, low, up, *tables)


def one_head(values, head):
    lane = lax.broadcasted_iota(jnp.int32, values.shape, 1)
    return jnp.where((lane // HEAD_DIM) == head, values, jnp.zeros_like(values))


def attend_kernel(place, query, key, value, *outs):
    *contexts, probs, shrinks, held = outs
    blocks, own = query.shape[1:3]
    tile = pl.program_id(1)
    keys = key[0].reshape(blocks * own, LANES)
    turned = value[0].reshape(blocks * own, LANES).T
    rows = jnp.concatenate([query[0, place[0] ^ (2 * tile + i)] for i in range(2)], axis=0)
    parts = []
    for head in range(2):
        mine = one_head(rows, head)
        held[...] = nt(keys, mine)
        top = jnp.max(held[...], axis=0, keepdims=True)

        def some(i, sums):
            at = pl.ds(pl.multiple_of(i * CH, CH), CH)
            raised = jnp.exp(held[at, :] - top)
            probs[0, 0, head, at, :] = raised.astype(BF)
            return sums + jnp.sum(raised.reshape(CH // 8, 8, raised.shape[1]), axis=0)

        sums = lax.fori_loop(0, blocks * own // CH, some, jnp.zeros((8, 2 * own), F32))
        shrink = 1.0 / jnp.sum(sums, axis=0, keepdims=True)
        shrinks[0, 0, head : head + 1] = shrink
        parts.append(nn(turned[head * HEAD_DIM : (head + 1) * HEAD_DIM], probs[0, 0, head]) * shrink)
    merged = jnp.concatenate(parts, axis=0).T.astype(BF)
    for half in range(blocks // 2):
        @pl.when(tile == half)
        def _():
            for i in range(2):
                contexts[2 * half + i][...] = merged[i * own : (i + 1) * own]


def attend(place, query, key, value, seq):
    _, blocks, own, wide = query.shape
    pairs = wide // LANES
    whole = pl.BlockSpec((1, blocks, own, LANES), lambda h, t, p: (seq, 0, 0, h))
    *contexts, probs, shrinks = pl.pallas_call(
        attend_kernel,
        grid_spec=pltpu.PrefetchScalarGridSpec(
            num_scalar_prefetch=1,
            grid=(pairs, blocks // 2),
            in_specs=[whole] * 3,
            out_specs=[pl.BlockSpec((own, LANES), lambda h, t, p: (0, h))] * blocks
            + [
                pl.BlockSpec((1, 1, 2, blocks * own, 2 * own), lambda h, t, p: (h, t, 0, 0, 0)),
                pl.BlockSpec((1, 1, 2, 2 * own), lambda h, t, p: (h, t, 0, 0)),
            ],
            scratch_shapes=[pltpu.VMEM((blocks * own, 2 * own), F32)],
        ),
        out_shape=[jax.ShapeDtypeStruct((own, wide), BF)] * blocks
        + [
            jax.ShapeDtypeStruct((pairs, blocks // 2, 2, blocks * own, 2 * own), BF),
            jax.ShapeDtypeStruct((pairs, blocks // 2, 2, 2 * own), F32),
        ],
        name="attend",
    )(place, query, key, value)
    return contexts, (probs, shrinks, list(contexts))


def attend_back_kernel(place, query, key, value, probs, shrinks, *refs):
    blocks, own = query.shape[1:3]
    contexts = refs[:blocks]
    pieces = refs[blocks : 2 * blocks]
    rows_in = refs[2 * blocks : 3 * blocks]
    cosine, sine, weight, low, up, down, here, there, up_grad, low_grad, total, small, turn_keys = refs[3 * blocks :]
    pair = pl.program_id(0)
    last = pl.num_programs(0) - 1
    wide = LANES * pl.num_programs(0)
    keys = key[0].reshape(blocks * own, LANES)
    values = value[0].reshape(blocks * own, LANES)
    turned = keys.T
    backs, mines, mine_grads = [], [], []
    grad_queries = []
    for step in range(0, blocks, 2):
        spots = [place[0] ^ (step + i) for i in range(2)]
        rows = jnp.concatenate([query[0, spot] for spot in spots], axis=0)
        outer = jnp.concatenate([pieces[step + i][0] for i in range(2)], axis=0).astype(F32)
        inner = jnp.concatenate([contexts[step + i][...] for i in range(2)], axis=0).astype(F32)
        product = (outer * inner).T
        factors = [shrinks[0, step // 2, head : head + 1] for head in range(2)]
        spread = jnp.concatenate([jnp.broadcast_to(f, (HEAD_DIM, 2 * own)) for f in factors], axis=0).T
        outer = (outer * spread).astype(BF)
        parts = []
        for head in range(2):
            mine_grad = one_head(outer, head)
            chances = probs[0, step // 2, head]
            half = product[head * HEAD_DIM : (head + 1) * HEAD_DIM]
            mean = jnp.sum(half, axis=0, keepdims=True) * factors[head]
            back = (chances.astype(F32) * (nt(values, mine_grad) - mean)).astype(BF)
            parts.append(nn(turned[head * HEAD_DIM : (head + 1) * HEAD_DIM], back))
            backs.append(back)
            mines.append(one_head(rows, head))
            mine_grads.append(mine_grad)
        queries = jnp.concatenate(parts, axis=0).T * HEAD_DIM**-0.5
        for i, spot in enumerate(spots):
            part = queries[i * own : (i + 1) * own]
            grad_queries.append(turn(part, cosine[spot], -sine[spot]).astype(BF))
    grad_keys = nn(jnp.concatenate(backs, axis=1), jnp.concatenate(mines, axis=0))
    chances = [probs[0, i // 2, i % 2] for i in range(blocks)]
    grad_values = nn(jnp.concatenate(chances, axis=1), jnp.concatenate(mine_grads, axis=0))
    for step in range(blocks):
        part = slice(step * own, (step + 1) * own)
        turn_keys[0, step] = turn(grad_keys[part], cosine[step], -sine[step]).astype(BF)
        turn_keys[1, step] = grad_values[part].astype(BF)
    grads = [
        jnp.concatenate(grad_queries, axis=0),
        jnp.concatenate([turn_keys[0, place[0] ^ step] for step in range(blocks)], axis=0),
        jnp.concatenate([turn_keys[1, place[0] ^ step] for step in range(blocks)], axis=0),
    ]
    grads = jnp.concatenate(grads, axis=1)
    firsts = [pl.multiple_of(kind * wide + pair * LANES, LANES) for kind in range(3)]
    table = jnp.concatenate([lanes_of(weight, first, LANES, place) for first in firsts], axis=0)
    ups = jnp.concatenate([up[0, :, pl.ds(first, LANES)] for first in firsts], axis=1)
    downs = jnp.concatenate([down[0, step] for step in range(blocks)], axis=0)
    more = nn(grads, table)
    more_small = nt(grads, ups)
    up_part = tn(downs, grads)
    for kind in range(3):
        up_grad[kind] = up_part[:, kind * LANES : (kind + 1) * LANES].astype(BF)

    @pl.when(pair == 0)
    def _():
        total[...] = more
        small[...] = more_small

    @pl.when(pair > 0)
    def _():
        total[...] += more
        small[...] += more_small

    @pl.when(pair == last)
    def _():
        narrow = (small[...] * ADAPTER_SCALE).astype(BF)
        low_grad[...] = tn(narrow, jnp.concatenate([piece[0] for piece in rows_in], axis=0)).astype(BF)
        done = total[...] + nn(narrow, low[0])
        for step in range(blocks):
            part = done[step * own : (step + 1) * own].astype(BF)
            (there if step % 2 else here)[step // 2] = part


def attend_back(place, seq, query, key, value, kept, grads, pieces, tables, weight, low, up, down):
    _, blocks, own, wide = query.shape
    _, rank, model = low.shape
    tall = up.shape[2]
    pairs = wide // LANES
    whole = lambda shape: pl.BlockSpec(shape, lambda h, p: (0,) * len(shape))
    of_seq = lambda shape: pl.BlockSpec((1,) + shape, lambda h, p: (seq,) + (0,) * len(shape))
    heads = pl.BlockSpec((1, blocks, own, LANES), lambda h, p: (seq, 0, 0, h))
    probs, shrinks, contexts = kept
    return pl.pallas_call(
        attend_back_kernel,
        grid_spec=pltpu.PrefetchScalarGridSpec(
            num_scalar_prefetch=1,
            grid=(pairs,),
            in_specs=[heads] * 3
            + [pl.BlockSpec((1,) + probs.shape[1:], lambda h, p: (h, 0, 0, 0, 0))]
            + [pl.BlockSpec((1,) + shrinks.shape[1:], lambda h, p: (h, 0, 0, 0))]
            + [pl.BlockSpec((own, LANES), lambda h, p: (0, h))] * blocks
            + [pl.BlockSpec((1, own, LANES), lambda h, p: (max(seq - 1, 0), 0, h))] * blocks
            + [of_seq((own, model))] * blocks
            + [whole((blocks, own, LANES))] * 2
            + [
                whole(weight.shape),
                of_seq((rank, model)),
                of_seq((rank, tall)),
                of_seq((blocks, own, rank)),
            ],
            out_specs=[
                whole((blocks // 2, own, model)),
                whole((blocks // 2, own, model)),
                pl.BlockSpec((3, rank, LANES), lambda h, p: (0, 0, h)),
                whole((rank, model)),
            ],
            scratch_shapes=[
                pltpu.VMEM((blocks * own, model), F32),
                pltpu.VMEM((blocks * own, rank), F32),
                pltpu.VMEM((2, blocks, own, LANES), BF),
            ],
        ),
        out_shape=[
            jax.ShapeDtypeStruct((blocks // 2, own, model), BF),
            jax.ShapeDtypeStruct((blocks // 2, own, model), BF),
            jax.ShapeDtypeStruct((3, rank, wide), BF),
            jax.ShapeDtypeStruct((rank, model), BF),
        ],
        name="attend_back",
    )(place, query, key, value, probs, shrinks, *contexts, *grads, *pieces, *tables, weight, low, up, down)


def merge_kernel(spot, *refs, blocks, seqs):
    contexts = refs[: blocks * seqs]
    start, near, far, low, up, gain, middle, normed, down = refs[blocks * seqs :]
    tables = [lanes_of((far if i // 2 else near).at[:, pl.ds(i % 2, 1)], spot=spot) for i in range(blocks)]
    for seq in range(seqs):
        total = start[seq].astype(F32)
        small = jnp.zeros(down.shape[1:], F32)
        for step in range(blocks):
            rows = contexts[seq * blocks + step][...]
            small += nt(rows, low[step, seq])
            total += nn(rows, tables[step])
        small = (small * ADAPTER_SCALE).astype(BF)
        down[seq] = small
        total += nn(small, up[seq])
        middle[seq] = total
        normed[seq] = (norm_parts(total)[0] * gain[...]).astype(BF)


def merge(spot, contexts, start, near, far, low, up, gain):
    seqs, own, model = start.shape
    blocks, _, rank, wide = low.shape
    inputs = [piece for context in contexts for piece in context]
    inputs += [start, near, far, low, up, gain]
    results = [
        jax.ShapeDtypeStruct((seqs, own, model), F32),
        jax.ShapeDtypeStruct((seqs, own, model), BF),
        jax.ShapeDtypeStruct((seqs, own, rank), BF),
    ]
    return pl.pallas_call(
        lambda *refs: merge_kernel(*refs, blocks=blocks, seqs=seqs),
        grid_spec=pltpu.PrefetchScalarGridSpec(
            num_scalar_prefetch=1,
            grid=(1,),
            in_specs=[full(each.shape) for each in inputs],
            out_specs=[full(each.shape) for each in results],
        ),
        out_shape=results,
        name="merge",
    )(spot, *inputs)


def gated_kernel(
    place, rows, out_grad, middle, expand, shrink, expand_up, shrink_low, expand_low, shrink_up, mask,
    near, far, merge_low, merge_up, gain, merge_down, *refs, width, blocks, seqs
):
    contexts = refs[: seqs * blocks]
    (
        result, expand_up_grad, shrink_low_grad, expand_low_grad, shrink_up_grad,
        grad_middle, merge_low_grad, merge_up_grad,
    ) = refs[seqs * blocks : seqs * blocks + 8]
    firsts = refs[seqs * blocks + 8 : seqs * blocks + 8 + blocks]
    others = refs[seqs * blocks + 8 + blocks : seqs * blocks + 8 + 2 * blocks]
    total, grad_rows, down, down_grad, late, late_grad = refs[seqs * blocks + 8 + 2 * blocks :]
    step = pl.program_id(0)
    scaled = ADAPTER_SCALE * mask[...]

    @pl.when(step == 0)
    def _():
        total[...] = middle[...]
        grad_rows[...] = jnp.zeros(grad_rows.shape, F32)
        down[...] = (nt(rows[...], expand_low[...]) * scaled).astype(BF)
        down_grad[...] = (nt(out_grad[...], shrink_up[...]) * scaled).astype(BF)
        late[...] = jnp.zeros(late.shape, F32)
        late_grad[...] = jnp.zeros(late_grad.shape, F32)

    values = lanes_of(expand, 0, width)
    gates = lanes_of(expand, width, width)
    outs = lanes_of(shrink)
    up_values = expand_up[0, :, :width]
    up_gates = expand_up[0, :, expand_up.shape[2] // 2 : expand_up.shape[2] // 2 + width]
    low_outs = shrink_low[0, :, :width]
    first = nt(rows[...], values) + nn(down[...], up_values)
    second = nt(rows[...], gates) + nn(down[...], up_gates)
    chance = 0.5 + 0.5 * lax.erf(first * (0.5**0.5))
    curve = first * chance
    slope = chance + first * (jnp.exp(-0.5 * first * first) * 0.3989422804014327)
    active = (curve * second).astype(BF)
    grads = nt(out_grad[...], outs) + nn(down_grad[...], low_outs)
    first_grad = (grads * second * slope).astype(BF)
    second_grad = (grads * curve).astype(BF)
    total[...] += nn(active, outs)
    late[...] += nt(active, low_outs)
    grad_rows[...] += nn(first_grad, values) + nn(second_grad, gates)
    late_grad[...] += nt(first_grad, up_values) + nt(second_grad, up_gates)
    expand_up_grad[0, 0] = tn(down[...], first_grad).astype(BF)
    expand_up_grad[0, 1] = tn(down[...], second_grad).astype(BF)
    shrink_low_grad[0] = tn(down_grad[...], active).astype(BF)

    @pl.when(step == blocks - 1)
    def _():
        small = (late[...] * scaled).astype(BF)
        result[...] = (total[...] + nn(small, shrink_up[...])).astype(BF)
        shrink_up_grad[...] = tn(small, out_grad[...]).astype(BF)
        small_grad = (late_grad[...] * scaled).astype(BF)
        expand_low_grad[...] = tn(small_grad, rows[...]).astype(BF)
        own = rows.shape[0] // seqs
        for seq in range(seqs):
            part = slice(seq * own, (seq + 1) * own)
            normed, scale = norm_parts(middle[part])
            grad_normed = grad_rows[part] + nn(small_grad[part], expand_low[...])
            whole = out_grad[part].astype(F32) + norm_back(grad_normed, normed, scale, gain[...])
            grad_middle[seq] = whole
            low_rows = whole.astype(BF)
            small = (nt(low_rows, merge_up[seq]) * ADAPTER_SCALE).astype(BF)
            for move in range(blocks):
                ref = far if move // 2 else near
                table = lanes_of(ref.at[:, pl.ds(move % 2, 1)], spot=place)
                out = (nt(low_rows, table) + nn(small, merge_low[move, seq])).astype(BF)
                if seq:
                    others[move][seq - 1] = out
                else:
                    firsts[move][0] = out
                merge_low_grad[seq, move] = tn(small, contexts[seq * blocks + move][...]).astype(BF)
            merge_up_grad[seq] = tn(merge_down[seq], low_rows).astype(BF)


def gated(
    place, rows, out_grad, middle, weights, width, expand_up, shrink_low, expand_low, shrink_up, mask,
    near, far, merge_low, merge_up, gain, merge_down, contexts
):
    count, model = rows.shape
    parts, blocks, _, lane = weights.shape
    seqs = len(contexts)
    own, wide = contexts[0][0].shape
    some = merge_up.shape[1]
    rank = expand_low.shape[0]
    pad = shrink_low.shape[2]
    pieces = [piece for context in contexts for piece in context]
    shapes = [
        ((count, model), BF),
        ((blocks, 2, rank, width), BF),
        ((blocks, rank, width), BF),
        ((rank, model), BF),
        ((rank, model), BF),
        ((seqs, own, model), F32),
        ((seqs, blocks, some, wide), BF),
        ((seqs, some, model), BF),
    ]
    shapes += [((1, own, wide), BF)] * blocks + [((seqs - 1, own, wide), BF)] * blocks
    out_specs = [full_once(shape) for shape, _ in shapes]
    out_specs[1] = pl.BlockSpec((1, 2, rank, width), lambda m, p: (m, 0, 0, 0))
    out_specs[2] = pl.BlockSpec((1, rank, width), lambda m, p: (m, 0, 0))
    return pl.pallas_call(
        lambda *refs: gated_kernel(*refs, width=width, blocks=blocks, seqs=seqs),
        grid_spec=pltpu.PrefetchScalarGridSpec(
            num_scalar_prefetch=1,
            grid=(blocks,),
            in_specs=[
                full_once((count, model)),
                full_once((count, model)),
                full_once((count, model)),
                pl.BlockSpec((parts, 1, 2 * width, lane), lambda m, p: (0, m, 0, 0)),
                pl.BlockSpec((parts, 1, width, lane), lambda m, p: (0, m, 2, 0)),
                pl.BlockSpec((1, rank, 2 * pad), lambda m, p: (p[0] ^ m, 0, 0)),
                pl.BlockSpec((1, rank, pad), lambda m, p: (p[0] ^ m, 0, 0)),
                full_once((rank, model)),
                full_once((rank, model)),
                full_once((count, rank)),
                full_once(near.shape),
                full_once(far.shape),
                full_once(merge_low.shape),
                full_once(merge_up.shape),
                full_once(gain.shape),
                full_once(merge_down.shape),
            ]
            + [full_once((own, wide))] * len(pieces),
            out_specs=out_specs,
            scratch_shapes=[
                pltpu.VMEM((count, model), F32),
                pltpu.VMEM((count, model), F32),
                pltpu.VMEM((count, rank), BF),
                pltpu.VMEM((count, rank), BF),
                pltpu.VMEM((count, rank), F32),
                pltpu.VMEM((count, rank), F32),
            ],
        ),
        out_shape=[jax.ShapeDtypeStruct(shape, kind) for shape, kind in shapes],
        name="gated",
    )(
        place, rows, out_grad, middle, weights, weights, expand_up, shrink_low, expand_low, shrink_up, mask,
        near, far, merge_low, merge_up, gain, merge_down, *pieces,
    )


def settle_early_kernel(place, got, low, shrink_up, merge_up, merge_low, expand_up, shrink_low, *, parts, blocks, sets, part, wide, width, pad):
    at = 3 * part
    for g in range(parts):
        for block in range(blocks):
            rows = got[g * blocks + block, :, :at].astype(F32)
            for i, out in enumerate((low, shrink_up, merge_up)):
                for two in range(2):
                    cut = rows[two * sets : (two + 1) * sets, i * part : (i + 1) * part]
                    out[:, two * parts + g, block * part : (block + 1) * part] = cut
        rows = got[g * blocks + place[0], :, at:].astype(F32)
        for two in range(2):
            cut = rows[two * sets : (two + 1) * sets]
            rank = two * parts + g
            merge_low[:, rank, :] = cut[:, :wide]
            for kind in range(2):
                first = wide + kind * pad
                expand_up[:, rank, kind, :] = cut[:, first : first + width]
            shrink_low[:, rank, :] = cut[:, wide + 2 * pad : wide + 2 * pad + width]


def settle_early(place, got, parts, sets, wide, width, pad):
    owners, rows, features = got.shape
    blocks = owners // parts
    rank = rows // sets * parts
    part = (features - wide - 3 * pad) // 3
    model = blocks * part
    shapes = [(rank, model)] * 3 + [(rank, wide), (rank, 2, width), (rank, width)]
    shapes = [(sets,) + shape for shape in shapes]
    whole = lambda shape: pl.BlockSpec(shape, lambda i, p: (0,) * len(shape))
    return pl.pallas_call(
        lambda *refs: settle_early_kernel(
            *refs, parts=parts, blocks=blocks, sets=sets, part=part, wide=wide, width=width, pad=pad
        ),
        grid_spec=pltpu.PrefetchScalarGridSpec(
            num_scalar_prefetch=1,
            grid=(1,),
            in_specs=[whole(got.shape)],
            out_specs=[whole(shape) for shape in shapes],
        ),
        out_shape=[jax.ShapeDtypeStruct(shape, F32) for shape in shapes],
        name="settle_early",
    )(place, got)


def settle_late_kernel(got, low, up, *, parts, blocks, sets, part, piece):
    wide = up.shape[3]
    for g in range(parts):
        rows = [got[g * blocks + block].astype(F32) for block in range(blocks)]
        tail = jnp.concatenate([row[:, part : part + piece] for row in rows], axis=1)
        for two in range(2):
            rank = two * parts + g
            for block, row in enumerate(rows):
                low[:, rank, block * part : (block + 1) * part] = row[two * sets : (two + 1) * sets, :part]
            for kind in range(up.shape[1]):
                up[:, kind, rank, :] = tail[two * sets : (two + 1) * sets, kind * wide : (kind + 1) * wide]


def settle_late(got, parts, sets, part, wide):
    owners, rows, features = got.shape
    blocks = owners // parts
    rank = rows // sets * parts
    piece = features - part
    shapes = [(sets, rank, blocks * part), (sets, blocks * piece // wide, rank, wide)]
    return pl.pallas_call(
        lambda *refs: settle_late_kernel(*refs, parts=parts, blocks=blocks, sets=sets, part=part, piece=piece),
        grid=(1,),
        in_specs=[full(got.shape)],
        out_specs=[full(shape) for shape in shapes],
        out_shape=[jax.ShapeDtypeStruct(shape, F32) for shape in shapes],
        name="settle_late",
    )(got)


def pair_swap(values, bit):
    size = lax.axis_size("mp")
    return lax.ppermute(values, "mp", [(i, i ^ bit) for i in range(size)])


def tie(values, after):
    return lax.optimization_barrier((values, after))[0]


def swap_all(values, axes):
    return lax.all_to_all(values, axes, 0, 0, tiled=True)


def share_all(values, axes):
    size = 1
    for axis in (axes,) if isinstance(axes, str) else axes:
        size *= lax.axis_size(axis)
    return swap_all(jnp.broadcast_to(values[None], (size,) + values.shape), axes)


def gather_parts(values):
    parts = lax.axis_size("dp")
    here = lax.axis_index("dp")
    every = jnp.arange(parts, dtype=jnp.int32)
    if parts != 8:
        return share_all(values, "dp"), every
    stack = [values]
    for shift in range(2, parts, 2):
        stack.append(lax.ppermute(values, "dp", [(i, (i + shift) % parts) for i in range(parts)]))
    stack = jnp.stack(stack)
    other = lax.ppermute(stack, "dp", [(i, i ^ 1) for i in range(parts)])
    order = (every % 2 ^ here % 2) * (parts // 2) + (here // 2 - every // 2) % (parts // 2)
    return jnp.concatenate([stack, other]), order.astype(jnp.int32)


def full_lanes(whole):
    parts, blocks, count, own = whole.shape
    if own == LANES:
        return whole
    tiles = parts * own // LANES
    whole = whole.transpose(1, 2, 0, 3).reshape(blocks, count, tiles, LANES)
    return whole.transpose(2, 0, 1, 3)


def local(
    hidden,
    cotangent,
    adapter_ids,
    attn_gain,
    mlp_gain,
    joined_weight,
    merge_weight_matrix,
    expand_weight,
    shrink_weight_matrix,
    joined_lower,
    joined_up_matrices,
    merge_lower,
    merge_up_matrices,
    expand_lower,
    expand_up_matrices,
    shrink_lower,
    shrink_up_matrices,
):
    parts, blocks = lax.axis_size("dp"), lax.axis_size("mp")
    place = lax.axis_index("mp")
    pair, core = place // 2, place % 2
    spot = place[None].astype(jnp.int32)
    seqs, own, model = hidden.shape
    length = own * blocks
    row_in = joined_weight.shape[0]
    wide = joined_weight.shape[2]
    width = expand_weight.shape[2]
    rank = joined_lower.shape[2]
    count = seqs * own

    rest = jnp.concatenate(
        [expand_weight.reshape(row_in, 2 * width).T, shrink_weight_matrix.T], axis=0
    )
    rest_whole = full_lanes(
        lax.all_gather(rest, ("dp", "mp"), axis=0, tiled=True).reshape(parts, blocks, 3 * width, row_in)
    )

    note = jnp.zeros((8, row_in), BF).at[0, :seqs].set(adapter_ids.astype(BF))
    joined_mine = jnp.concatenate(
        [joined_weight.reshape(row_in, 3 * wide).T, merge_weight_matrix.T, note], axis=0
    )
    joined_got, order = gather_parts(joined_mine)
    every_id = joined_got[:, 4 * wide, :seqs][order].astype(jnp.int32)
    if row_in != LANES:
        order = jnp.arange(model // LANES, dtype=jnp.int32)
    spot = jnp.concatenate([spot, order])
    joined_whole = full_lanes(joined_got[:, None])

    attn_scale = attn_gain.astype(F32)[None, :]
    mlp_scale = mlp_gain.astype(F32)[None, :]
    first_normed, first_scale = norm_parts(hidden.astype(F32))
    normed = (first_normed * attn_scale).astype(BF)
    def pick(table):
        return table.at[adapter_ids].get(mode="promise_in_bounds")

    def pick_low(table):
        return pick(table).transpose(0, 2, 1)

    def pick_up(table):
        return pick(table).reshape(seqs, rank, -1)

    joined_low, joined_up = pick_low(joined_lower), pick_up(joined_up_matrices)
    expand_low = pick_low(expand_lower).reshape(seqs * rank, model)
    merge_up = pick_up(merge_up_matrices)
    shrink_up = pick_up(shrink_up_matrices).reshape(seqs * rank, model)
    pad = -(-width // LANES) * LANES
    side = [(0, 0), (0, 0), (0, pad - width)]
    expand_mine = pick(expand_up_matrices)
    mine = jnp.concatenate(
        [
            pick_low(merge_lower),
            jnp.pad(expand_mine[:, :, 0], side),
            jnp.pad(expand_mine[:, :, 1], side),
            jnp.pad(pick_low(shrink_lower), side),
        ],
        axis=2,
    )
    far_sets = pair_swap(mine, 2)
    split_sets = jnp.stack([mine, pair_swap(mine, 1), far_sets, pair_swap(far_sets, 1)])
    merge_low = split_sets[:, :, :, :wide]
    expand_up = split_sets[:, :, :, wide : wide + 2 * pad].reshape(blocks, seqs * rank, 2 * pad)
    shrink_low = split_sets[:, :, :, wide + 2 * pad :].reshape(blocks, seqs * rank, pad)
    mask = (
        (jnp.arange(count) // own)[:, None] == (jnp.arange(seqs * rank) // rank)[None, :]
    ).astype(F32)

    half = HEAD_DIM // 2
    inverse = ROPE_BASE ** (-((jnp.arange(LANES) % half).astype(F32) * 2.0 / HEAD_DIM))
    angles = jnp.arange(length, dtype=F32)[:, None] * inverse[None, :]
    tables = [table.reshape(blocks, own, LANES) for table in (jnp.cos(angles), jnp.sin(angles))]

    across = pair_swap(normed, 2)
    beside = pair_swap(normed, 1)
    (
        across, joined_low, joined_up, tables, merge_low, merge_up,
        expand_low, expand_up, shrink_low, shrink_up, mask,
    ) = lax.optimization_barrier(
        (
            across, joined_low, joined_up, tables, merge_low, merge_up,
            expand_low, expand_up, shrink_low, shrink_up, mask,
        )
    )
    corner = pair_swap(across, 1)
    pieces = (normed, beside, across, corner)
    query, key, value, joined_down = project(
        spot, pieces, joined_whole, joined_low, joined_up,
        tables,
    )
    merge_own = joined_whole[:, :, 3 * wide : 4 * wide]
    merge_near = jnp.concatenate([merge_own, pair_swap(merge_own, 1)], axis=1)
    contexts, logs = [], []
    for seq in range(seqs):
        if seq:
            query = tie(query, context[0])
        context, probs = attend(spot, query, key, value, seq)
        context = [context[0]] + [pair_swap(context[bit], bit) for bit in range(1, blocks)]
        contexts.append(context)
        logs.append(probs)
    merge_far = pair_swap(merge_near, 2)
    middle, normed_mlp, merge_down = merge(
        spot, contexts, hidden, merge_near, merge_far, merge_low, merge_up, mlp_scale
    )
    (
        result, expand_up_grad, shrink_low_grad, expand_low_grad, shrink_up_grad,
        grad_middle, merge_low_grads, merge_up_grads, *grad_contexts,
    ) = gated(
        spot, normed_mlp.reshape(count, model), cotangent.reshape(count, model),
        middle.reshape(count, model), rest_whole, width,
        expand_up, shrink_low, expand_low, shrink_up, mask,
        merge_near, merge_far, merge_low, merge_up, mlp_scale, merge_down, contexts,
    )
    result = result.reshape(middle.shape)
    halfway = []
    for some in (grad_contexts[:blocks], grad_contexts[blocks:]):
        halfway.append([some[0]] + [pair_swap(some[bit], bit) for bit in range(1, blocks)])

    paired = rank == 2 * parts
    everyone = ("dp", "mp")
    owners = parts * blocks
    ids = jnp.broadcast_to(every_id[:, None], (parts, blocks, seqs))
    choose = (jnp.arange(ADAPTERS)[:, None] == ids.reshape(1, -1)).astype(BF)
    choose_own = (jnp.arange(ADAPTERS)[:, None] == every_id.reshape(1, -1)).astype(BF)
    part_width = model // blocks

    def by_block(grad):
        return grad.reshape(seqs * rank, blocks, -1).transpose(1, 0, 2)

    def ranks_out(grad):
        if paired:
            split = grad.reshape(grad.shape[0], seqs, 2, parts, -1).transpose(3, 0, 1, 2, 4)
            return split.reshape(split.shape[:3] + (-1,))
        return grad.reshape(grad.shape[0], seqs, parts, -1).transpose(2, 0, 1, 3)

    def ranks_in(whole, features):
        whole = whole.transpose(2, 1, 0, 3).reshape(ADAPTERS, whole.shape[1], rank, features)
        return whole.transpose(0, 2, 1, 3)

    def tall(values):
        return values.transpose(0, 2, 1).astype(F32)

    joined_low_grads, joined_up_grads = [], []
    grad_normeds = []
    early = jnp.concatenate(
        [
            piece.astype(BF)
            for piece in (
                by_block(expand_low_grad),
                by_block(shrink_up_grad),
                by_block(merge_up_grads.reshape(seqs * rank, model)),
                jnp.take(
                    merge_low_grads.transpose(1, 0, 2, 3).reshape(blocks, seqs * rank, wide),
                    place ^ jnp.arange(blocks), axis=0,
                ),
                jnp.pad(expand_up_grad[:, 0], side),
                jnp.pad(expand_up_grad[:, 1], side),
                jnp.pad(shrink_low_grad, side),
            )
        ],
        axis=2,
    )
    early_width = early.shape[2]

    early, halfway[0] = lax.optimization_barrier((early, halfway[0]))
    early = swap_all(ranks_out(early).reshape(owners, seqs, -1), everyone)
    chip, far = None, None
    for seq in range(seqs):
        pieces_back = list(halfway[min(seq, 1)])
        if seq:
            pieces_back[0] = tie(pieces_back[0], here)
        here, there, up_grad, low_grad = attend_back(
            spot, seq, query, key, value, logs[seq], pieces_back, pieces, tables,
            joined_whole, joined_low, joined_up, joined_down,
        )
        if seq == 0:
            there, halfway[1] = lax.optimization_barrier((there, halfway[1]))
        if seq == 1:
            there, far, early = lax.optimization_barrier((there, far, early))
            by_seq = choose.reshape(ADAPTERS, owners, seqs)
            early = sum(
                jnp.dot(by_seq[:, :, i], early[:, i], preferred_element_type=F32) for i in range(seqs)
            )
            if paired:
                early = jnp.concatenate([early[:, :early_width], early[:, early_width:]], axis=0)
            shared = lax.all_gather(early.astype(BF), everyone, axis=0)
        if seq == 2:
            there, far = lax.optimization_barrier((there, far))
        if seq:
            grad_normeds.append(chip + (far,))
        joined_up_grads.append(up_grad.transpose(1, 0, 2).reshape(rank, 3 * wide))
        joined_low_grads.append(low_grad)
        there = pair_swap(there, 1)
        give = (here[1].astype(F32) + there[1].astype(F32)).astype(BF)
        chip = (here[0], there[0])
        far = pair_swap(give, 2)

    piece = 3 * wide // blocks
    late_low = ranks_out(by_block(jnp.concatenate(joined_low_grads)).astype(BF))
    late_up = jnp.stack(joined_up_grads).astype(BF).reshape(seqs * rank, blocks, piece)
    late_up = ranks_out(late_up.transpose(1, 0, 2))
    some = 2 if paired else 1
    late_low, late_up = (each.reshape(owners, seqs * some, -1) for each in (late_low, late_up))
    low_size = late_low.shape[2]
    late = jnp.concatenate([late_low, late_up], axis=2)
    late = tie(late, there)
    late, far = lax.optimization_barrier((swap_all(late, everyone), far))
    late = late.reshape(parts, blocks, seqs, some, -1)
    grad_normeds.append(chip + (far,))
    grad_normeds = [sum(part.astype(F32) for part in parts_of) for parts_of in grad_normeds]
    grad_hidden = grad_middle + norm_back(jnp.stack(grad_normeds), first_normed, first_scale, attn_scale)
    late_low = late[..., :low_size].reshape(owners * seqs, -1)
    late_up = late[..., low_size:].transpose(1, 0, 2, 3, 4).reshape(blocks, parts * seqs, -1)
    late_low = jnp.dot(choose, late_low, preferred_element_type=F32).astype(BF)
    late_up = jnp.einsum("as,bsf->baf", choose_own, late_up, preferred_element_type=F32).astype(BF)
    if paired:
        half_low, half_up = late_low.shape[1] // 2, late_up.shape[2] // 2
        late_low = jnp.concatenate([late_low[:, :half_low], late_low[:, half_low:]], axis=0)
        late_up = jnp.concatenate([late_up[:, :, :half_up], late_up[:, :, half_up:]], axis=1)
    late = jnp.concatenate(
        [jnp.broadcast_to(late_low[None], (blocks,) + late_low.shape), late_up], axis=2
    )
    late = jnp.broadcast_to(late[None], (parts,) + late.shape).reshape((owners,) + late.shape[1:])
    late = swap_all(late, everyone)
    if paired:
        (
            expand_low_out, shrink_up_out, merge_up_out, merge_low_out, expand_up_out, shrink_low_out,
        ) = settle_early(spot, shared, parts, ADAPTERS, wide, width, pad)
        late, shrink_up_out = lax.optimization_barrier((late, shrink_up_out))
        joined_low_out, joined_up_out = settle_late(late, parts, ADAPTERS, part_width, wide)
        joined_up_out = joined_up_out.transpose(0, 2, 1, 3)
        joined_low_out, expand_low_out, merge_low_out, shrink_low_out = (
            tall(each) for each in (joined_low_out, expand_low_out, merge_low_out, shrink_low_out)
        )
    else:
        late = late.reshape(parts, blocks, ADAPTERS, -1)
        joined_low_out = tall(ranks_in(late[..., :low_size], part_width).reshape(ADAPTERS, rank, model))
        joined_up_out = ranks_in(late[..., low_size:], piece).reshape(ADAPTERS, rank, 3, wide).astype(F32)
        shared = ranks_in(shared.reshape(parts, blocks, ADAPTERS, -1), early_width).astype(F32)
        expand_low_out, shrink_up_out, merge_up_out = (
            shared[..., i * part_width : (i + 1) * part_width].reshape(ADAPTERS, rank, model)
            for i in range(3)
        )
        expand_low_out = tall(expand_low_out)
        divided = lax.dynamic_index_in_dim(shared[..., 3 * part_width :], place, 2, keepdims=False)
        merge_low_out = tall(divided[:, :, :wide])
        expand_up_out = jnp.stack(
            [divided[:, :, wide + i * pad : wide + i * pad + width] for i in range(2)], axis=2
        )
        shrink_low_out = tall(divided[:, :, wide + 2 * pad : wide + 2 * pad + width])
    return (
        result,
        grad_hidden.astype(BF),
        joined_low_out,
        joined_up_out,
        merge_low_out,
        merge_up_out,
        expand_low_out,
        expand_up_out,
        shrink_low_out,
        shrink_up_out,
    )


def solution(mesh):
    in_specs = (
        P("dp", "mp", None),
        P("dp", "mp", None),
        P("dp"),
        P(),
        P(),
        P("dp", None, "mp"),
        P("dp", "mp"),
        P("dp", None, "mp"),
        P("dp", "mp"),
        P(),
        P(None, None, None, "mp"),
        P(None, "mp", None),
        P(),
        P(),
        P(None, None, None, "mp"),
        P(None, "mp", None),
        P(),
    )
    out_specs = (
        P("dp", "mp", None),
        P("dp", "mp", None),
        P(),
        P(None, None, None, "mp"),
        P(None, "mp", None),
        P(),
        P(),
        P(None, None, None, "mp"),
        P(None, "mp", None),
        P(),
    )
    return jax.shard_map(local, mesh=mesh, in_specs=in_specs, out_specs=out_specs, check_vma=False)
```

```python
import jax
import jax.numpy as jnp
from jax import lax
from jax.experimental import pallas as pl
from jax.experimental.pallas import tpu as pltpu
from jax.sharding import PartitionSpec as P

HEAD_DIM = 64
ADAPTERS = 8
ADAPTER_SCALE = 2.0
NORM_EPS = 1e-05
ROPE_BASE = 160000.0
LANES = 128
CH = 256
BF = jnp.bfloat16
F32 = jnp.float32


def nt(a, b):
    return lax.dot_general(a, b, (((1,), (1,)), ((), ())), preferred_element_type=F32)


def nn(a, b):
    return lax.dot_general(a, b, (((1,), (0,)), ((), ())), preferred_element_type=F32)


def tn(a, b):
    return lax.dot_general(a, b, (((0,), (0,)), ((), ())), preferred_element_type=F32)


def lanes_of(ref, first=0, count=None, spot=None):
    count = ref.shape[2] if count is None else count
    places = [part if spot is None else spot[1 + part] for part in range(ref.shape[0])]
    return jnp.concatenate([ref[place, 0, pl.ds(first, count), :] for place in places], axis=1)


def full(shape):
    return pl.BlockSpec(shape, lambda *_: (0,) * len(shape))


def full_once(shape):
    return pl.BlockSpec(shape, lambda *_: (0,) * len(shape), pipeline_mode=pl.Buffered(1))


def norm_parts(values):
    centred = values - jnp.mean(values, axis=-1, keepdims=True)
    spread = jnp.mean(centred * centred, axis=-1, keepdims=True)
    scale = lax.rsqrt(spread + NORM_EPS)
    return centred * scale, scale


def norm_back(grads, normed, scale, gain):
    weighted = grads * gain
    return scale * (
        weighted
        - jnp.mean(weighted, axis=-1, keepdims=True)
        - normed * jnp.mean(weighted * normed, axis=-1, keepdims=True)
    )


def turn(values, cosine, sine):
    width = values.shape[1]
    half = HEAD_DIM // 2
    many = width // LANES
    if many > 1:
        cosine = jnp.concatenate([cosine] * many, axis=1)
        sine = jnp.concatenate([sine] * many, axis=1)
    lane = lax.broadcasted_iota(jnp.int32, values.shape, 1)
    turned = jnp.where(
        lane % HEAD_DIM < half,
        -pltpu.roll(values, width - half, 1),
        pltpu.roll(values, half, 1),
    )
    return values * cosine + turned * sine


def project_kernel(
    place, own, beside, across, corner, weight, low, up, cosine, sine,
    query, key, value, down, *, wide
):
    table = lanes_of(weight, 0, 3 * wide, place)
    for step, piece in enumerate((own, beside, across, corner)):
        spot = place[0] ^ step
        rows = piece[0]
        small = (nt(rows, low[0]) * ADAPTER_SCALE).astype(BF)
        down[0, step] = small
        out = nt(rows, table) + nn(small, up[0])
        cos, sin = cosine[spot], sine[spot]
        turned = turn(out[:, :wide], cos, sin)
        query[0, spot] = (turned * HEAD_DIM**-0.5).astype(BF)
        key[0, spot] = turn(out[:, wide : 2 * wide], cos, sin).astype(BF)
        value[0, spot] = out[:, 2 * wide :].astype(BF)


def project(place, pieces, weight, low, up, tables):
    seqs, own, model = pieces[0].shape
    tall = up.shape[2]
    wide = tall // 3
    rank = low.shape[1]
    blocks = len(pieces)
    piece = pl.BlockSpec((1, own, model), lambda s, p: (s, 0, 0))
    result = pl.BlockSpec((1, blocks, own, wide), lambda s, p: (s, 0, 0, 0))
    table = pl.BlockSpec((blocks, own, LANES), lambda s, p: (0, 0, 0))
    return pl.pallas_call(
        lambda *refs: project_kernel(*refs, wide=wide),
        grid_spec=pltpu.PrefetchScalarGridSpec(
            num_scalar_prefetch=1,
            grid=(seqs,),
            in_specs=[piece] * blocks
            + [
                pl.BlockSpec(weight.shape, lambda s, p: (0, 0, 0, 0)),
                pl.BlockSpec((1, rank, model), lambda s, p: (s, 0, 0)),
                pl.BlockSpec((1, rank, tall), lambda s, p: (s, 0, 0)),
                table,
                table,
            ],
            out_specs=[result] * 3
            + [pl.BlockSpec((1, blocks, own, rank), lambda s, p: (s, 0, 0, 0))],
        ),
        out_shape=[jax.ShapeDtypeStruct((seqs, blocks, own, wide), BF)] * 3
        + [jax.ShapeDtypeStruct((seqs, blocks, own, rank), BF)],
        name="project",
    )(place, *pieces, weight, low, up, *tables)


def one_head(values, head):
    lane = lax.broadcasted_iota(jnp.int32, values.shape, 1)
    return jnp.where((lane // HEAD_DIM) == head, values, jnp.zeros_like(values))


def attend_kernel(place, query, key, value, *outs):
    *contexts, probs, shrinks, held = outs
    blocks, own = query.shape[1:3]
    tile = pl.program_id(1)
    keys = key[0].reshape(blocks * own, LANES)
    turned = value[0].reshape(blocks * own, LANES).T
    rows = jnp.concatenate([query[0, place[0] ^ (2 * tile + i)] for i in range(2)], axis=0)
    parts = []
    for head in range(2):
        mine = one_head(rows, head)
        held[...] = nt(keys, mine)
        top = jnp.max(held[...], axis=0, keepdims=True)

        def some(i, sums):
            at = pl.ds(pl.multiple_of(i * CH, CH), CH)
            raised = jnp.exp(held[at, :] - top)
            probs[0, 0, head, at, :] = raised.astype(BF)
            return sums + jnp.sum(raised.reshape(CH // 8, 8, raised.shape[1]), axis=0)

        sums = lax.fori_loop(0, blocks * own // CH, some, jnp.zeros((8, 2 * own), F32))
        shrink = 1.0 / jnp.sum(sums, axis=0, keepdims=True)
        shrinks[0, 0, head : head + 1] = shrink
        parts.append(nn(turned[head * HEAD_DIM : (head + 1) * HEAD_DIM], probs[0, 0, head]) * shrink)
    merged = jnp.concatenate(parts, axis=0).T.astype(BF)
    for half in range(blocks // 2):
        @pl.when(tile == half)
        def _():
            for i in range(2):
                contexts[2 * half + i][...] = merged[i * own : (i + 1) * own]


def attend(place, query, key, value, seq):
    _, blocks, own, wide = query.shape
    pairs = wide // LANES
    whole = pl.BlockSpec((1, blocks, own, LANES), lambda h, t, p: (seq, 0, 0, h))
    *contexts, probs, shrinks = pl.pallas_call(
        attend_kernel,
        grid_spec=pltpu.PrefetchScalarGridSpec(
            num_scalar_prefetch=1,
            grid=(pairs, blocks // 2),
            in_specs=[whole] * 3,
            out_specs=[pl.BlockSpec((own, LANES), lambda h, t, p: (0, h))] * blocks
            + [
                pl.BlockSpec((1, 1, 2, blocks * own, 2 * own), lambda h, t, p: (h, t, 0, 0, 0)),
                pl.BlockSpec((1, 1, 2, 2 * own), lambda h, t, p: (h, t, 0, 0)),
            ],
            scratch_shapes=[pltpu.VMEM((blocks * own, 2 * own), F32)],
        ),
        out_shape=[jax.ShapeDtypeStruct((own, wide), BF)] * blocks
        + [
            jax.ShapeDtypeStruct((pairs, blocks // 2, 2, blocks * own, 2 * own), BF),
            jax.ShapeDtypeStruct((pairs, blocks // 2, 2, 2 * own), F32),
        ],
        name="attend",
    )(place, query, key, value)
    return contexts, (probs, shrinks, list(contexts))


def attend_back_kernel(place, query, key, value, probs, shrinks, *refs):
    blocks, own = query.shape[1:3]
    contexts = refs[:blocks]
    pieces = refs[blocks : 2 * blocks]
    rows_in = refs[2 * blocks : 3 * blocks]
    cosine, sine, weight, low, up, down, here, there, up_grad, low_grad, total, small, turn_keys = refs[3 * blocks :]
    pair = pl.program_id(0)
    last = pl.num_programs(0) - 1
    wide = LANES * pl.num_programs(0)
    keys = key[0].reshape(blocks * own, LANES)
    values = value[0].reshape(blocks * own, LANES)
    turned = keys.T
    backs, mines, mine_grads = [], [], []
    grad_queries = []
    for step in range(0, blocks, 2):
        spots = [place[0] ^ (step + i) for i in range(2)]
        rows = jnp.concatenate([query[0, spot] for spot in spots], axis=0)
        outer = jnp.concatenate([pieces[step + i][0] for i in range(2)], axis=0).astype(F32)
        inner = jnp.concatenate([contexts[step + i][...] for i in range(2)], axis=0).astype(F32)
        product = (outer * inner).T
        factors = [shrinks[0, step // 2, head : head + 1] for head in range(2)]
        spread = jnp.concatenate([jnp.broadcast_to(f, (HEAD_DIM, 2 * own)) for f in factors], axis=0).T
        outer = (outer * spread).astype(BF)
        parts = []
        for head in range(2):
            mine_grad = one_head(outer, head)
            chances = probs[0, step // 2, head]
            half = product[head * HEAD_DIM : (head + 1) * HEAD_DIM]
            mean = jnp.sum(half, axis=0, keepdims=True) * factors[head]
            back = (chances.astype(F32) * (nt(values, mine_grad) - mean)).astype(BF)
            parts.append(nn(turned[head * HEAD_DIM : (head + 1) * HEAD_DIM], back))
            backs.append(back)
            mines.append(one_head(rows, head))
            mine_grads.append(mine_grad)
        queries = jnp.concatenate(parts, axis=0).T * HEAD_DIM**-0.5
        for i, spot in enumerate(spots):
            part = queries[i * own : (i + 1) * own]
            grad_queries.append(turn(part, cosine[spot], -sine[spot]).astype(BF))
    grad_keys = nn(jnp.concatenate(backs, axis=1), jnp.concatenate(mines, axis=0))
    chances = [probs[0, i // 2, i % 2] for i in range(blocks)]
    grad_values = nn(jnp.concatenate(chances, axis=1), jnp.concatenate(mine_grads, axis=0))
    for step in range(blocks):
        part = slice(step * own, (step + 1) * own)
        turn_keys[0, step] = turn(grad_keys[part], cosine[step], -sine[step]).astype(BF)
        turn_keys[1, step] = grad_values[part].astype(BF)
    grads = [
        jnp.concatenate(grad_queries, axis=0),
        jnp.concatenate([turn_keys[0, place[0] ^ step] for step in range(blocks)], axis=0),
        jnp.concatenate([turn_keys[1, place[0] ^ step] for step in range(blocks)], axis=0),
    ]
    grads = jnp.concatenate(grads, axis=1)
    firsts = [pl.multiple_of(kind * wide + pair * LANES, LANES) for kind in range(3)]
    table = jnp.concatenate([lanes_of(weight, first, LANES, place) for first in firsts], axis=0)
    ups = jnp.concatenate([up[0, :, pl.ds(first, LANES)] for first in firsts], axis=1)
    downs = jnp.concatenate([down[0, step] for step in range(blocks)], axis=0)
    more = nn(grads, table)
    more_small = nt(grads, ups)
    up_part = tn(downs, grads)
    for kind in range(3):
        up_grad[kind] = up_part[:, kind * LANES : (kind + 1) * LANES].astype(BF)

    @pl.when(pair == 0)
    def _():
        total[...] = more
        small[...] = more_small

    @pl.when(pair > 0)
    def _():
        total[...] += more
        small[...] += more_small

    @pl.when(pair == last)
    def _():
        narrow = (small[...] * ADAPTER_SCALE).astype(BF)
        low_grad[...] = tn(narrow, jnp.concatenate([piece[0] for piece in rows_in], axis=0)).astype(BF)
        done = total[...] + nn(narrow, low[0])
        for step in range(blocks):
            part = done[step * own : (step + 1) * own].astype(BF)
            (there if step % 2 else here)[step // 2] = part


def attend_back(place, seq, query, key, value, kept, grads, pieces, tables, weight, low, up, down):
    _, blocks, own, wide = query.shape
    _, rank, model = low.shape
    tall = up.shape[2]
    pairs = wide // LANES
    whole = lambda shape: pl.BlockSpec(shape, lambda h, p: (0,) * len(shape))
    of_seq = lambda shape: pl.BlockSpec((1,) + shape, lambda h, p: (seq,) + (0,) * len(shape))
    heads = pl.BlockSpec((1, blocks, own, LANES), lambda h, p: (seq, 0, 0, h))
    probs, shrinks, contexts = kept
    return pl.pallas_call(
        attend_back_kernel,
        grid_spec=pltpu.PrefetchScalarGridSpec(
            num_scalar_prefetch=1,
            grid=(pairs,),
            in_specs=[heads] * 3
            + [pl.BlockSpec((1,) + probs.shape[1:], lambda h, p: (h, 0, 0, 0, 0))]
            + [pl.BlockSpec((1,) + shrinks.shape[1:], lambda h, p: (h, 0, 0, 0))]
            + [pl.BlockSpec((own, LANES), lambda h, p: (0, h))] * blocks
            + [pl.BlockSpec((1, own, LANES), lambda h, p: (seq, 0, h))] * blocks
            + [of_seq((own, model))] * blocks
            + [whole((blocks, own, LANES))] * 2
            + [
                whole(weight.shape),
                of_seq((rank, model)),
                of_seq((rank, tall)),
                of_seq((blocks, own, rank)),
            ],
            out_specs=[
                whole((blocks // 2, own, model)),
                whole((blocks // 2, own, model)),
                pl.BlockSpec((3, rank, LANES), lambda h, p: (0, 0, h)),
                whole((rank, model)),
            ],
            scratch_shapes=[
                pltpu.VMEM((blocks * own, model), F32),
                pltpu.VMEM((blocks * own, rank), F32),
                pltpu.VMEM((2, blocks, own, LANES), BF),
            ],
        ),
        out_shape=[
            jax.ShapeDtypeStruct((blocks // 2, own, model), BF),
            jax.ShapeDtypeStruct((blocks // 2, own, model), BF),
            jax.ShapeDtypeStruct((3, rank, wide), BF),
            jax.ShapeDtypeStruct((rank, model), BF),
        ],
        name="attend_back",
    )(place, query, key, value, probs, shrinks, *contexts, *grads, *pieces, *tables, weight, low, up, down)


def merge_kernel(spot, *refs, blocks, seqs):
    contexts = refs[: blocks * seqs]
    start, near, far, low, up, gain, middle, normed, down = refs[blocks * seqs :]
    tables = [lanes_of((far if i // 2 else near).at[:, pl.ds(i % 2, 1)], spot=spot) for i in range(blocks)]
    for seq in range(seqs):
        total = start[seq].astype(F32)
        small = jnp.zeros(down.shape[1:], F32)
        for step in range(blocks):
            rows = contexts[seq * blocks + step][...]
            small += nt(rows, low[step, seq])
            total += nn(rows, tables[step])
        small = (small * ADAPTER_SCALE).astype(BF)
        down[seq] = small
        total += nn(small, up[seq])
        middle[seq] = total
        normed[seq] = (norm_parts(total)[0] * gain[...]).astype(BF)


def merge(spot, contexts, start, near, far, low, up, gain):
    seqs, own, model = start.shape
    blocks, _, rank, wide = low.shape
    inputs = [piece for context in contexts for piece in context]
    inputs += [start, near, far, low, up, gain]
    results = [
        jax.ShapeDtypeStruct((seqs, own, model), F32),
        jax.ShapeDtypeStruct((seqs, own, model), BF),
        jax.ShapeDtypeStruct((seqs, own, rank), BF),
    ]
    return pl.pallas_call(
        lambda *refs: merge_kernel(*refs, blocks=blocks, seqs=seqs),
        grid_spec=pltpu.PrefetchScalarGridSpec(
            num_scalar_prefetch=1,
            grid=(1,),
            in_specs=[full(each.shape) for each in inputs],
            out_specs=[full(each.shape) for each in results],
        ),
        out_shape=results,
        name="merge",
    )(spot, *inputs)


def gated_kernel(
    place, rows, out_grad, middle, expand, shrink, expand_up, shrink_low, expand_low, shrink_up, mask,
    near, far, merge_low, merge_up, gain, merge_down, *refs, width, blocks, seqs
):
    contexts = refs[: seqs * blocks]
    (
        result, expand_up_grad, shrink_low_grad, expand_low_grad, shrink_up_grad,
        grad_middle, merge_low_grad, merge_up_grad,
    ) = refs[seqs * blocks : seqs * blocks + 8]
    grad_contexts = refs[seqs * blocks + 8 : seqs * blocks + 8 + blocks]
    total, grad_rows, down, down_grad, late, late_grad = refs[seqs * blocks + 8 + blocks :]
    step = pl.program_id(0)
    scaled = ADAPTER_SCALE * mask[...]

    @pl.when(step == 0)
    def _():
        total[...] = middle[...]
        grad_rows[...] = jnp.zeros(grad_rows.shape, F32)
        down[...] = (nt(rows[...], expand_low[...]) * scaled).astype(BF)
        down_grad[...] = (nt(out_grad[...], shrink_up[...]) * scaled).astype(BF)
        late[...] = jnp.zeros(late.shape, F32)
        late_grad[...] = jnp.zeros(late_grad.shape, F32)

    values = lanes_of(expand, 0, width)
    gates = lanes_of(expand, width, width)
    outs = lanes_of(shrink)
    up_values = expand_up[0, :, :width]
    up_gates = expand_up[0, :, expand_up.shape[2] // 2 : expand_up.shape[2] // 2 + width]
    low_outs = shrink_low[0, :, :width]
    first = nt(rows[...], values) + nn(down[...], up_values)
    second = nt(rows[...], gates) + nn(down[...], up_gates)
    chance = 0.5 + 0.5 * lax.erf(first * (0.5**0.5))
    curve = first * chance
    slope = chance + first * (jnp.exp(-0.5 * first * first) * 0.3989422804014327)
    active = (curve * second).astype(BF)
    grads = nt(out_grad[...], outs) + nn(down_grad[...], low_outs)
    first_grad = (grads * second * slope).astype(BF)
    second_grad = (grads * curve).astype(BF)
    total[...] += nn(active, outs)
    late[...] += nt(active, low_outs)
    grad_rows[...] += nn(first_grad, values) + nn(second_grad, gates)
    late_grad[...] += nt(first_grad, up_values) + nt(second_grad, up_gates)
    expand_up_grad[0, 0] = tn(down[...], first_grad).astype(BF)
    expand_up_grad[0, 1] = tn(down[...], second_grad).astype(BF)
    shrink_low_grad[0] = tn(down_grad[...], active).astype(BF)

    @pl.when(step == blocks - 1)
    def _():
        small = (late[...] * scaled).astype(BF)
        result[...] = (total[...] + nn(small, shrink_up[...])).astype(BF)
        shrink_up_grad[...] = tn(small, out_grad[...]).astype(BF)
        small_grad = (late_grad[...] * scaled).astype(BF)
        expand_low_grad[...] = tn(small_grad, rows[...]).astype(BF)
        own = rows.shape[0] // seqs
        for seq in range(seqs):
            part = slice(seq * own, (seq + 1) * own)
            normed, scale = norm_parts(middle[part])
            grad_normed = grad_rows[part] + nn(small_grad[part], expand_low[...])
            whole = out_grad[part].astype(F32) + norm_back(grad_normed, normed, scale, gain[...])
            grad_middle[seq] = whole
            low_rows = whole.astype(BF)
            small = (nt(low_rows, merge_up[seq]) * ADAPTER_SCALE).astype(BF)
            for move in range(blocks):
                ref = far if move // 2 else near
                table = lanes_of(ref.at[:, pl.ds(move % 2, 1)], spot=place)
                out = (nt(low_rows, table) + nn(small, merge_low[move, seq])).astype(BF)
                grad_contexts[move][seq] = out
                merge_low_grad[seq, move] = tn(small, contexts[seq * blocks + move][...]).astype(BF)
            merge_up_grad[seq] = tn(merge_down[seq], low_rows).astype(BF)


def gated(
    place, rows, out_grad, middle, weights, width, expand_up, shrink_low, expand_low, shrink_up, mask,
    near, far, merge_low, merge_up, gain, merge_down, contexts
):
    count, model = rows.shape
    parts, blocks, _, lane = weights.shape
    seqs = len(contexts)
    own, wide = contexts[0][0].shape
    some = merge_up.shape[1]
    rank = expand_low.shape[0]
    pad = shrink_low.shape[2]
    pieces = [piece for context in contexts for piece in context]
    shapes = [
        ((count, model), BF),
        ((blocks, 2, rank, width), BF),
        ((blocks, rank, width), BF),
        ((rank, model), BF),
        ((rank, model), BF),
        ((seqs, own, model), F32),
        ((seqs, blocks, some, wide), BF),
        ((seqs, some, model), BF),
    ]
    shapes += [((seqs, own, wide), BF)] * blocks
    out_specs = [full_once(shape) for shape, _ in shapes]
    out_specs[1] = pl.BlockSpec((1, 2, rank, width), lambda m, p: (m, 0, 0, 0))
    out_specs[2] = pl.BlockSpec((1, rank, width), lambda m, p: (m, 0, 0))
    return pl.pallas_call(
        lambda *refs: gated_kernel(*refs, width=width, blocks=blocks, seqs=seqs),
        grid_spec=pltpu.PrefetchScalarGridSpec(
            num_scalar_prefetch=1,
            grid=(blocks,),
            in_specs=[
                full_once((count, model)),
                full_once((count, model)),
                full_once((count, model)),
                pl.BlockSpec((parts, 1, 2 * width, lane), lambda m, p: (0, m, 0, 0)),
                pl.BlockSpec((parts, 1, width, lane), lambda m, p: (0, m, 2, 0)),
                pl.BlockSpec((1, rank, 2 * pad), lambda m, p: (p[0] ^ m, 0, 0)),
                pl.BlockSpec((1, rank, pad), lambda m, p: (p[0] ^ m, 0, 0)),
                full_once((rank, model)),
                full_once((rank, model)),
                full_once((count, rank)),
                full_once(near.shape),
                full_once(far.shape),
                full_once(merge_low.shape),
                full_once(merge_up.shape),
                full_once(gain.shape),
                full_once(merge_down.shape),
            ]
            + [full_once((own, wide))] * len(pieces),
            out_specs=out_specs,
            scratch_shapes=[
                pltpu.VMEM((count, model), F32),
                pltpu.VMEM((count, model), F32),
                pltpu.VMEM((count, rank), BF),
                pltpu.VMEM((count, rank), BF),
                pltpu.VMEM((count, rank), F32),
                pltpu.VMEM((count, rank), F32),
            ],
        ),
        out_shape=[jax.ShapeDtypeStruct(shape, kind) for shape, kind in shapes],
        name="gated",
    )(
        place, rows, out_grad, middle, weights, weights, expand_up, shrink_low, expand_low, shrink_up, mask,
        near, far, merge_low, merge_up, gain, merge_down, *pieces,
    )


def settle_early_kernel(place, got, low, shrink_up, merge_up, merge_low, expand_up, shrink_low, *, parts, blocks, sets, part, wide, width, pad):
    at = 3 * part
    for g in range(parts):
        for block in range(blocks):
            rows = got[g * blocks + block, :, :at].astype(F32)
            for i, out in enumerate((low, shrink_up, merge_up)):
                for two in range(2):
                    cut = rows[two * sets : (two + 1) * sets, i * part : (i + 1) * part]
                    out[:, two * parts + g, block * part : (block + 1) * part] = cut
        rows = got[g * blocks + place[0], :, at:].astype(F32)
        for two in range(2):
            cut = rows[two * sets : (two + 1) * sets]
            rank = two * parts + g
            merge_low[:, rank, :] = cut[:, :wide]
            for kind in range(2):
                first = wide + kind * pad
                expand_up[:, rank, kind, :] = cut[:, first : first + width]
            shrink_low[:, rank, :] = cut[:, wide + 2 * pad : wide + 2 * pad + width]


def settle_early(place, got, parts, sets, wide, width, pad):
    owners, rows, features = got.shape
    blocks = owners // parts
    rank = rows // sets * parts
    part = (features - wide - 3 * pad) // 3
    model = blocks * part
    shapes = [(rank, model)] * 3 + [(rank, wide), (rank, 2, width), (rank, width)]
    shapes = [(sets,) + shape for shape in shapes]
    whole = lambda shape: pl.BlockSpec(shape, lambda i, p: (0,) * len(shape))
    return pl.pallas_call(
        lambda *refs: settle_early_kernel(
            *refs, parts=parts, blocks=blocks, sets=sets, part=part, wide=wide, width=width, pad=pad
        ),
        grid_spec=pltpu.PrefetchScalarGridSpec(
            num_scalar_prefetch=1,
            grid=(1,),
            in_specs=[whole(got.shape)],
            out_specs=[whole(shape) for shape in shapes],
        ),
        out_shape=[jax.ShapeDtypeStruct(shape, F32) for shape in shapes],
        name="settle_early",
    )(place, got)


def settle_late_kernel(got, low, up, *, parts, blocks, sets, part, piece):
    wide = up.shape[3]
    for g in range(parts):
        rows = [got[g * blocks + block].astype(F32) for block in range(blocks)]
        tail = jnp.concatenate([row[:, part : part + piece] for row in rows], axis=1)
        for two in range(2):
            rank = two * parts + g
            for block, row in enumerate(rows):
                low[:, rank, block * part : (block + 1) * part] = row[two * sets : (two + 1) * sets, :part]
            for kind in range(up.shape[1]):
                up[:, kind, rank, :] = tail[two * sets : (two + 1) * sets, kind * wide : (kind + 1) * wide]


def settle_late(got, parts, sets, part, wide):
    owners, rows, features = got.shape
    blocks = owners // parts
    rank = rows // sets * parts
    piece = features - part
    shapes = [(sets, rank, blocks * part), (sets, blocks * piece // wide, rank, wide)]
    return pl.pallas_call(
        lambda *refs: settle_late_kernel(*refs, parts=parts, blocks=blocks, sets=sets, part=part, piece=piece),
        grid=(1,),
        in_specs=[full(got.shape)],
        out_specs=[full(shape) for shape in shapes],
        out_shape=[jax.ShapeDtypeStruct(shape, F32) for shape in shapes],
        name="settle_late",
    )(got)


def pair_swap(values, bit):
    size = lax.axis_size("mp")
    return lax.ppermute(values, "mp", [(i, i ^ bit) for i in range(size)])


def tie(values, after):
    return lax.optimization_barrier((values, after))[0]


def swap_all(values, axes):
    return lax.all_to_all(values, axes, 0, 0, tiled=True)


def share_all(values, axes):
    size = 1
    for axis in (axes,) if isinstance(axes, str) else axes:
        size *= lax.axis_size(axis)
    return swap_all(jnp.broadcast_to(values[None], (size,) + values.shape), axes)


def gather_parts(values):
    parts = lax.axis_size("dp")
    here = lax.axis_index("dp")
    every = jnp.arange(parts, dtype=jnp.int32)
    if parts != 8:
        return share_all(values, "dp"), every
    stack = [values]
    for shift in range(2, parts, 2):
        stack.append(lax.ppermute(values, "dp", [(i, (i + shift) % parts) for i in range(parts)]))
    stack = jnp.stack(stack)
    other = lax.ppermute(stack, "dp", [(i, i ^ 1) for i in range(parts)])
    order = (every % 2 ^ here % 2) * (parts // 2) + (here // 2 - every // 2) % (parts // 2)
    return jnp.concatenate([stack, other]), order.astype(jnp.int32)


def full_lanes(whole):
    parts, blocks, count, own = whole.shape
    if own == LANES:
        return whole
    tiles = parts * own // LANES
    whole = whole.transpose(1, 2, 0, 3).reshape(blocks, count, tiles, LANES)
    return whole.transpose(2, 0, 1, 3)


def local(
    hidden,
    cotangent,
    adapter_ids,
    attn_gain,
    mlp_gain,
    joined_weight,
    merge_weight_matrix,
    expand_weight,
    shrink_weight_matrix,
    joined_lower,
    joined_up_matrices,
    merge_lower,
    merge_up_matrices,
    expand_lower,
    expand_up_matrices,
    shrink_lower,
    shrink_up_matrices,
):
    parts, blocks = lax.axis_size("dp"), lax.axis_size("mp")
    place = lax.axis_index("mp")
    pair, core = place // 2, place % 2
    spot = place[None].astype(jnp.int32)
    seqs, own, model = hidden.shape
    length = own * blocks
    row_in = joined_weight.shape[0]
    wide = joined_weight.shape[2]
    width = expand_weight.shape[2]
    rank = joined_lower.shape[2]
    count = seqs * own

    rest = jnp.concatenate(
        [expand_weight.reshape(row_in, 2 * width).T, shrink_weight_matrix.T], axis=0
    )
    rest_whole = full_lanes(
        lax.all_gather(rest, ("dp", "mp"), axis=0, tiled=True).reshape(parts, blocks, 3 * width, row_in)
    )

    note = jnp.zeros((8, row_in), BF).at[0, :seqs].set(adapter_ids.astype(BF))
    joined_mine = jnp.concatenate(
        [joined_weight.reshape(row_in, 3 * wide).T, merge_weight_matrix.T, note], axis=0
    )
    joined_got, order = gather_parts(joined_mine)
    every_id = joined_got[:, 4 * wide, :seqs][order].astype(jnp.int32)
    if row_in != LANES:
        order = jnp.arange(model // LANES, dtype=jnp.int32)
    spot = jnp.concatenate([spot, order])
    joined_whole = full_lanes(joined_got[:, None])

    attn_scale = attn_gain.astype(F32)[None, :]
    mlp_scale = mlp_gain.astype(F32)[None, :]
    first_normed, first_scale = norm_parts(hidden.astype(F32))
    normed = (first_normed * attn_scale).astype(BF)
    def pick(table):
        return table.at[adapter_ids].get(mode="promise_in_bounds")

    def pick_low(table):
        return pick(table).transpose(0, 2, 1)

    def pick_up(table):
        return pick(table).reshape(seqs, rank, -1)

    joined_low, joined_up = pick_low(joined_lower), pick_up(joined_up_matrices)
    expand_low = pick_low(expand_lower).reshape(seqs * rank, model)
    merge_up = pick_up(merge_up_matrices)
    shrink_up = pick_up(shrink_up_matrices).reshape(seqs * rank, model)
    pad = -(-width // LANES) * LANES
    side = [(0, 0), (0, 0), (0, pad - width)]
    expand_mine = pick(expand_up_matrices)
    mine = jnp.concatenate(
        [
            pick_low(merge_lower),
            jnp.pad(expand_mine[:, :, 0], side),
            jnp.pad(expand_mine[:, :, 1], side),
            jnp.pad(pick_low(shrink_lower), side),
        ],
        axis=2,
    )
    far_sets = pair_swap(mine, 2)
    split_sets = jnp.stack([mine, pair_swap(mine, 1), far_sets, pair_swap(far_sets, 1)])
    merge_low = split_sets[:, :, :, :wide]
    expand_up = split_sets[:, :, :, wide : wide + 2 * pad].reshape(blocks, seqs * rank, 2 * pad)
    shrink_low = split_sets[:, :, :, wide + 2 * pad :].reshape(blocks, seqs * rank, pad)
    mask = (
        (jnp.arange(count) // own)[:, None] == (jnp.arange(seqs * rank) // rank)[None, :]
    ).astype(F32)

    half = HEAD_DIM // 2
    inverse = ROPE_BASE ** (-((jnp.arange(LANES) % half).astype(F32) * 2.0 / HEAD_DIM))
    angles = jnp.arange(length, dtype=F32)[:, None] * inverse[None, :]
    tables = [table.reshape(blocks, own, LANES) for table in (jnp.cos(angles), jnp.sin(angles))]

    across = pair_swap(normed, 2)
    beside = pair_swap(normed, 1)
    (
        across, joined_low, joined_up, tables, merge_low, merge_up,
        expand_low, expand_up, shrink_low, shrink_up, mask,
    ) = lax.optimization_barrier(
        (
            across, joined_low, joined_up, tables, merge_low, merge_up,
            expand_low, expand_up, shrink_low, shrink_up, mask,
        )
    )
    corner = pair_swap(across, 1)
    pieces = (normed, beside, across, corner)
    query, key, value, joined_down = project(
        spot, pieces, joined_whole, joined_low, joined_up,
        tables,
    )
    merge_own = joined_whole[:, :, 3 * wide : 4 * wide]
    merge_near = jnp.concatenate([merge_own, pair_swap(merge_own, 1)], axis=1)
    contexts, logs = [], []
    for seq in range(seqs):
        if seq:
            query = tie(query, context[0])
        context, probs = attend(spot, query, key, value, seq)
        context = [context[0]] + [pair_swap(context[bit], bit) for bit in range(1, blocks)]
        contexts.append(context)
        logs.append(probs)
    merge_far = pair_swap(merge_near, 2)
    middle, normed_mlp, merge_down = merge(
        spot, contexts, hidden, merge_near, merge_far, merge_low, merge_up, mlp_scale
    )
    (
        result, expand_up_grad, shrink_low_grad, expand_low_grad, shrink_up_grad,
        grad_middle, merge_low_grads, merge_up_grads, *grad_contexts,
    ) = gated(
        spot, normed_mlp.reshape(count, model), cotangent.reshape(count, model),
        middle.reshape(count, model), rest_whole, width,
        expand_up, shrink_low, expand_low, shrink_up, mask,
        merge_near, merge_far, merge_low, merge_up, mlp_scale, merge_down, contexts,
    )
    result = result.reshape(middle.shape)
    halfway = [grad_contexts[0]] + [pair_swap(grad_contexts[bit], bit) for bit in range(1, blocks)]

    paired = rank == 2 * parts
    everyone = ("dp", "mp")
    owners = parts * blocks
    ids = jnp.broadcast_to(every_id[:, None], (parts, blocks, seqs))
    choose = (jnp.arange(ADAPTERS)[:, None] == ids.reshape(1, -1)).astype(BF)
    choose_own = (jnp.arange(ADAPTERS)[:, None] == every_id.reshape(1, -1)).astype(BF)
    part_width = model // blocks

    def by_block(grad):
        return grad.reshape(seqs * rank, blocks, -1).transpose(1, 0, 2)

    def ranks_out(grad):
        if paired:
            split = grad.reshape(grad.shape[0], seqs, 2, parts, -1).transpose(3, 0, 1, 2, 4)
            return split.reshape(split.shape[:3] + (-1,))
        return grad.reshape(grad.shape[0], seqs, parts, -1).transpose(2, 0, 1, 3)

    def ranks_in(whole, features):
        whole = whole.transpose(2, 1, 0, 3).reshape(ADAPTERS, whole.shape[1], rank, features)
        return whole.transpose(0, 2, 1, 3)

    def tall(values):
        return values.transpose(0, 2, 1).astype(F32)

    joined_low_grads, joined_up_grads = [], []
    grad_normeds = []
    early = jnp.concatenate(
        [
            piece.astype(BF)
            for piece in (
                by_block(expand_low_grad),
                by_block(shrink_up_grad),
                by_block(merge_up_grads.reshape(seqs * rank, model)),
                jnp.take(
                    merge_low_grads.transpose(1, 0, 2, 3).reshape(blocks, seqs * rank, wide),
                    place ^ jnp.arange(blocks), axis=0,
                ),
                jnp.pad(expand_up_grad[:, 0], side),
                jnp.pad(expand_up_grad[:, 1], side),
                jnp.pad(shrink_low_grad, side),
            )
        ],
        axis=2,
    )
    early_width = early.shape[2]

    early = ranks_out(early).reshape(owners, seqs, -1)
    early, halfway = lax.optimization_barrier((early, halfway))
    early = swap_all(early, everyone)
    chip, far = None, None
    for seq in range(seqs):
        pieces_back = list(halfway)
        if seq:
            pieces_back[0] = tie(pieces_back[0], here)
        here, there, up_grad, low_grad = attend_back(
            spot, seq, query, key, value, logs[seq], pieces_back, pieces, tables,
            joined_whole, joined_low, joined_up, joined_down,
        )
        if seq == 1:
            there, far, early = lax.optimization_barrier((there, far, early))
            by_seq = choose.reshape(ADAPTERS, owners, seqs)
            early = sum(
                jnp.dot(by_seq[:, :, i], early[:, i], preferred_element_type=F32) for i in range(seqs)
            )
            if paired:
                early = jnp.concatenate([early[:, :early_width], early[:, early_width:]], axis=0)
            shared = lax.all_gather(early.astype(BF), everyone, axis=0)
        if seq == 2:
            there, far = lax.optimization_barrier((there, far))
        if seq:
            grad_normeds.append(chip + (far,))
        joined_up_grads.append(up_grad.transpose(1, 0, 2).reshape(rank, 3 * wide))
        joined_low_grads.append(low_grad)
        there = pair_swap(there, 1)
        give = (here[1].astype(F32) + there[1].astype(F32)).astype(BF)
        chip = (here[0], there[0])
        far = pair_swap(give, 2)

    piece = 3 * wide // blocks
    late_low = ranks_out(by_block(jnp.concatenate(joined_low_grads)).astype(BF))
    late_up = jnp.stack(joined_up_grads).astype(BF).reshape(seqs * rank, blocks, piece)
    late_up = ranks_out(late_up.transpose(1, 0, 2))
    some = 2 if paired else 1
    late_low, late_up = (each.reshape(owners, seqs * some, -1) for each in (late_low, late_up))
    low_size = late_low.shape[2]
    late = jnp.concatenate([late_low, late_up], axis=2)
    late = tie(late, there)
    late, far = lax.optimization_barrier((swap_all(late, everyone), far))
    late = late.reshape(parts, blocks, seqs, some, -1)
    grad_normeds.append(chip + (far,))
    grad_normeds = [sum(part.astype(F32) for part in parts_of) for parts_of in grad_normeds]
    grad_hidden = grad_middle + norm_back(jnp.stack(grad_normeds), first_normed, first_scale, attn_scale)
    late_low = late[..., :low_size].reshape(owners * seqs, -1)
    late_up = late[..., low_size:].transpose(1, 0, 2, 3, 4).reshape(blocks, parts * seqs, -1)
    late_low = jnp.dot(choose, late_low, preferred_element_type=F32).astype(BF)
    late_up = jnp.einsum("as,bsf->baf", choose_own, late_up, preferred_element_type=F32).astype(BF)
    if paired:
        half_low, half_up = late_low.shape[1] // 2, late_up.shape[2] // 2
        late_low = jnp.concatenate([late_low[:, :half_low], late_low[:, half_low:]], axis=0)
        late_up = jnp.concatenate([late_up[:, :, :half_up], late_up[:, :, half_up:]], axis=1)
    late = jnp.concatenate(
        [jnp.broadcast_to(late_low[None], (blocks,) + late_low.shape), late_up], axis=2
    )
    late = jnp.broadcast_to(late[None], (parts,) + late.shape).reshape((owners,) + late.shape[1:])
    late = swap_all(late, everyone)
    if paired:
        (
            expand_low_out, shrink_up_out, merge_up_out, merge_low_out, expand_up_out, shrink_low_out,
        ) = settle_early(spot, shared, parts, ADAPTERS, wide, width, pad)
        late, shrink_up_out = lax.optimization_barrier((late, shrink_up_out))
        joined_low_out, joined_up_out = settle_late(late, parts, ADAPTERS, part_width, wide)
        joined_up_out = joined_up_out.transpose(0, 2, 1, 3)
        joined_low_out, expand_low_out, merge_low_out, shrink_low_out = (
            tall(each) for each in (joined_low_out, expand_low_out, merge_low_out, shrink_low_out)
        )
    else:
        late = late.reshape(parts, blocks, ADAPTERS, -1)
        joined_low_out = tall(ranks_in(late[..., :low_size], part_width).reshape(ADAPTERS, rank, model))
        joined_up_out = ranks_in(late[..., low_size:], piece).reshape(ADAPTERS, rank, 3, wide).astype(F32)
        shared = ranks_in(shared.reshape(parts, blocks, ADAPTERS, -1), early_width).astype(F32)
        expand_low_out, shrink_up_out, merge_up_out = (
            shared[..., i * part_width : (i + 1) * part_width].reshape(ADAPTERS, rank, model)
            for i in range(3)
        )
        expand_low_out = tall(expand_low_out)
        divided = lax.dynamic_index_in_dim(shared[..., 3 * part_width :], place, 2, keepdims=False)
        merge_low_out = tall(divided[:, :, :wide])
        expand_up_out = jnp.stack(
            [divided[:, :, wide + i * pad : wide + i * pad + width] for i in range(2)], axis=2
        )
        shrink_low_out = tall(divided[:, :, wide + 2 * pad : wide + 2 * pad + width])
    return (
        result,
        grad_hidden.astype(BF),
        joined_low_out,
        joined_up_out,
        merge_low_out,
        merge_up_out,
        expand_low_out,
        expand_up_out,
        shrink_low_out,
        shrink_up_out,
    )


def solution(mesh):
    in_specs = (
        P("dp", "mp", None),
        P("dp", "mp", None),
        P("dp"),
        P(),
        P(),
        P("dp", None, "mp"),
        P("dp", "mp"),
        P("dp", None, "mp"),
        P("dp", "mp"),
        P(),
        P(None, None, None, "mp"),
        P(None, "mp", None),
        P(),
        P(),
        P(None, None, None, "mp"),
        P(None, "mp", None),
        P(),
    )
    out_specs = (
        P("dp", "mp", None),
        P("dp", "mp", None),
        P(),
        P(None, None, None, "mp"),
        P(None, "mp", None),
        P(),
        P(),
        P(None, None, None, "mp"),
        P(None, "mp", None),
        P(),
    )
    return jax.shard_map(local, mesh=mesh, in_specs=in_specs, out_specs=out_specs, check_vma=False)
```
